256 devices in a mesh: req: 8 (over z_lo, y), dev: 32 (over z_hi, x, core).
Axes of the slice: x: 4, y: 4, z: 8 (z_hi: 4, z_lo: 2; z = z_hi * 2 + z_lo), core: 2. Of those that a mesh axis runs over, the one named last changes fastest.
Arguments:
- hidden_in: bfloat16 [8, 1024, 2048], P('req', 'dev'), may hold values from -60 to 60
- attention_gain: float32 [2048], replicated, may hold values from 0.1 to 1.9
- query_weight: bfloat16 [2048, 2048], P('dev'), may hold values from -0.625 to 0.625
- keyval_weight: bfloat16 [1024, 2048], P('dev'), may hold values from -0.5 to 0.5
- out_weight: bfloat16 [2048, 2048], P('dev'), may hold values from -0.0625 to 0.0625
- feedforward_gain: float32 [2048], replicated, may hold values from 0.1 to 1.9
- gate_weight: bfloat16 [8192, 2048], P(('req', 'dev')), may hold values from -0.125 to 0.125
- up_weight: bfloat16 [8192, 2048], P(('req', 'dev')), may hold values from -0.125 to 0.125
- down_weight: bfloat16 [8192, 2048], P(('req', 'dev')), may hold values from -0.0625 to 0.0625
- prefix_pool: bfloat16 [8, 256, 16, 8, 128], P('req', 'dev'), may hold values from -640 to 640
- page_table: int32 [8, 256], P('req'), may hold values from 0 to 255, each once within a row
- prefix_length: int32 [8], P('req'), may hold values from 1 to 4096, 20480 in all
Outputs:
- hidden_out: bfloat16 [8, 1024, 2048], P('req', 'dev')
- new_keyval: bfloat16 [8, 1024, 8, 128], P('req', 'dev')
The draws below stay inside these ranges and needn't reach their ends.
Inputs may be any that keep to these rules, and one draw needn't show every extreme that they name: `page_table`: each row names every page of the request's pool once. `prefix_length`: the longest cached prefix is exactly 4096.
All inputs are finite; a program needn't handle non-finite values. No bound on the sum of `prefix_length` on one device may be relied on, other than what follows from the above.
Results may differ from the reference program's by a relative error of at most 0.013.
The reference program's roundings to bfloat16 on the way count: a program that leaves them out, or rounds other values in their place, can miss the bound.
Values may be sent and summed in bfloat16 or wider, within the bound.
A program may use at most 64 MiB of HBM per device.

```python
import math
import jax
import jax.numpy as jnp
import numpy as np
from jax import lax

D = 2048
HQ = 32
KVH = 8
HD = 64
FF = 8192
PAGE = 16
REQS = 8
TOK = 1024
BLOCKS = 32
Q_DEV = 1
HID_DEV = 32
POOL = 256
PREF = 4096
N_REQ = 8


def draw_hidden_in(key, part):
    keys = jax.random.split(key, 3)
    shape = (REQS, TOK, D)
    spread = 0.5 * math.log(10.0)
    row_scale = jnp.exp(jax.random.uniform(keys[1], (REQS, TOK, 1), jnp.float32, -spread, spread))
    column_scale = jnp.exp(jax.random.uniform(keys[2], (1, 1, D), jnp.float32, -spread, spread))
    base = jax.random.normal(keys[0], shape, jnp.float32)
    base = jnp.clip(base, -6.0, 6.0)
    return (base * row_scale * column_scale).astype(jnp.bfloat16)


def draw_prefix_pool(key, part):
    keys = jax.random.split(key, 1)
    full_shape = (REQS, POOL, PAGE // 2, 2, KVH, 2 * HD)
    base = jnp.clip(4.0 * jax.random.normal(keys[0], full_shape, jnp.float32), -24.0, 24.0)
    return base.reshape(REQS, POOL, PAGE, KVH, 2 * HD).astype(jnp.bfloat16)


def shard_levels(rng, extent, pieces, least, largest):
    level, own = 1.0, jax.random.fold_in(rng, 6)
    for dim, shards_of in pieces:
        draws = jnp.exp(jax.random.uniform(jax.random.fold_in(own, dim), (shards_of,), jnp.float32, least / len(pieces), largest / len(pieces)))
        level = level * jnp.repeat(draws, extent[dim] // shards_of).reshape([-1 if axis == dim else 1 for axis in range(len(extent))])
    return level


def length_profile(number_of, total, bound, skew):
    weights = [(1 << 20) // math.isqrt(grade ** skew) + 1 for grade in range(2, number_of + 1)]
    surplus, counts = total - bound - (number_of - 1), [1] * (number_of - 1)
    while surplus > 0:
        movable = [i for i in range(number_of - 1) if counts[i] < bound]
        pool, budget = sum([weights[i] for i in movable]), surplus
        for i in movable:
            addition = min(bound - counts[i], max(1, budget * weights[i] // pool), surplus)
            counts[i] = counts[i] + addition
            surplus = surplus - addition
    return np.array([bound] + counts)


def ragged(key, number_of, total, reach, lean):
    if number_of == 2:
        one = jax.random.randint(key, (), max(1, total - reach), min(reach, total - 1) + 1)
        return jnp.stack([one, total - one])
    sizes = jnp.asarray(length_profile(number_of, total, reach, lean), jnp.int32)
    pairs = (number_of - 1) // 2
    giver, sink = sizes[1:1 + 2 * pairs:2], sizes[2:2 + 2 * pairs:2]
    room = jnp.minimum(giver - 1, reach - sink)
    shifted = jax.random.randint(jax.random.fold_in(key, 1), (pairs,), 0, 1 << 20) % (room + 1)
    sizes = sizes.at[1:1 + 2 * pairs:2].set(giver - shifted).at[2:2 + 2 * pairs:2].set(sink + shifted)
    return sizes[jax.random.permutation(jax.random.fold_in(key, 2), number_of)]


def normal_values(own_key, extent, scale, bound, cuts=(), kind=jnp.bfloat16):
    gain = shard_levels(own_key, extent, cuts, -0.22, 0.18) if cuts else 1.0
    values = jax.random.normal(own_key, extent, jnp.float32) * scale * gain
    return jnp.minimum(jnp.maximum(values, -bound), bound).astype(kind)


def setup_inputs(seed: int = 0) -> dict:
    streams_of = jax.random.split(jax.random.key(seed), 13)
    hidden_in = draw_hidden_in(jax.random.fold_in(streams_of[12], 71), 0)
    attention_gain = jnp.clip(1.0 + 0.18 * jax.random.normal(streams_of[1], (D,), jnp.float32), 0.1, 1.9)
    query_weight = normal_values(streams_of[2], (HQ * HD, D), (D // 25) ** -0.5, 0.625, ((0, 32),))
    keyval_weight = normal_values(streams_of[3], (2 * KVH * HD, D), (D // 16) ** -0.5, 0.5, ((0, 32),))
    out_weight = normal_values(streams_of[4], (HQ * HD, D), (HQ * HD * 4) ** -0.5, 0.0625, ((0, 32),))
    feedforward_gain = jnp.clip(1.0 + 0.18 * jax.random.normal(streams_of[5], (D,), jnp.float32), 0.1, 1.9)
    gate_weight = normal_values(streams_of[6], (FF, D), D ** -0.5, 0.125, ((0, 256),))
    up_weight = normal_values(streams_of[7], (FF, D), D ** -0.5, 0.125, ((0, 256),))
    down_weight = normal_values(streams_of[8], (FF, D), FF ** -0.5, 0.0625, ((0, 256),))
    prefix_pool = draw_prefix_pool(jax.random.fold_in(streams_of[12], 71), 0)
    page_table = jax.vmap(lambda own: jax.random.permutation(own, POOL))(jax.random.split(streams_of[10], REQS)).reshape((REQS, POOL)).astype(jnp.int32)
    prefix_length = ragged(streams_of[11], REQS, REQS * PREF * 5 // 8, PREF, 1).astype(jnp.int32)
    return {"hidden_in": hidden_in, "attention_gain": attention_gain, "query_weight": query_weight, "keyval_weight": keyval_weight, "out_weight": out_weight, "feedforward_gain": feedforward_gain, "gate_weight": gate_weight, "up_weight": up_weight, "down_weight": down_weight, "prefix_pool": prefix_pool, "page_table": page_table, "prefix_length": prefix_length}


ROPE_BASE = 10000000.0
EPS = 1e-05
ATTENTION_SCALE = 0.015625
MASKED = -1e+30

def root_norm(activations, norm_gain):
    widened = activations.astype(jnp.float32)
    inverse_rms = lax.rsqrt(lax.optimization_barrier(jnp.mean(widened * widened, axis=-1, keepdims=True)) + EPS)
    return (widened * inverse_rms * norm_gain).astype(jnp.bfloat16)

def rotate(vector, positions):
    half_width = vector.shape[-1] // 2
    frequency = ROPE_BASE ** (-jnp.arange(half_width, dtype=jnp.float32) / half_width)
    angles = positions.astype(jnp.float32)[:, None] * frequency[None, :]
    cosine = jnp.cos(angles)[:, None, :]
    sine_part = jnp.sin(angles)[:, None, :]
    leading = vector[..., :half_width]
    trailing = vector[..., half_width:]
    return jnp.concatenate([leading * cosine - trailing * sine_part, trailing * cosine + leading * sine_part], axis=-1)

def rounded(partial_value):
    return lax.optimization_barrier(partial_value.astype(jnp.bfloat16)).astype(jnp.float32)

def transposed_product(left, right):
    return lax.dot_general(left, right, (((1,), (1,)), ((), ())), preferred_element_type=jnp.float32)

def reference(hidden_in, attention_gain, query_weight, keyval_weight, out_weight, feedforward_gain, gate_weight, up_weight, down_weight, prefix_pool, page_table, prefix_length):
    group_size = HQ // KVH
    out_blocks = out_weight.reshape(BLOCKS, Q_DEV * HD, D)
    gate_blocks = gate_weight.reshape(N_REQ, BLOCKS, HID_DEV, D).transpose(1, 0, 2, 3).reshape(BLOCKS, N_REQ * HID_DEV, D)
    up_blocks = up_weight.reshape(N_REQ, BLOCKS, HID_DEV, D).transpose(1, 0, 2, 3).reshape(BLOCKS, N_REQ * HID_DEV, D)
    down_blocks = down_weight.reshape(N_REQ, BLOCKS, HID_DEV, D).transpose(1, 0, 2, 3).reshape(BLOCKS, N_REQ * HID_DEV, D)

    def one_request(inputs):
        tokens, pool_pages, page_rows, length = inputs
        normed = root_norm(tokens, attention_gain)
        positions = length + jnp.arange(TOK, dtype=jnp.int32)
        raw_pairs = transposed_product(normed, keyval_weight).astype(jnp.bfloat16).reshape(TOK, KVH, 2 * HD)
        keys_new = rotate(raw_pairs[..., :HD].astype(jnp.float32), positions).astype(jnp.bfloat16)
        new_keyval = jnp.concatenate([keys_new, raw_pairs[..., HD:]], axis=-1)
        query_full = transposed_product(normed, query_weight).reshape(TOK, HQ, HD)
        queries = (rotate(query_full, positions) * ATTENTION_SCALE).astype(jnp.bfloat16)
        stored = jnp.take(pool_pages, page_rows, axis=0).reshape(PREF, KVH, 2 * HD)
        keyval = jnp.concatenate([stored, new_keyval], axis=0)
        slot_ids = jnp.arange(PREF + TOK, dtype=jnp.int32)[None, :]
        query_ids = jnp.arange(TOK, dtype=jnp.int32)[:, None]
        visible = jnp.where(slot_ids < PREF, slot_ids < length, slot_ids - PREF <= query_ids)

        def head_output(head_index):
            query_head = lax.dynamic_index_in_dim(queries, head_index, 1, keepdims=False)
            shared = lax.dynamic_index_in_dim(keyval, head_index // group_size, 1, keepdims=False)
            scores = transposed_product(query_head, shared[:, :HD])
            scores = jnp.where(visible, scores, MASKED)
            row_max = lax.optimization_barrier(jnp.max(scores, axis=1, keepdims=True))
            weights = jnp.where(visible, jnp.exp(scores - row_max), 0.0)
            row_total = lax.optimization_barrier(jnp.sum(weights, axis=1, keepdims=True))
            mixture = jnp.dot(weights.astype(jnp.bfloat16), shared[:, HD:], preferred_element_type=jnp.float32)
            return (mixture / row_total).astype(jnp.bfloat16)
        head_outputs = lax.map(head_output, jnp.arange(HQ, dtype=jnp.int32))
        attention = head_outputs.transpose(1, 0, 2).reshape(TOK, BLOCKS, Q_DEV * HD).transpose(1, 0, 2)

        def add_attention(running, operands):
            block_rows, block_weight = operands
            partial_value = jnp.dot(block_rows, block_weight, preferred_element_type=jnp.float32)
            return (running + rounded(partial_value), None)
        attention_sum, _ = lax.scan(add_attention, jnp.zeros((TOK, D), jnp.float32), (attention, out_blocks))
        residual = tokens.astype(jnp.float32) + attention_sum
        normed_second = root_norm(residual, feedforward_gain)

        def add_feedforward(running, triple):
            gate_rows, up_rows, down_rows = triple
            gate_act = transposed_product(normed_second, gate_rows)
            up_act = transposed_product(normed_second, up_rows)
            activated = (jax.nn.silu(gate_act) * up_act).astype(jnp.bfloat16)
            partial_value = jnp.dot(activated, down_rows, preferred_element_type=jnp.float32)
            return (running + rounded(partial_value), None)
        feedforward_sum, _ = lax.scan(add_feedforward, jnp.zeros((TOK, D), jnp.float32), (gate_blocks, up_blocks, down_blocks))
        return ((residual + feedforward_sum).astype(jnp.bfloat16), new_keyval)
    outputs, caches = lax.map(one_request, (hidden_in, prefix_pool, page_table, prefix_length))
    return (outputs, caches)
```

```python
import jax
import jax.numpy as jnp
from jax import lax
from jax.experimental import pallas as pl
from jax.experimental.pallas import tpu as pltpu
from jax.sharding import PartitionSpec as P

MESH = pl.DeviceIdType.MESH
HQ = 32
KVH = 8
HD = 64
PAGE = 16
ROPE_BASE = 10000000.0
EPS = 1e-05
ATTENTION_SCALE = 0.015625
MASKED = -1e30
BF = jnp.bfloat16
F32 = jnp.float32
QT = 256
KC = 512


def root_norm(activations, norm_gain):
    widened = activations.astype(F32)
    inverse_rms = lax.rsqrt(jnp.mean(widened * widened, axis=-1, keepdims=True) + EPS)
    return (widened * inverse_rms * norm_gain).astype(BF)


def transposed_product(left, right):
    return lax.dot_general(left, right, (((1,), (1,)), ((), ())), preferred_element_type=F32)


def dev_of(zh, x, c):
    return (zh * 4 + x) * 2 + c


def place():
    d = lax.axis_index("dev")
    return d // 8, (d // 2) % 4, d % 2


class Links:
    def __init__(self, send_sems, recv_sems):
        self.send_sems, self.recv_sems = send_sems, recv_sems
        self.copies = []

    def make(self, i, src, dst, to):
        return pltpu.make_async_remote_copy(
            src_ref=src,
            dst_ref=dst,
            send_sem=self.send_sems.at[i],
            recv_sem=self.recv_sems.at[i],
            device_id=to,
            device_id_type=MESH,
        )

    def send(self, src, dst, to):
        i = len(self.copies)
        copy = self.make(i, src, dst, to)
        copy.start()
        self.copies.append(copy)
        return i, to

    def recv(self, handle, region):
        i, to = handle
        self.make(i, region, region, to).wait_recv()

    def drain(self):
        for copy in self.copies:
            copy.wait_send()


class Locals:
    def __init__(self, sems):
        self.sems, self.copies = sems, []

    def copy(self, src, dst):
        copy = pltpu.make_async_copy(src, dst, self.sems.at[len(self.copies)])
        copy.start()
        self.copies.append(copy)
        return copy


def greet(partners):
    barrier = pltpu.get_barrier_semaphore()
    for partner in partners:
        pl.semaphore_signal(barrier, inc=1, device_id=partner, device_id_type=MESH)
    pl.semaphore_wait(barrier, len(partners))


def halves(ref, i):
    rows = ref.shape[1] // 2
    return [ref.at[i, pl.ds(0, rows)], ref.at[i, pl.ds(rows, rows)]]


class Gather:
    def __init__(self, links, own, out):
        self.l, self.own, self.out = links, own, out
        zh, x, c = place()
        self.zh, self.x, self.c = zh, x, c
        self.zs = [{"dev": dev_of((zh + s) % 4, x, c)} for s in (1, 3)]
        self.xs = [{"dev": dev_of(zh, (x + s) % 4, c)} for s in (1, 3)]
        self.mate = {"dev": dev_of(zh, x, 1 - c)}
        self.waits = []

    def id(self, dz, dx, other=False):
        c = 1 - self.c if other else self.c
        return dev_of((self.zh + dz) % 4, (self.x + dx) % 4, c)

    def blk(self, dz, dx, other=False):
        return self.out.at[self.id(dz, dx, other)]

    def core(self, dz, dx, half=None):
        if half is None:
            here, there = self.blk(dz, dx), self.blk(dz, dx, True)
        else:
            here = halves(self.out, self.id(dz, dx))[half]
            there = halves(self.out, self.id(dz, dx, True))[half]
        self.waits.append((self.l.send(here, here, self.mate), there))

    def both_x(self, src, dst):
        return [self.l.send(src, dst, self.xs[0]), self.l.send(src, dst, self.xs[1])]

    def start(self):
        own, mine = self.own, self.blk(0, 0)
        self.z = [self.l.send(own, mine, self.zs[0]), self.l.send(own, mine, self.zs[1])]
        self.xh = {0: self.both_x(own, mine)}
        self.waits.append((self.l.send(own, mine, self.mate), self.blk(0, 0, True)))

    def z_near(self):
        self.zfar = []
        for s, dz in ((0, 3), (1, 1)):
            self.l.recv(self.z[s], self.blk(dz, 0))
            piece = halves(self.out, self.id(dz, 0))[s]
            self.zfar.append(self.l.send(piece, piece, self.zs[s]))
            self.xh[dz] = self.both_x(self.blk(dz, 0), self.blk(dz, 0))
            self.core(dz, 0)

    def x_near(self, dz):
        self.xfar = getattr(self, "xfar", {})
        self.xfar[dz] = []
        for s, dx in ((0, 3), (1, 1)):
            self.l.recv(self.xh[dz][s], self.blk(dz, dx))
            piece = halves(self.out, self.id(dz, dx))[s]
            self.xfar[dz].append(self.l.send(piece, piece, self.xs[s]))
            self.core(dz, dx)

    def z_far(self):
        self.xh2 = []
        for s in (0, 1):
            piece = halves(self.out, self.id(2, 0))[s]
            self.l.recv(self.zfar[s], piece)
            self.xh2.append(self.both_x(piece, piece))
        self.core(2, 0)

    def x_near_far(self):
        self.xfar[2] = []
        for s, dx in ((0, 3), (1, 1)):
            pieces = halves(self.out, self.id(2, dx))
            self.l.recv(self.xh2[s][s], pieces[s])
            self.xfar[2].append(self.l.send(pieces[s], pieces[s], self.xs[s]))
        for s, dx in ((0, 3), (1, 1)):
            pieces = halves(self.out, self.id(2, dx))
            self.l.recv(self.xh2[1 - s][s], pieces[1 - s])
            self.core(2, dx)

    def x_far(self, dz):
        pieces = halves(self.out, self.id(dz, 2))
        for s in (0, 1):
            self.l.recv(self.xfar[dz][s], pieces[s])
        self.core(dz, 2)

    def finish(self):
        for handle, region in self.waits:
            self.l.recv(handle, region)


GATHER_COPIES = 48


class ReqGather:
    def __init__(self, links, own, out):
        self.l, self.own, self.out = links, own, out
        r = lax.axis_index("req")
        self.zl, self.y = r // 4, r % 4
        self.zm = {"req": (1 - self.zl) * 4 + self.y}
        self.ys = [{"req": self.zl * 4 + (self.y + s) % 4} for s in (1, 3)]

    def id(self, other, dy):
        zl = 1 - self.zl if other else self.zl
        return zl * 4 + (self.y + dy) % 4

    def start(self):
        mine = self.out.at[self.id(False, 0)]
        self.zh = self.l.send(self.own, mine, self.zm)
        self.yh = [[self.l.send(self.own, mine, to) for to in self.ys]]

    def second(self):
        block = self.out.at[self.id(True, 0)]
        self.l.recv(self.zh, block)
        self.yh.append([self.l.send(block, block, to) for to in self.ys])

    def forward(self, other):
        self.fh = getattr(self, "fh", [])
        self.fh.append([])
        for s, dy in ((0, 3), (1, 1)):
            i = self.id(other, dy)
            self.l.recv(self.yh[other][s], self.out.at[i])
            piece = halves(self.out, i)[s]
            self.fh[other].append(self.l.send(piece, piece, self.ys[s]))

    def finish(self):
        for other in (0, 1):
            for s in (0, 1):
                self.l.recv(self.fh[other][s], halves(self.out, self.id(other, 2))[s])


def gather_kernel(
    hid, pool, wkv, gate, up, down,
    hid_all, kv_all, wkv_all, gate_all, up_all, down_all,
    pz, send_sems, recv_sems, local_sems,
):
    zh, x, c = place()
    r = lax.axis_index("req")
    links, local = Links(send_sems, recv_sems), Locals(local_sems)
    ag = Gather(links, hid, hid_all)
    mate_x, cross = {"dev": dev_of(zh, x + 1 - 2 * (x % 2), c)}, {"dev": dev_of(zh, 3 - x, c)}
    zfar = {"dev": dev_of((zh + 2) % 4, x, c)}
    weights = [ReqGather(links, *pair) for pair in ((gate, gate_all), (up, up_all), (down, down_all))]
    greet(ag.zs + ag.xs + [ag.mate, zfar, weights[0].zm] + weights[0].ys)

    ag.start()
    zstage = []
    for dz, to in ((1, ag.zs[0]), (3, ag.zs[1]), (2, zfar)):
        row = (zh + dz) % 4
        zstage.append((links.send(pool.at[pl.ds(2 * row, 2)], pz.at[zh], to), pz.at[(zh + 4 - dz) % 4]))
    for w in weights:
        w.start()
    j = (x % 2) * 2 + c
    w_mate = links.send(wkv, wkv_all.at[j], mate_x)
    w_core = links.send(wkv, wkv_all.at[j], ag.mate)
    own_pages = local.copy(pool.at[pl.ds(2 * zh, 2)], pz.at[zh])
    local.copy(hid, hid_all.at[dev_of(zh, x, c)])
    local.copy(wkv, wkv_all.at[j])
    for own, out in ((gate, gate_all), (up, up_all), (down, down_all)):
        local.copy(own, out.at[r])

    ag.z_near()
    ag.x_near(0)
    weights[0].second()
    own_pages.wait()
    for handle, region in zstage:
        links.recv(handle, region)
    pair = x // 2
    mx = x + 1 - 2 * (x % 2)
    local.copy(pz.at[:, pair], kv_all.at[x * 2 + c])
    p_mate = links.send(pz.at[:, pair], kv_all.at[x * 2 + c], mate_x)
    p_cross = links.send(pz.at[:, 1 - pair], kv_all.at[x * 2 + c], cross)
    p_core = [(links.send(pz.at[:, pair], kv_all.at[x * 2 + c], ag.mate), x)]
    ag.z_far()
    ag.x_near(3)
    ag.x_near(1)
    weights[1].second()
    weights[2].second()
    links.recv(w_mate, wkv_all.at[(1 - x % 2) * 2 + c])
    w_fwd = links.send(wkv_all.at[(1 - x % 2) * 2 + c], wkv_all.at[(1 - x % 2) * 2 + c], ag.mate)
    links.recv(p_cross, kv_all.at[(3 - x) * 2 + c])
    got = kv_all.at[(3 - x) * 2 + c]
    p_fwd = links.send(got, got, mate_x)
    p_core.append((links.send(got, got, ag.mate), 3 - x))
    links.recv(p_mate, kv_all.at[mx * 2 + c])
    got = kv_all.at[mx * 2 + c]
    p_core.append((links.send(got, got, ag.mate), mx))
    weights[0].forward(0)
    weights[0].forward(1)
    ag.x_near_far()
    ag.x_far(0)
    weights[1].forward(0)
    weights[1].forward(1)
    ag.x_far(3)
    ag.x_far(1)
    links.recv(p_fwd, kv_all.at[(3 - mx) * 2 + c])
    got = kv_all.at[(3 - mx) * 2 + c]
    p_core.append((links.send(got, got, ag.mate), 3 - mx))
    weights[2].forward(0)
    weights[2].forward(1)
    ag.x_far(2)
    links.recv(w_core, wkv_all.at[(x % 2) * 2 + 1 - c])
    links.recv(w_fwd, wkv_all.at[(1 - x % 2) * 2 + 1 - c])
    for handle, xx in p_core:
        links.recv(handle, kv_all.at[xx * 2 + 1 - c])
    for w in weights:
        w.finish()
    ag.finish()
    for copy in local.copies[1:]:
        copy.wait()
    links.drain()


def attention_kernel(q_ref, kv_ref, fresh_ref, bias_ref, out_ref, s_ref):
    tile = pl.program_id(0)
    q = q_ref[...]
    prefix = kv_ref.shape[0]
    chunks = prefix // KC

    def lanes_max(running, scores):
        for k in range(scores.shape[1] // 128):
            running = jnp.maximum(running, scores[:, k * 128 : (k + 1) * 128])
        return running

    def score_prefix(i, running):
        at = pl.ds(pl.multiple_of(i * KC, KC), KC)
        scores = transposed_product(q, kv_ref[at, :]) + bias_ref[:, at]
        s_ref[:, at] = scores
        return lanes_max(running, scores)

    running = lax.fori_loop(0, chunks, score_prefix, jnp.full((QT, 128), MASKED, F32))
    row = lax.broadcasted_iota(jnp.int32, (QT, QT), 0)
    col = lax.broadcasted_iota(jnp.int32, (QT, QT), 1)

    def score_fresh(i, running):
        at = pl.ds(pl.multiple_of(i * QT, QT), QT)
        scores = transposed_product(q, fresh_ref[at, :])
        scores = jnp.where(col + i * QT <= row + tile * QT, scores, MASKED)
        s_ref[:, pl.ds(pl.multiple_of(prefix + i * QT, QT), QT)] = scores
        return lanes_max(running, scores)

    running = lax.fori_loop(0, tile + 1, score_fresh, running)
    top = jnp.max(running, axis=1, keepdims=True)

    def weigh(at, keys, carried):
        total, summed = carried
        weights = jnp.exp(s_ref[:, at] - top)
        for k in range(weights.shape[1] // 128):
            total = total + weights[:, k * 128 : (k + 1) * 128]
        summed = summed + jnp.dot(weights.astype(BF), keys, preferred_element_type=F32)
        return total, summed

    def weigh_prefix(i, carried):
        at = pl.ds(pl.multiple_of(i * KC, KC), KC)
        return weigh(at, kv_ref[at, :], carried)

    def weigh_fresh(i, carried):
        at = pl.ds(pl.multiple_of(prefix + i * QT, QT), QT)
        return weigh(at, fresh_ref[pl.ds(pl.multiple_of(i * QT, QT), QT), :], carried)

    carried = (jnp.zeros((QT, 128), F32), jnp.zeros((QT, 2 * HD), F32))
    carried = lax.fori_loop(0, chunks, weigh_prefix, carried)
    total, summed = lax.fori_loop(0, tile + 1, weigh_fresh, carried)
    out_ref[...] = (summed / jnp.sum(total, axis=1, keepdims=True)).astype(BF)


class Scatter:
    def __init__(self, links, part, rc, q, xh, xf, res, zhalf, zfull):
        self.l = links
        self.part, self.rc, self.q, self.xh, self.xf = part, rc, q, xh, xf
        self.res, self.zhalf, self.zfull = res, zhalf, zfull
        zh, x, c = place()
        self.zh, self.x, self.c = zh, x, c
        self.zs = [{"dev": dev_of((zh + s) % 4, x, c)} for s in (1, 3)]
        self.xs = [{"dev": dev_of(zh, (x + s) % 4, c)} for s in (1, 3)]
        self.mate = {"dev": dev_of(zh, x, 1 - c)}
        self.dz = (2, 1, 3, 0)
        self.dx = (2, 1, 3, 0)
        self.ch, self.x1, self.x2 = {}, {}, {}

    def row(self, i):
        return (self.zh + self.dz[i]) % 4

    def block(self, i, k, other=False):
        return dev_of(self.row(i), (self.x + self.dx[k]) % 4, 1 - self.c if other else self.c)

    def cores(self, i):
        self.ch[i] = [self.l.send(self.part.at[self.block(i, k, True)], self.rc.at[i * 4 + k], self.mate) for k in range(4)]

    def pair_sum(self, i, k):
        self.l.recv(self.ch[i][k], self.rc.at[i * 4 + k])
        return self.part[self.block(i, k)].astype(F32) + self.rc[i * 4 + k].astype(F32)

    def first(self, i):
        self.q[i * 3] = self.pair_sum(i, 0).astype(BF)
        pieces = halves(self.q, i * 3)
        self.x1[i] = [self.l.send(pieces[s], self.xh.at[i * 2 + s], self.xs[s]) for s in (0, 1)]

    def second(self, i):
        self.x2[i] = []
        for s in (0, 1):
            value = self.pair_sum(i, 1 + s)
            self.l.recv(self.x1[i][s], self.xh.at[i * 2 + s])
            arrived = self.xh[i * 2 + s].astype(F32)
            top = value[:16] + arrived if s == 0 else value[:16]
            low = value[16:] + arrived if s == 1 else value[16:]
            self.q[i * 3 + 1 + s, pl.ds(0, 16)] = top.astype(BF)
            self.q[i * 3 + 1 + s, pl.ds(16, 16)] = low.astype(BF)
            self.x2[i].append(self.l.send(self.q.at[i * 3 + 1 + s], self.xf.at[i * 2 + s], self.xs[s]))

    def row_sum(self, i):
        value = self.pair_sum(i, 3)
        for s in (0, 1):
            self.l.recv(self.x2[i][s], self.xf.at[i * 2 + s])
            value = value + self.xf[i * 2 + s].astype(F32)
        return value

    def third(self, i):
        value = self.row_sum(i)
        if i == 0:
            self.res[0] = value.astype(BF)
            pieces = halves(self.res, 0)
            self.z1 = [self.l.send(pieces[s], self.zhalf.at[s], self.zs[s]) for s in (0, 1)]
            self.z2 = [None, None]
            return None
        if i == 3:
            for s in (0, 1):
                self.l.recv(self.z2[s], self.zfull.at[s])
                value = value + self.zfull[s].astype(F32)
            return value
        s = i - 1
        self.l.recv(self.z1[s], self.zhalf.at[s])
        arrived = self.zhalf[s].astype(F32)
        top = value[:16] + arrived if s == 0 else value[:16]
        low = value[16:] + arrived if s == 1 else value[16:]
        self.res[i, pl.ds(0, 16)] = top.astype(BF)
        self.res[i, pl.ds(16, 16)] = low.astype(BF)
        self.z2[s] = self.l.send(self.res.at[i], self.zfull.at[s], self.zs[s])
        return None

    def run(self, produce):
        produce(self.row(0))
        self.cores(0)
        produce(self.row(1))
        self.cores(1)
        self.first(0)
        produce(self.row(2))
        self.cores(2)
        self.first(1)
        self.second(0)
        produce(self.row(3))
        self.cores(3)
        self.first(2)
        self.second(1)
        self.third(0)
        self.first(3)
        self.second(2)
        self.third(1)
        self.second(3)
        self.third(2)
        return self.third(3)


SCATTER_COPIES = 36


def scatter_scratch(width):
    return [
        pltpu.VMEM((32, 32, width), BF),
        pltpu.VMEM((16, 32, width), BF),
        pltpu.VMEM((12, 32, width), BF),
        pltpu.VMEM((8, 16, width), BF),
        pltpu.VMEM((8, 32, width), BF),
        pltpu.VMEM((3, 32, width), BF),
        pltpu.VMEM((2, 16, width), BF),
        pltpu.VMEM((2, 32, width), BF),
    ]


def tail_kernel(att, wo, fresh, hid, gain, gate, up, down, out, kv_out, *scratch):
    s1, s2 = scratch[:8], scratch[8:16]
    normed, rows, act, send_sems, recv_sems, local_sems = scratch[16:]
    zh, x, c = place()
    d = lax.axis_index("dev")
    width = wo.shape[1]
    links, local = Links(send_sems, recv_sems), Locals(local_sems)
    one, two = Scatter(links, *s1), Scatter(links, *s2)
    ag = Gather(links, normed, rows)
    peers = [{"dev": (d + 4 * m) % 32} for m in range(1, 8)]
    greet(peers + ag.xs + [ag.mate])

    kv_h = []
    for m in range(1, 8):
        to = (d + 4 * m) % 32
        src = fresh.at[pl.ds(pl.multiple_of(to * 32, 32), 32)]
        kv_h.append(links.send(src, kv_out.at[d // 4], peers[m - 1]))
    own_kv = local.copy(fresh.at[pl.ds(pl.multiple_of(d * 32, 32), 32)], kv_out.at[d // 4])

    def project(row):
        tokens = att[pl.ds(pl.multiple_of(row * 256, 256), 256), :]

        def columns(n, carry):
            at = pl.ds(pl.multiple_of(n * 512, 512), 512)
            term = jnp.dot(tokens, wo[:, at], preferred_element_type=F32).astype(BF)
            one.part[pl.ds(row * 8, 8), :, at] = term.reshape(8, 32, 512)
            return carry

        lax.fori_loop(0, width // 512, columns, 0)

    residual = one.run(project) + hid[...].astype(F32)
    normed[...] = root_norm(residual, gain[...])
    ag.start()
    own_rows = local.copy(normed, rows.at[d])
    ag.z_near()
    ag.x_near(0)
    ag.z_far()
    ag.x_near(3)
    ag.x_near(1)
    ag.x_near_far()
    ag.x_far(0)
    ag.x_far(3)
    ag.x_far(1)
    ag.x_far(2)
    ag.finish()
    own_rows.wait()

    def feed(row):
        tokens = rows[pl.ds(row * 8, 8)].reshape(256, width)
        gated = transposed_product(tokens, gate[...])
        raised = transposed_product(tokens, up[...])
        act[...] = (gated / (1.0 + jnp.exp(-gated)) * raised).astype(BF)

        def columns(n, carry):
            at = pl.ds(pl.multiple_of(n * 512, 512), 512)
            term = jnp.dot(act[...], down[:, at], preferred_element_type=F32).astype(BF)
            two.part[pl.ds(row * 8, 8), :, at] = term.reshape(8, 32, 512)
            return carry

        lax.fori_loop(0, width // 512, columns, 0)

    out[...] = (residual + two.run(feed)).astype(BF)
    for m in range(1, 8):
        links.recv(kv_h[m - 1], kv_out.at[((d + 32 - 4 * m) % 32) // 4])
    own_kv.wait()
    links.drain()


def vmem(count):
    return [pl.BlockSpec(memory_space=pltpu.VMEM)] * count


def on_device(
    hidden_in, attention_gain, query_weight, keyval_weight, out_weight, feedforward_gain,
    gate_weight, up_weight, down_weight, prefix_pool, page_table, prefix_length,
):
    width = hidden_in.shape[2]
    tokens = 1024
    member = lax.axis_index("dev")
    length = prefix_length[0]
    own_tokens = hidden_in[0]
    slots = prefix_pool.shape[1] * PAGE
    pool = prefix_pool[0].transpose(2, 0, 1, 3).reshape(KVH, slots, 2 * HD)
    count = 110
    hidden_all, kv_all, wkv_all, gate_all, up_all, down_all = pl.pallas_call(
        gather_kernel,
        out_shape=[
            jax.ShapeDtypeStruct((32, 32, width), BF),
            jax.ShapeDtypeStruct((8, 4, slots, 2 * HD), BF),
            jax.ShapeDtypeStruct((4, 32, width), BF),
            jax.ShapeDtypeStruct((8, 32, width), BF),
            jax.ShapeDtypeStruct((8, 32, width), BF),
            jax.ShapeDtypeStruct((8, 32, width), BF),
        ],
        in_specs=vmem(6),
        out_specs=vmem(6),
        scratch_shapes=[
            pltpu.VMEM((4, 2, slots, 2 * HD), BF),
            pltpu.SemaphoreType.DMA((count,)),
            pltpu.SemaphoreType.DMA((count,)),
            pltpu.SemaphoreType.DMA((8,)),
        ],
        compiler_params=pltpu.CompilerParams(collective_id=0, has_side_effects=True, vmem_limit_bytes=60 << 20),
        name="gathers",
    )(own_tokens, pool, keyval_weight, gate_weight, up_weight, down_weight)

    logical = jnp.sum(
        jnp.where(
            page_table[0][None, :] == jnp.arange(256, dtype=jnp.int32)[:, None],
            jnp.arange(256, dtype=jnp.int32)[None, :],
            0,
        ),
        axis=1,
    )
    slot = logical[:, None] * PAGE + jnp.arange(PAGE, dtype=jnp.int32)[None, :]
    bias = jnp.where(slot < length, 0.0, MASKED).astype(F32)
    bias = bias.reshape(4, 8, slots).transpose(1, 0, 2).reshape(1, 32 * slots)

    normed = root_norm(hidden_all.reshape(tokens, width), attention_gain)
    columns = jnp.concatenate([query_weight, wkv_all.reshape(4 * 32, width)], axis=0)
    projected = transposed_product(normed, columns)
    positions = (length + jnp.arange(tokens, dtype=jnp.int32)).astype(F32)
    half = HD // 2
    frequency = ROPE_BASE ** (-jnp.arange(half, dtype=F32) / half)
    angles = positions[:, None] * frequency[None, :]
    cosine, sine = jnp.cos(angles), jnp.sin(angles)

    def rotate(vector):
        leading, trailing = vector[:, :half], vector[:, half:]
        return jnp.concatenate([leading * cosine - trailing * sine, trailing * cosine + leading * sine], axis=-1)

    queries = (rotate(projected[:, :HD]) * ATTENTION_SCALE).astype(BF)
    queries = jnp.concatenate([queries, jnp.zeros_like(queries)], axis=1)
    raw = projected[:, HD:].astype(BF)
    fresh = jnp.concatenate([rotate(raw[:, :HD].astype(F32)).astype(BF), raw[:, HD:]], axis=1)

    whole = lambda shape: pl.BlockSpec(shape, lambda i: (0, 0))
    attended = pl.pallas_call(
        attention_kernel,
        out_shape=jax.ShapeDtypeStruct((tokens, 2 * HD), BF),
        grid=(tokens // QT,),
        in_specs=[
            pl.BlockSpec((QT, 2 * HD), lambda i: (i, 0)),
            whole((32 * slots, 2 * HD)),
            whole((tokens, 2 * HD)),
            whole((1, 32 * slots)),
        ],
        out_specs=pl.BlockSpec((QT, 2 * HD), lambda i: (i, 0)),
        scratch_shapes=[pltpu.VMEM((QT, 32 * slots + tokens), F32)],
        name="attention",
    )(queries, kv_all.reshape(32 * slots, 2 * HD), fresh, bias)
    attended = attended[:, HD:]

    copies = GATHER_COPIES + 2 * SCATTER_COPIES + 8
    hidden_out, kv_out = pl.pallas_call(
        tail_kernel,
        out_shape=[jax.ShapeDtypeStruct((32, width), BF), jax.ShapeDtypeStruct((8, 32, 2 * HD), BF)],
        in_specs=vmem(8),
        out_specs=vmem(2),
        scratch_shapes=scatter_scratch(width) + scatter_scratch(width) + [
            pltpu.VMEM((32, width), BF),
            pltpu.VMEM((32, 32, width), BF),
            pltpu.VMEM((256, 256), BF),
            pltpu.SemaphoreType.DMA((copies,)),
            pltpu.SemaphoreType.DMA((copies,)),
            pltpu.SemaphoreType.DMA((2,)),
        ],
        compiler_params=pltpu.CompilerParams(collective_id=1, has_side_effects=True, vmem_limit_bytes=60 << 20),
        name="tail",
    )(
        attended, out_weight, fresh, own_tokens, feedforward_gain.reshape(1, width),
        gate_all.reshape(256, width), up_all.reshape(256, width), down_all.reshape(256, width),
    )
    return hidden_out[None], kv_out.transpose(1, 0, 2)[None]


def solution(mesh):
    placed = (
        P("req", "dev", None),
        P(),
        P("dev", None),
        P("dev", None),
        P("dev", None),
        P(),
        P(("req", "dev"), None),
        P(("req", "dev"), None),
        P(("req", "dev"), None),
        P("req", "dev", None, None, None),
        P("req", None),
        P("req"),
    )
    return jax.shard_map(
        on_device,
        mesh=mesh,
        in_specs=placed,
        out_specs=(P("req", "dev", None), P("req", "dev", None, None)),
        check_vma=False,
    )
```

```python
import jax
import jax.numpy as jnp
from jax import lax
from jax.experimental import pallas as pl
from jax.experimental.pallas import tpu as pltpu
from jax.sharding import PartitionSpec as P

MESH = pl.DeviceIdType.MESH
HQ = 32
KVH = 8
HD = 64
PAGE = 16
ROPE_BASE = 10000000.0
EPS = 1e-05
ATTENTION_SCALE = 0.015625
MASKED = -1e30
BF = jnp.bfloat16
F32 = jnp.float32
QT = 256
KC = 1024


def root_norm(activations, norm_gain):
    widened = activations.astype(F32)
    inverse_rms = lax.rsqrt(jnp.mean(widened * widened, axis=-1, keepdims=True) + EPS)
    return (widened * inverse_rms * norm_gain).astype(BF)


def transposed_product(left, right):
    return lax.dot_general(left, right, (((1,), (1,)), ((), ())), preferred_element_type=F32)


def dev_of(zh, x, c):
    return (zh * 4 + x) * 2 + c


def place():
    d = lax.axis_index("dev")
    return d // 8, (d // 2) % 4, d % 2


class Links:
    def __init__(self, send_sems, recv_sems):
        self.send_sems, self.recv_sems = send_sems, recv_sems
        self.copies = []

    def make(self, i, src, dst, to):
        return pltpu.make_async_remote_copy(
            src_ref=src,
            dst_ref=dst,
            send_sem=self.send_sems.at[i],
            recv_sem=self.recv_sems.at[i],
            device_id=to,
            device_id_type=MESH,
        )

    def send(self, src, dst, to):
        i = len(self.copies)
        copy = self.make(i, src, dst, to)
        copy.start()
        self.copies.append(copy)
        return i, to

    def recv(self, handle, region):
        i, to = handle
        self.make(i, region, region, to).wait_recv()

    def drain(self):
        for copy in self.copies:
            copy.wait_send()


class Locals:
    def __init__(self, sems):
        self.sems, self.copies = sems, []

    def copy(self, src, dst):
        copy = pltpu.make_async_copy(src, dst, self.sems.at[len(self.copies)])
        copy.start()
        self.copies.append(copy)
        return copy


def greet(partners):
    barrier = pltpu.get_barrier_semaphore()
    for partner in partners:
        pl.semaphore_signal(barrier, inc=1, device_id=partner, device_id_type=MESH)
    pl.semaphore_wait(barrier, len(partners))


def halves(ref, i):
    rows = ref.shape[1] // 2
    return [ref.at[i, pl.ds(0, rows)], ref.at[i, pl.ds(rows, rows)]]


class Gather:
    def __init__(self, links, own, out):
        self.l, self.own, self.out = links, own, out
        zh, x, c = place()
        self.zh, self.x, self.c = zh, x, c
        self.zs = [{"dev": dev_of((zh + s) % 4, x, c)} for s in (1, 3)]
        self.xs = [{"dev": dev_of(zh, (x + s) % 4, c)} for s in (1, 3)]
        self.mate = {"dev": dev_of(zh, x, 1 - c)}
        self.waits = {0: [], 1: [], 2: [], 3: []}
        self.xfar, self.xh = {}, {}

    def id(self, dz, dx, other=False):
        c = 1 - self.c if other else self.c
        return dev_of((self.zh + dz) % 4, (self.x + dx) % 4, c)

    def blk(self, dz, dx, other=False):
        return self.out.at[self.id(dz, dx, other)]

    def core(self, dz, dx):
        here, there = self.blk(dz, dx), self.blk(dz, dx, True)
        self.waits[dz].append((self.l.send(here, here, self.mate), there))

    def both_x(self, src, dst):
        return [self.l.send(src, dst, self.xs[0]), self.l.send(src, dst, self.xs[1])]

    def start(self):
        own, mine = self.own, self.blk(0, 0)
        self.z = [self.l.send(own, mine, self.zs[0]), self.l.send(own, mine, self.zs[1])]
        self.xh[0] = self.both_x(own, mine)
        self.waits[0].append((self.l.send(own, mine, self.mate), self.blk(0, 0, True)))

    def z_near(self):
        self.zfar = []
        for s, dz in ((0, 3), (1, 1)):
            self.l.recv(self.z[s], self.blk(dz, 0))
            piece = halves(self.out, self.id(dz, 0))[s]
            self.zfar.append(self.l.send(piece, piece, self.zs[s]))
            self.xh[dz] = self.both_x(self.blk(dz, 0), self.blk(dz, 0))
            self.core(dz, 0)

    def x_near(self, dz):
        self.xfar[dz] = []
        for s, dx in ((0, 3), (1, 1)):
            self.l.recv(self.xh[dz][s], self.blk(dz, dx))
            piece = halves(self.out, self.id(dz, dx))[s]
            self.xfar[dz].append(self.l.send(piece, piece, self.xs[s]))
            self.core(dz, dx)

    def z_far(self):
        self.xh2 = []
        for s in (0, 1):
            piece = halves(self.out, self.id(2, 0))[s]
            self.l.recv(self.zfar[s], piece)
            self.xh2.append(self.both_x(piece, piece))
        self.core(2, 0)

    def x_near_far(self):
        self.xfar[2] = []
        for s, dx in ((0, 3), (1, 1)):
            pieces = halves(self.out, self.id(2, dx))
            self.l.recv(self.xh2[s][s], pieces[s])
            self.xfar[2].append(self.l.send(pieces[s], pieces[s], self.xs[s]))
        for s, dx in ((0, 3), (1, 1)):
            pieces = halves(self.out, self.id(2, dx))
            self.l.recv(self.xh2[1 - s][s], pieces[1 - s])
            self.core(2, dx)

    def x_far(self, dz):
        pieces = halves(self.out, self.id(dz, 2))
        for s in (0, 1):
            self.l.recv(self.xfar[dz][s], pieces[s])
        self.core(dz, 2)

    def ready(self, dz):
        for handle, region in self.waits[dz]:
            self.l.recv(handle, region)


class WeightGather:
    def __init__(self, links, owns, out):
        self.l, self.owns, self.out = links, owns, out
        zh, x, c = place()
        r = lax.axis_index("req")
        self.zh, self.zl, self.y = zh, r // 4, r % 4
        self.zs = [{"dev": dev_of((zh + s) % 4, x, c)} for s in (1, 3)]
        self.ys = [{"req": self.zl * 4 + (self.y + s) % 4} for s in (1, 3)]
        self.yh, self.yfar = {}, {}

    def id(self, dz, dy):
        return ((self.zh + dz) % 4) * 4 + (self.y + dy) % 4

    def blk(self, dz, dy):
        return self.out.at[:, self.id(dz, dy)]

    def half(self, dz, dy, s):
        return self.out.at[:, self.id(dz, dy), pl.ds(16 * s, 16)]

    def spread(self, targets):
        mine = self.id(0, 0)
        return [[self.l.send(own, self.out.at[a, mine], to) for a, own in enumerate(self.owns)] for to in targets]

    def start_y(self):
        self.yh[0] = self.spread(self.ys)

    def start_z(self):
        self.z = self.spread(self.zs)

    def both_y(self, ref):
        return [self.l.send(ref, ref, to) for to in self.ys]

    def y_own(self):
        self.yfar[0] = []
        for s, dy in ((0, 3), (1, 1)):
            for a in range(3):
                self.l.recv(self.yh[0][s][a], self.out.at[a, self.id(0, dy)])
            piece = self.half(0, dy, s)
            self.yfar[0].append(self.l.send(piece, piece, self.ys[s]))

    def z_near(self):
        self.zfar = []
        for s, dz in ((0, 3), (1, 1)):
            for a in range(3):
                self.l.recv(self.z[s][a], self.out.at[a, self.id(dz, 0)])
            piece = self.half(dz, 0, s)
            self.zfar.append(self.l.send(piece, piece, self.zs[s]))
            self.yh[dz] = self.both_y(self.blk(dz, 0))

    def z_far(self):
        self.yh2 = []
        for s in (0, 1):
            piece = self.half(2, 0, s)
            self.l.recv(self.zfar[s], piece)
            self.yh2.append(self.both_y(piece))

    def y_near(self, dz):
        self.yfar[dz] = []
        for s, dy in ((0, 3), (1, 1)):
            self.l.recv(self.yh[dz][s], self.blk(dz, dy))
            piece = self.half(dz, dy, s)
            self.yfar[dz].append(self.l.send(piece, piece, self.ys[s]))

    def y_near_far(self):
        self.yfar[2] = []
        for s, dy in ((0, 3), (1, 1)):
            piece = self.half(2, dy, s)
            self.l.recv(self.yh2[s][s], piece)
            self.yfar[2].append(self.l.send(piece, piece, self.ys[s]))
        for s, dy in ((0, 3), (1, 1)):
            self.l.recv(self.yh2[1 - s][s], self.half(2, dy, 1 - s))

    def y_far(self, dz):
        for s in (0, 1):
            self.l.recv(self.yfar[dz][s], self.half(dz, 2, s))


class RowScatter:
    def __init__(self, links, part, rc, q, xh, xf):
        self.l = links
        self.part, self.rc, self.q, self.xh, self.xf = part, rc, q, xh, xf
        zh, x, c = place()
        self.x, self.c = x, c
        self.xs = [{"dev": dev_of(zh, (x + s) % 4, c)} for s in (1, 3)]
        self.mate = {"dev": dev_of(zh, x, 1 - c)}
        self.dx = (2, 1, 3, 0)

    def block(self, k, other=False):
        return ((self.x + self.dx[k]) % 4) * 2 + (1 - self.c if other else self.c)

    def cores(self):
        self.ch = [self.l.send(self.part.at[self.block(k, True)], self.rc.at[k], self.mate) for k in range(4)]

    def pair_sum(self, k):
        self.l.recv(self.ch[k], self.rc.at[k])
        return self.part[self.block(k)].astype(F32) + self.rc[k].astype(F32)

    def first(self):
        self.q[0] = self.pair_sum(0).astype(BF)
        pieces = halves(self.q, 0)
        self.x1 = [self.l.send(pieces[s], self.xh.at[s], self.xs[s]) for s in (0, 1)]

    def second(self):
        self.x2 = []
        for s in (0, 1):
            value = self.pair_sum(1 + s)
            self.l.recv(self.x1[s], self.xh.at[s])
            arrived = self.xh[s].astype(F32)
            top = value[:16] + arrived if s == 0 else value[:16]
            low = value[16:] + arrived if s == 1 else value[16:]
            self.q[1 + s, pl.ds(0, 16)] = top.astype(BF)
            self.q[1 + s, pl.ds(16, 16)] = low.astype(BF)
            self.x2.append(self.l.send(self.q.at[1 + s], self.xf.at[s], self.xs[s]))

    def total(self):
        value = self.pair_sum(3)
        for s in (0, 1):
            self.l.recv(self.x2[s], self.xf.at[s])
            value = value + self.xf[s].astype(F32)
        return value


class RowGather:
    def __init__(self, links, own, out):
        self.l, self.own, self.out = links, own, out
        zh, x, c = place()
        r = lax.axis_index("req")
        self.x, self.c = x, c
        self.zm = {"req": (1 - r // 4) * 4 + r % 4}
        self.xs = [{"dev": dev_of(zh, (x + s) % 4, c)} for s in (1, 3)]
        self.mate = {"dev": dev_of(zh, x, 1 - c)}
        self.waits, self.xh, self.xfar = [[], []], {}, {}

    def id(self, dx, other=False):
        return ((self.x + dx) % 4) * 2 + (1 - self.c if other else self.c)

    def core(self, row, dx, src=None):
        here, there = self.out.at[row, self.id(dx)], self.out.at[row, self.id(dx, True)]
        self.waits[row].append((self.l.send(here if src is None else src, here, self.mate), there))

    def both_x(self, row, src):
        dst = self.out.at[row, self.id(0)]
        self.xh[row] = [self.l.send(src, dst, to) for to in self.xs]

    def start(self):
        self.zh = self.l.send(self.own, self.out.at[1, self.id(0)], self.zm)
        self.both_x(0, self.own)
        self.core(0, 0, self.own)

    def second(self):
        block = self.out.at[1, self.id(0)]
        self.l.recv(self.zh, block)
        self.both_x(1, block)
        self.core(1, 0)

    def half(self, row, dx, s):
        return self.out.at[row, self.id(dx), pl.ds(16 * s, 16)]

    def near(self, row):
        self.xfar[row] = []
        for s, dx in ((0, 3), (1, 1)):
            self.l.recv(self.xh[row][s], self.out.at[row, self.id(dx)])
            piece = self.half(row, dx, s)
            self.xfar[row].append(self.l.send(piece, piece, self.xs[s]))
            self.core(row, dx)

    def far(self, row):
        for s in (0, 1):
            self.l.recv(self.xfar[row][s], self.half(row, 2, s))
        self.core(row, 2)

    def ready(self, row):
        for handle, region in self.waits[row]:
            self.l.recv(handle, region)


def layer_kernel(
    hid, pool, wq, wkv, wo, gate, up, down, gain_one, gain_two, cosine, sine, bias,
    out, kv_out,
    hid_all, pz, kv_all, wcat, wo_all, wall, nrm, q_all, fresh, s_ref, att_out, att_in,
    part1, rc1, q1, xh1, xf1, residual, n2, rows, act, part2, rc2, q2, xh2, xf2, zsend, zrecv,
    send_sems, recv_sems, local_sems,
):
    zh, x, c = place()
    d = lax.axis_index("dev")
    r = lax.axis_index("req")
    y = r % 4
    width = hid.shape[1]
    links, local = Links(send_sems, recv_sems), Locals(local_sems)
    ag = Gather(links, hid, hid_all)
    ffw = WeightGather(links, (gate, up, down), wall)
    ag2 = RowGather(links, n2, rows)
    mx = x + 1 - 2 * (x % 2)
    mate_x, cross = {"dev": dev_of(zh, mx, c)}, {"dev": dev_of(zh, 3 - x, c)}
    zfar = {"dev": dev_of((zh + 2) % 4, x, c)}
    peers = {m: {"dev": (d + 4 * m) % 32} for m in range(1, 8)}
    greet(ag.zs + ag.xs + [ag.mate, zfar, ag2.zm] + ffw.ys + [peers[m] for m in (1, 3, 5, 7)])

    ag.start()
    ffw.start_y()
    j = (x % 2) * 2 + c
    w_mate = links.send(wkv, wcat.at[2 + j], mate_x)
    w_core = links.send(wkv, wcat.at[2 + j], ag.mate)
    own_pages = local.copy(pool.at[pl.ds(2 * zh, 2)], pz.at[zh])
    local.copy(hid, hid_all.at[d])
    local.copy(wkv, wcat.at[2 + j])
    local.copy(wq, wcat.at[pl.ds(0, 2)])
    own_wo = local.copy(wo, wo_all.at[zh, pl.ds(64, 64)])
    ffw_own = [local.copy(own, wall.at[a, ffw.id(0, 0)]) for a, own in enumerate((gate, up, down))]
    for k in range(4):
        wo_all[k, pl.ds(0, 64)] = jnp.zeros((64, width), BF)

    ag.z_near()
    zstage = []
    for dz, to in ((2, zfar), (1, ag.zs[0]), (3, ag.zs[1])):
        row = (zh + dz) % 4
        zstage.append((links.send(pool.at[pl.ds(2 * row, 2)], pz.at[zh], to), pz.at[(zh + 4 - dz) % 4]))
    quarter = pl.ds(64 + 16 * y, 16)
    wo_own = wo.at[pl.ds(16 * y, 16)]
    wo_z = [links.send(wo_own, wo_all.at[zh, quarter], to) for to in ag.zs]
    ffw.start_z()
    ag.x_near(0)
    ag.z_far()
    own_pages.wait()
    for handle, region in zstage:
        links.recv(handle, region)
    pair = x // 2
    local.copy(pz.at[:, pair], kv_all.at[x * 2 + c])
    p_cross = links.send(pz.at[:, 1 - pair], kv_all.at[x * 2 + c], cross)
    p_mate = links.send(pz.at[:, pair], kv_all.at[x * 2 + c], mate_x)
    p_core = [(links.send(pz.at[:, pair], kv_all.at[x * 2 + c], ag.mate), x)]
    ag.x_near(3)
    ag.x_near(1)
    ag.x_far(0)
    links.recv(w_mate, wcat.at[2 + (1 - x % 2) * 2 + c])
    got = wcat.at[2 + (1 - x % 2) * 2 + c]
    w_fwd = links.send(got, got, ag.mate)
    links.recv(w_core, wcat.at[2 + (x % 2) * 2 + 1 - c])
    ffw.y_own()
    wo_far = []
    for s, dz in ((0, 3), (1, 1)):
        block = (zh + dz) % 4
        links.recv(wo_z[s], wo_all.at[block, quarter])
        piece = wo_all.at[block, quarter, pl.ds(s * (width // 2), width // 2)]
        wo_far.append(links.send(piece, piece, ag.zs[s]))
    links.recv(w_fwd, wcat.at[2 + (1 - x % 2) * 2 + 1 - c])
    for copy in local.copies[1:4]:
        copy.wait()

    lane = lax.broadcasted_iota(jnp.int32, (256, 2 * HD), 1)
    first_half = lane % HD < HD // 2

    def project(dz):
        row = (zh + dz) % 4
        at = pl.ds(pl.multiple_of(row * 256, 256), 256)

        def norm(i, carry):
            nrm[pl.ds(pl.multiple_of(i * 32, 32), 32), :] = root_norm(hid_all[row * 8 + i], gain_one[...])
            return carry

        lax.fori_loop(0, 8, norm, 0)
        projected = transposed_product(nrm[...], wcat[...].reshape(192, width))
        pairs = projected[:, : 2 * HD]
        pairs = jnp.where(lane < HD, pairs, pairs.astype(BF).astype(F32))
        swapped = jnp.where(first_half, pltpu.roll(pairs, 96, 1), pltpu.roll(pairs, 32, 1))
        turned = pairs * cosine[at, :] + swapped * sine[at, :]
        q_all[at, :] = jnp.where(lane < HD, turned * ATTENTION_SCALE, 0.0).astype(BF)
        fresh[at, :] = jnp.concatenate([turned[:, HD:], projected[:, 2 * HD :]], axis=1).astype(BF)

    ag.ready(0)
    project(0)
    ag.x_near_far()
    ag.x_far(3)
    ag.x_far(1)
    got = kv_all.at[(3 - x) * 2 + c]
    links.recv(p_cross, got)
    p_fwd = links.send(got, got, mate_x)
    p_core.append((links.send(got, got, ag.mate), 3 - x))
    ag.ready(3)
    project(3)
    got = kv_all.at[mx * 2 + c]
    links.recv(p_mate, got)
    p_core.append((links.send(got, got, ag.mate), mx))
    ag.ready(1)
    project(1)
    for s in (0, 1):
        links.recv(wo_far[s], wo_all.at[(zh + 2) % 4, quarter, pl.ds(s * (width // 2), width // 2)])
    own_wo.wait()

    def wo_rows(dy):
        return pl.ds(64 + 16 * ((y + dy) % 4), 16)

    wo_y = []
    for to in ffw.ys:
        wo_y.append([links.send(wo_all.at[(zh + dz) % 4, quarter], wo_all.at[(zh + dz) % 4, quarter], to) for dz in (1, 2, 3)])
    ag.x_far(2)
    ag.ready(2)
    project(2)
    got = kv_all.at[(3 - mx) * 2 + c]
    links.recv(p_fwd, got)
    p_core.append((links.send(got, got, ag.mate), 3 - mx))
    kv_h = []
    for m in range(1, 8):
        src = fresh.at[pl.ds(pl.multiple_of(((d + 4 * m) % 32) * 32, 32), 32)]
        kv_h.append(links.send(src, kv_out.at[d // 4], peers[m]))
    own_kv = local.copy(fresh.at[pl.ds(pl.multiple_of(d * 32, 32), 32)], kv_out.at[d // 4])
    for handle, xx in p_core:
        links.recv(handle, kv_all.at[xx * 2 + 1 - c])
    local.copies[4 + 4].wait()

    prefix = 4096
    per_block = KC // 512

    def lanes_max(running, scores):
        for k in range(scores.shape[1] // 128):
            running = jnp.maximum(running, scores[:, k * 128 : (k + 1) * 128])
        return running

    def attend(tile, out_to):
        q = q_all[pl.ds(pl.multiple_of(tile * QT, QT), QT), :]

        def keys_at(i):
            return kv_all[pl.ds(i * per_block, per_block)].reshape(KC, 2 * HD)

        def score_prefix(i, running):
            at = pl.ds(pl.multiple_of(i * KC, KC), KC)
            scores = transposed_product(q, keys_at(i)) + bias[:, at]
            s_ref[:, at] = scores
            return lanes_max(running, scores)

        running = lax.fori_loop(0, prefix // KC, score_prefix, jnp.full((QT, 128), MASKED, F32), unroll=2)
        row = lax.broadcasted_iota(jnp.int32, (QT, QT), 0)
        col = lax.broadcasted_iota(jnp.int32, (QT, QT), 1)

        def score_fresh(i, running):
            at = pl.ds(pl.multiple_of(i * QT, QT), QT)
            scores = transposed_product(q, fresh[at, :])
            scores = jnp.where(col + i * QT <= row + tile * QT, scores, MASKED)
            s_ref[:, pl.ds(pl.multiple_of(prefix + i * QT, QT), QT)] = scores
            return lanes_max(running, scores)

        running = lax.fori_loop(0, tile + 1, score_fresh, running)
        top = jnp.broadcast_to(jnp.max(running, axis=1, keepdims=True), (QT, 128))

        def weigh(at, keys, carried):
            total, summed = carried
            scores = s_ref[:, at]
            pieces = []
            for k in range(scores.shape[1] // 128):
                weights = jnp.exp(scores[:, k * 128 : (k + 1) * 128] - top)
                total = total + weights
                pieces.append(weights.astype(BF))
            weights = jnp.concatenate(pieces, axis=1)
            return total, summed + jnp.dot(weights, keys, preferred_element_type=F32)

        def weigh_prefix(i, carried):
            return weigh(pl.ds(pl.multiple_of(i * KC, KC), KC), keys_at(i), carried)

        def weigh_fresh(i, carried):
            at = pl.ds(pl.multiple_of(prefix + i * QT, QT), QT)
            return weigh(at, fresh[pl.ds(pl.multiple_of(i * QT, QT), QT), :], carried)

        carried = (jnp.zeros((QT, 128), F32), jnp.zeros((QT, 2 * HD), F32))
        carried = lax.fori_loop(0, prefix // KC, weigh_prefix, carried, unroll=2)
        total, summed = lax.fori_loop(0, tile + 1, weigh_fresh, carried)
        out_to[...] = (summed / jnp.sum(total, axis=1, keepdims=True)).astype(BF)

    a2a = []
    steps = weight_steps(ffw)
    for i, (dz, to) in enumerate(((2, zfar), (1, ag.zs[0]), (3, ag.zs[1]))):
        attend((zh + dz) % 4, att_out.at[i])
        a2a.append((links.send(att_out.at[i], att_in.at[zh], to), att_in.at[(zh + 4 - dz) % 4]))
        for step in steps[i]:
            step()
    wo_yfar = []
    for s, dy in ((0, 3), (1, 1)):
        for k, dz in enumerate((1, 2, 3)):
            links.recv(wo_y[s][k], wo_all.at[(zh + dz) % 4, wo_rows(dy)])
        for dz in (1, 2, 3):
            piece = wo_all.at[(zh + dz) % 4, wo_rows(dy), pl.ds(s * (width // 2), width // 2)]
            wo_yfar.append((links.send(piece, piece, ffw.ys[s]), dz, s))
    attend(zh, att_in.at[zh])
    for step in steps[3]:
        step()
    for handle, dz, s in wo_yfar:
        links.recv(handle, wo_all.at[(zh + dz) % 4, wo_rows(2), pl.ds(s * (width // 2), width // 2)])
    for handle, region in a2a:
        links.recv(handle, region)

    one = RowScatter(links, part1, rc1, q1, xh1, xf1)

    def out_columns(n, carry):
        at = pl.ds(pl.multiple_of(n * 512, 512), 512)
        term = None
        for k in (0, 2):
            heads = jnp.concatenate([att_in[k], att_in[k + 1]], axis=1)
            product = jnp.dot(heads, wo_all[pl.ds(k, 2), :, at].reshape(256, 512), preferred_element_type=F32)
            term = product if term is None else term + product
        part1[:, :, at] = term.astype(BF).reshape(8, 32, 512)
        return carry

    lax.fori_loop(0, width // 512, out_columns, 0)
    one.cores()
    one.first()
    one.second()
    residual[...] = one.total() + hid[...].astype(F32)
    n2[...] = root_norm(residual[...], gain_two[...])
    ag2.start()
    own_rows = local.copy(n2, rows.at[0, x * 2 + c])
    for step in steps[4]:
        step()
    ag2.second()
    ag2.near(0)
    ag2.near(1)
    ag2.far(0)
    ag2.far(1)
    ag2.ready(0)
    own_rows.wait()
    for step in steps[5]:
        step()
    for copy in ffw_own:
        copy.wait()

    twos = [RowScatter(links, part2.at[i], rc2.at[i], q2.at[i], xh2.at[i], xf2.at[i]) for i in (0, 1)]

    def feed(row):
        def units(h, carry):
            tokens = rows[row].reshape(256, width)
            some = pl.ds(h * 8, 8)
            gated = transposed_product(tokens, wall[0, some].reshape(256, width))
            raised = transposed_product(tokens, wall[1, some].reshape(256, width))
            act[h] = (gated / (1.0 + jnp.exp(-gated)) * raised).astype(BF)
            return carry

        lax.fori_loop(0, 2, units, 0)

        def columns(n, carry):
            at = pl.ds(pl.multiple_of(n * 512, 512), 512)
            activated = jnp.concatenate([act[0], act[1]], axis=1)
            term = jnp.dot(activated, wall[2, :, :, at].reshape(512, 512), preferred_element_type=F32)
            part2[row, :, :, at] = term.astype(BF).reshape(8, 32, 512)
            return carry

        lax.fori_loop(0, width // 512, columns, 0)

    feed(0)
    twos[0].cores()
    ag2.ready(1)
    feed(1)
    twos[1].cores()
    twos[1].first()
    twos[0].first()
    twos[1].second()
    twos[0].second()
    zsend[...] = twos[1].total().astype(BF)
    last = links.send(zsend, zrecv, ag2.zm)
    value = residual[...] + twos[0].total()
    links.recv(last, zrecv)
    out[...] = (value + zrecv[...].astype(F32)).astype(BF)
    for m in range(1, 8):
        links.recv(kv_h[m - 1], kv_out.at[((d + 32 - 4 * m) % 32) // 4])
    own_kv.wait()
    links.drain()


def weight_steps(ffw):
    return [
        [],
        [ffw.z_near],
        [],
        [ffw.z_far, lambda: ffw.y_near(3), lambda: ffw.y_near(1)],
        [],
        [ffw.y_near_far, lambda: ffw.y_far(0), lambda: ffw.y_far(3), lambda: ffw.y_far(1), lambda: ffw.y_far(2)],
    ]


def vmem(count):
    return [pl.BlockSpec(memory_space=pltpu.VMEM)] * count


def on_device(
    hidden_in, attention_gain, query_weight, keyval_weight, out_weight, feedforward_gain,
    gate_weight, up_weight, down_weight, prefix_pool, page_table, prefix_length,
):
    width = hidden_in.shape[2]
    tokens = 1024
    length = prefix_length[0]
    slots = prefix_pool.shape[1] * PAGE
    pool = prefix_pool[0].transpose(2, 0, 1, 3).reshape(KVH, slots, 2 * HD)

    logical = jnp.sum(
        jnp.where(
            page_table[0][None, :] == jnp.arange(256, dtype=jnp.int32)[:, None],
            jnp.arange(256, dtype=jnp.int32)[None, :],
            0,
        ),
        axis=1,
    )
    slot = logical[:, None] * PAGE + jnp.arange(PAGE, dtype=jnp.int32)[None, :]
    bias = jnp.where(slot < length, 0.0, MASKED).astype(F32)
    bias = bias.reshape(4, 8, slots).transpose(1, 0, 2).reshape(1, 32 * slots)

    positions = (length + jnp.arange(tokens, dtype=jnp.int32)).astype(F32)
    half = HD // 2
    frequency = ROPE_BASE ** (-jnp.arange(half, dtype=F32) / half)
    angles = positions[:, None] * frequency[None, :]
    cosine, sine = jnp.cos(angles), jnp.sin(angles)
    cosine = jnp.concatenate([cosine] * 4, axis=1)
    sine = jnp.concatenate([-sine, sine, -sine, sine], axis=1)

    buffers = [
        ((32, 32, width), BF),
        ((4, 2, slots, 2 * HD), BF),
        ((8, 4, slots, 2 * HD), BF),
        ((6, 32, width), BF),
        ((4, 128, width), BF),
        ((3, 16, 32, width), BF),
        ((256, width), BF),
        ((tokens, 2 * HD), BF),
        ((tokens, 2 * HD), BF),
        ((QT, 32 * slots + tokens), F32),
        ((3, 256, 2 * HD), BF),
        ((4, 256, 2 * HD), BF),
        ((8, 32, width), BF),
        ((4, 32, width), BF),
        ((3, 32, width), BF),
        ((2, 16, width), BF),
        ((2, 32, width), BF),
        ((32, width), F32),
        ((32, width), BF),
        ((2, 8, 32, width), BF),
        ((2, 256, 256), BF),
        ((2, 8, 32, width), BF),
        ((2, 4, 32, width), BF),
        ((2, 3, 32, width), BF),
        ((2, 2, 16, width), BF),
        ((2, 2, 32, width), BF),
        ((32, width), BF),
        ((32, width), BF),
    ]
    hidden_out, kv_out = pl.pallas_call(
        layer_kernel,
        out_shape=[jax.ShapeDtypeStruct((32, width), BF), jax.ShapeDtypeStruct((8, 32, 2 * HD), BF)],
        in_specs=vmem(13),
        out_specs=vmem(2),
        scratch_shapes=[pltpu.VMEM(*b) for b in buffers] + [
            pltpu.SemaphoreType.DMA((COPIES,)),
            pltpu.SemaphoreType.DMA((COPIES,)),
            pltpu.SemaphoreType.DMA((16,)),
        ],
        compiler_params=pltpu.CompilerParams(collective_id=0, has_side_effects=True, vmem_limit_bytes=60 << 20),
        name="layer",
    )(
        hidden_in[0], pool, query_weight.reshape(2, 32, width), keyval_weight, out_weight,
        gate_weight, up_weight, down_weight,
        attention_gain.reshape(1, width), feedforward_gain.reshape(1, width), cosine, sine, bias,
    )
    return hidden_out[None], kv_out.transpose(1, 0, 2)[None]


COPIES = 200


def solution(mesh):
    placed = (
        P("req", "dev", None),
        P(),
        P("dev", None),
        P("dev", None),
        P("dev", None),
        P(),
        P(("req", "dev"), None),
        P(("req", "dev"), None),
        P(("req", "dev"), None),
        P("req", "dev", None, None, None),
        P("req", None),
        P("req"),
    )
    return jax.shard_map(
        on_device,
        mesh=mesh,
        in_specs=placed,
        out_specs=(P("req", "dev", None), P("req", "dev", None, None)),
        check_vma=False,
    )
```

```python
import jax
import jax.numpy as jnp
from jax import lax
from jax.experimental import pallas as pl
from jax.experimental.pallas import tpu as pltpu
from jax.sharding import PartitionSpec as P

MESH = pl.DeviceIdType.MESH
HQ = 32
KVH = 8
HD = 64
PAGE = 16
ROPE_BASE = 10000000.0
EPS = 1e-05
ATTENTION_SCALE = 0.015625
MASKED = -1e30
BF = jnp.bfloat16
F32 = jnp.float32
QT = 256
KC = 1024


def root_norm(activations, norm_gain):
    widened = activations.astype(F32)
    inverse_rms = lax.rsqrt(jnp.mean(widened * widened, axis=-1, keepdims=True) + EPS)
    return (widened * inverse_rms * norm_gain).astype(BF)


def transposed_product(left, right):
    return lax.dot_general(left, right, (((1,), (1,)), ((), ())), preferred_element_type=F32)


def dev_of(zh, x, c):
    return (zh * 4 + x) * 2 + c


def place():
    d = lax.axis_index("dev")
    return d // 8, (d // 2) % 4, d % 2


class Links:
    def __init__(self, send_sems, recv_sems):
        self.send_sems, self.recv_sems = send_sems, recv_sems
        self.copies = []

    def make(self, i, src, dst, to):
        return pltpu.make_async_remote_copy(
            src_ref=src,
            dst_ref=dst,
            send_sem=self.send_sems.at[i],
            recv_sem=self.recv_sems.at[i],
            device_id=to,
            device_id_type=MESH,
        )

    def send(self, src, dst, to):
        i = len(self.copies)
        copy = self.make(i, src, dst, to)
        copy.start()
        self.copies.append(copy)
        return i, to

    def recv(self, handle, region):
        i, to = handle
        self.make(i, region, region, to).wait_recv()

    def drain(self):
        for copy in self.copies:
            copy.wait_send()


class Locals:
    def __init__(self, sems):
        self.sems, self.copies = sems, []

    def copy(self, src, dst):
        copy = pltpu.make_async_copy(src, dst, self.sems.at[len(self.copies)])
        copy.start()
        self.copies.append(copy)
        return copy


def greet(partners):
    barrier = pltpu.get_barrier_semaphore()
    for partner in partners:
        pl.semaphore_signal(barrier, inc=1, device_id=partner, device_id_type=MESH)
    pl.semaphore_wait(barrier, len(partners))


def halves(ref, i):
    rows = ref.shape[1] // 2
    return [ref.at[i, pl.ds(0, rows)], ref.at[i, pl.ds(rows, rows)]]


class Ring:
    def __init__(self, links, i, tos, blk, half, own=None, mate=None, there=None):
        self.l, self.i, self.tos, self.blk, self.half = links, i, tos, blk, half
        self.own = blk(i) if own is None else own
        self.mate, self.there = mate, there
        self.waits = []

    def core(self, j, src=None):
        if self.mate is not None:
            here = self.blk(j)
            self.waits.append((self.l.send(here if src is None else src, here, self.mate), self.there(j)))

    def start(self, core=True):
        mine = self.blk(self.i)
        self.h = [self.l.send(self.own, mine, to) for to in self.tos]
        if core:
            self.core(self.i, self.own)

    def near(self):
        self.f = []
        for s, off in ((0, 3), (1, 1)):
            j = (self.i + off) % 4
            self.l.recv(self.h[s], self.blk(j))
            piece = self.half(j, s)
            self.f.append(self.l.send(piece, piece, self.tos[s]))
            self.core(j)

    def far(self):
        j = (self.i + 2) % 4
        for s in (0, 1):
            self.l.recv(self.f[s], self.half(j, s))
        self.core(j)

    def ready(self):
        for handle, region in self.waits:
            self.l.recv(handle, region)


class PlaneGather:
    def __init__(self, links, own, out):
        self.l, self.own, self.out = links, own, out
        zh, x, c = place()
        r = lax.axis_index("req")
        self.zh, self.zl, self.y = zh, r // 4, r % 4
        self.zs = [{"dev": dev_of((zh + s) % 4, x, c)} for s in (1, 3)]
        self.ys = [{"req": self.zl * 4 + (self.y + s) % 4} for s in (1, 3)]
        self.yh, self.yfar = {}, {}

    def id(self, dz, dy):
        return ((self.zh + dz) % 4) * 4 + (self.y + dy) % 4

    def blk(self, dz, dy):
        return self.out.at[self.id(dz, dy)]

    def half(self, dz, dy, s):
        return self.out.at[self.id(dz, dy), pl.ds(16 * s, 16)]

    def start_y(self):
        self.yh[0] = [self.l.send(self.own, self.blk(0, 0), to) for to in self.ys]

    def start_z(self):
        self.z = [self.l.send(self.own, self.blk(0, 0), to) for to in self.zs]

    def both_y(self, ref):
        return [self.l.send(ref, ref, to) for to in self.ys]

    def z_near(self):
        self.zfar = []
        for s, dz in ((0, 3), (1, 1)):
            self.l.recv(self.z[s], self.blk(dz, 0))
            piece = self.half(dz, 0, s)
            self.zfar.append(self.l.send(piece, piece, self.zs[s]))
            self.yh[dz] = self.both_y(self.blk(dz, 0))

    def z_far(self):
        self.yh2 = []
        for s in (0, 1):
            piece = self.half(2, 0, s)
            self.l.recv(self.zfar[s], piece)
            self.yh2.append(self.both_y(piece))

    def y_near(self, dz):
        self.yfar[dz] = []
        for s, dy in ((0, 3), (1, 1)):
            self.l.recv(self.yh[dz][s], self.blk(dz, dy))
            piece = self.half(dz, dy, s)
            self.yfar[dz].append(self.l.send(piece, piece, self.ys[s]))

    def y_near_far(self):
        self.yfar[2] = []
        for s, dy in ((0, 3), (1, 1)):
            piece = self.half(2, dy, s)
            self.l.recv(self.yh2[s][s], piece)
            self.yfar[2].append(self.l.send(piece, piece, self.ys[s]))
        for s, dy in ((0, 3), (1, 1)):
            self.l.recv(self.yh2[1 - s][s], self.half(2, dy, 1 - s))

    def y_far(self, dz):
        for s in (0, 1):
            self.l.recv(self.yfar[dz][s], self.half(dz, 2, s))


class RowScatter:
    def __init__(self, links, part, rc, q, xh, xf, along_z=False):
        self.l = links
        self.part, self.rc, self.q, self.xh, self.xf = part, rc, q, xh, xf
        zh, x, c = place()
        self.x, self.c = zh if along_z else x, c
        if along_z:
            self.xs = [{"dev": dev_of((zh + s) % 4, x, c)} for s in (1, 3)]
        else:
            self.xs = [{"dev": dev_of(zh, (x + s) % 4, c)} for s in (1, 3)]
        self.mate = {"dev": dev_of(zh, x, 1 - c)}
        self.dx = (2, 1, 3, 0)

    def block(self, k, other=False):
        return ((self.x + self.dx[k]) % 4) * 2 + (1 - self.c if other else self.c)

    def cores(self):
        self.ch = [self.l.send(self.part.at[self.block(k, True)], self.rc.at[k], self.mate) for k in range(4)]

    def pair_sum(self, k):
        self.l.recv(self.ch[k], self.rc.at[k])
        return self.part[self.block(k)].astype(F32) + self.rc[k].astype(F32)

    def first(self):
        self.q[0] = self.pair_sum(0).astype(BF)
        pieces = halves(self.q, 0)
        self.x1 = [self.l.send(pieces[s], self.xh.at[s], self.xs[s]) for s in (0, 1)]

    def second(self):
        self.x2 = []
        for s in (0, 1):
            value = self.pair_sum(1 + s)
            self.l.recv(self.x1[s], self.xh.at[s])
            arrived = self.xh[s].astype(F32)
            top = value[:16] + arrived if s == 0 else value[:16]
            low = value[16:] + arrived if s == 1 else value[16:]
            self.q[1 + s, pl.ds(0, 16)] = top.astype(BF)
            self.q[1 + s, pl.ds(16, 16)] = low.astype(BF)
            self.x2.append(self.l.send(self.q.at[1 + s], self.xf.at[s], self.xs[s]))

    def total(self):
        value = self.pair_sum(3)
        for s in (0, 1):
            self.l.recv(self.x2[s], self.xf.at[s])
            value = value + self.xf[s].astype(F32)
        return value


class RowGather:
    def __init__(self, links, own, out):
        self.l, self.own, self.out = links, own, out
        zh, x, c = place()
        r = lax.axis_index("req")
        self.x, self.c = x, c
        self.zm = {"req": (1 - r // 4) * 4 + r % 4}
        self.xs = [{"dev": dev_of(zh, (x + s) % 4, c)} for s in (1, 3)]
        self.mate = {"dev": dev_of(zh, x, 1 - c)}
        self.waits, self.xh, self.xfar = [[], []], {}, {}

    def id(self, dx, other=False):
        return ((self.x + dx) % 4) * 2 + (1 - self.c if other else self.c)

    def core(self, row, dx, src=None):
        here, there = self.out.at[row, self.id(dx)], self.out.at[row, self.id(dx, True)]
        self.waits[row].append((self.l.send(here if src is None else src, here, self.mate), there))

    def both_x(self, row, src):
        dst = self.out.at[row, self.id(0)]
        self.xh[row] = [self.l.send(src, dst, to) for to in self.xs]

    def start(self):
        self.zh = self.l.send(self.own, self.out.at[1, self.id(0)], self.zm)
        self.both_x(0, self.own)
        self.core(0, 0, self.own)

    def second(self):
        block = self.out.at[1, self.id(0)]
        self.l.recv(self.zh, block)
        self.both_x(1, block)
        self.core(1, 0)

    def half(self, row, dx, s):
        return self.out.at[row, self.id(dx), pl.ds(16 * s, 16)]

    def near(self, row):
        self.xfar[row] = []
        for s, dx in ((0, 3), (1, 1)):
            self.l.recv(self.xh[row][s], self.out.at[row, self.id(dx)])
            piece = self.half(row, dx, s)
            self.xfar[row].append(self.l.send(piece, piece, self.xs[s]))
            self.core(row, dx)

    def far(self, row):
        for s in (0, 1):
            self.l.recv(self.xfar[row][s], self.half(row, 2, s))
        self.core(row, 2)

    def ready(self, row):
        for handle, region in self.waits[row]:
            self.l.recv(handle, region)


def layer_kernel(
    hid, pool, wq, wkv, wo, gate, up, down, gain_one, gain_two, cosine, sine, bias,
    out, kv_out,
    hid_col, relay, kv_all, wq_all, wkv_all, wo_all, wall, nrm, q_all, fresh, s_ref, att,
    part1, rc1, q1, xh1, xf1, residual, n2, rows, act, part2, rc2, q2, xh2, xf2, zsend, zrecv,
    send_sems, recv_sems, local_sems,
):
    zh, x, c = place()
    r = lax.axis_index("req")
    width = hid.shape[1]
    links, local = Links(send_sems, recv_sems), Locals(local_sems)
    zs = [{"dev": dev_of((zh + s) % 4, x, c)} for s in (1, 3)]
    xs = [{"dev": dev_of(zh, (x + s) % 4, c)} for s in (1, 3)]
    mate = {"dev": dev_of(zh, x, 1 - c)}
    planes = [PlaneGather(links, own, wall.at[a]) for a, own in enumerate((gate, up, down))]
    ag2 = RowGather(links, n2, rows)
    column = {(dz, dc): {"dev": dev_of((zh + dz) % 4, x, (c + dc) % 2)} for dz in range(4) for dc in range(2)}
    del column[0, 0]

    hidden = Ring(
        links, zh, zs, lambda j: hid_col.at[j * 2 + c], lambda j, s: hid_col.at[j * 2 + c, pl.ds(16 * s, 16)],
        hid, mate, lambda j: hid_col.at[j * 2 + 1 - c],
    )
    q_ring = Ring(links, x, xs, lambda j: wq_all.at[j], lambda j, s: wq_all.at[j, s], wq)
    kv_ring = Ring(
        links, x, xs, lambda j: wkv_all.at[j * 2 + c], lambda j, s: wkv_all.at[j * 2 + c, pl.ds(16 * s, 16)],
        wkv, mate, lambda j: wkv_all.at[j * 2 + 1 - c],
    )
    pages = Ring(
        links, x, xs, lambda j: kv_all.at[:, j * 2 + c], lambda j, s: kv_all.at[s, j * 2 + c],
        None, mate, lambda j: kv_all.at[:, j * 2 + 1 - c],
    )
    o_ring = Ring(
        links, x, xs, lambda j: wo_all.at[j, pl.ds(64, 64)], lambda j, s: wo_all.at[j, pl.ds(64 + 32 * s, 32)], wo,
    )
    new = Ring(
        links, x, xs, lambda j: fresh.at[c, :, j], lambda j, s: fresh.at[c, pl.ds(2 * s, 2), j],
        None, mate, lambda j: fresh.at[1 - c, :, j],
    )
    greet(list(column.values()) + xs + [ag2.zm] + planes[0].ys)

    mine = x * 2 + c
    near_pages, relayed = [], []
    for s, dz in ((0, 1), (1, 3)):
        near_pages.append(links.send(pool.at[pl.ds(2 * ((zh + dz) % 4), 2)], kv_all.at[:, mine, zh], zs[s]))
        relayed.append(links.send(pool.at[2 * ((zh + 2) % 4) + s], relay.at[s], zs[s]))
    q_ring.start()
    hidden.start()
    kv_ring.start()
    for plane in planes:
        plane.start_y()
    own_pages = local.copy(pool.at[pl.ds(2 * zh, 2)], kv_all.at[:, mine, zh])
    early = [
        local.copy(hid, hid_col.at[zh * 2 + c]),
        local.copy(wkv, wkv_all.at[mine]),
        local.copy(wq, wq_all.at[x]),
    ]
    own_wo = local.copy(wo, wo_all.at[x, pl.ds(64, 64)])
    own_planes = [local.copy(plane.own, plane.blk(0, 0)) for plane in planes]
    far_pages = []
    for s, dz in ((0, 3), (1, 1)):
        links.recv(relayed[s], relay.at[s])
        far_pages.append(links.send(relay.at[s], kv_all.at[s, mine, (zh + dz) % 4], zs[s]))
    for s, dz in ((0, 3), (1, 1)):
        links.recv(near_pages[s], kv_all.at[:, mine, (zh + dz) % 4])
    q_ring.near()
    own_pages.wait()
    for s in (0, 1):
        links.recv(far_pages[s], kv_all.at[s, mine, (zh + 2) % 4])
    pages.start()
    kv_ring.near()
    hidden.near()
    for plane in planes:
        plane.start_z()
    for plane in planes:
        plane.y_near(0)
    for k in range(4):
        wo_all[k, pl.ds(0, 64)] = jnp.zeros((64, width), BF)
    q_ring.far()
    kv_ring.far()
    hidden.far()
    pages.near()
    o_ring.start()
    for copy in early:
        copy.wait()
    hidden.ready()
    kv_ring.ready()

    def norm(i, carry):
        nrm[pl.ds(pl.multiple_of(i * 32, 32), 32), :] = root_norm(hid_col[i], gain_one[...])
        return carry

    lax.fori_loop(0, 8, norm, 0)
    lane = lax.broadcasted_iota(jnp.int32, (256, 2 * HD), 1)
    first_half = lane % HD < HD // 2

    def rotate(pairs):
        swapped = jnp.where(first_half, pltpu.roll(pairs, 96, 1), pltpu.roll(pairs, 32, 1))
        return pairs * cosine[...] + swapped * sine[...]

    keyvals = transposed_product(nrm[...], wkv_all[...].reshape(256, width)).astype(BF)
    for k in (0, 1):
        pairs = keyvals[:, k * 128 : (k + 1) * 128].astype(F32)
        fresh[k, :, x] = jnp.where(lane < HD, rotate(pairs), pairs).astype(BF).reshape(4, 64, 128)
    new.start(False)
    kv_h = []
    for (dz, dc), to in column.items():
        src = fresh.at[c, (zh + dz) % 4, x, pl.ds(32 * ((c + dc) % 2), 32)]
        kv_h.append((links.send(src, kv_out.at[2 * zh + c], to), kv_out.at[2 * ((zh + 4 - dz) % 4) + (c + dc) % 2]))
    own_kv = local.copy(fresh.at[c, zh, x, pl.ds(32 * c, 32)], kv_out.at[2 * zh + c])
    queries = transposed_product(nrm[...], wq_all[...].reshape(256, width))
    for k in (0, 1):
        turned = rotate(queries[:, k * 128 : (k + 1) * 128]) * ATTENTION_SCALE
        for i in (0, 1):
            head = turned if i == 0 else pltpu.roll(turned, 64, 1)
            q_all[k, :, i] = jnp.where(lane < HD, head, 0.0).astype(BF).reshape(4, 64, 128)
    new.near()
    pages.far()
    new.far()
    new.ready()
    pages.ready()

    prefix = 4096
    per_block = KC // 512

    def lanes_max(running, scores):
        for k in range(scores.shape[1] // 128):
            running = jnp.maximum(running, scores[:, k * 128 : (k + 1) * 128])
        return running

    def attend(k, p):
        q = q_all[k, 2 * p : 2 * p + 2].reshape(QT, 2 * HD)

        def keys_at(i):
            return kv_all[k, pl.ds(i * per_block, per_block)].reshape(KC, 2 * HD)

        def score_prefix(i, running):
            at = pl.ds(pl.multiple_of(i * KC, KC), KC)
            scores = transposed_product(q, keys_at(i)) + bias[:, at]
            s_ref[:, at] = scores
            return lanes_max(running, scores)

        running = lax.fori_loop(0, prefix // KC, score_prefix, jnp.full((QT, 128), MASKED, F32), unroll=2)
        row = lax.broadcasted_iota(jnp.int32, (QT, 256), 0)
        token = (2 * p + row // 128) * 256 + x * 64 + row % 64
        col = lax.broadcasted_iota(jnp.int32, (QT, 256), 1)
        for i in range(2 * p + 2):
            scores = transposed_product(q, fresh[k, i].reshape(256, 2 * HD))
            scores = jnp.where(col + i * 256 <= token, scores, MASKED)
            s_ref[:, prefix + i * 256 : prefix + (i + 1) * 256] = scores
            running = lanes_max(running, scores)
        top = jnp.broadcast_to(jnp.max(running, axis=1, keepdims=True), (QT, 128))

        def weigh(at, keys, carried):
            total, summed = carried
            scores = s_ref[:, at]
            pieces = []
            for n in range(scores.shape[1] // 128):
                weights = jnp.exp(scores[:, n * 128 : (n + 1) * 128] - top)
                total = total + weights
                pieces.append(weights.astype(BF))
            weights = jnp.concatenate(pieces, axis=1)
            return total, summed + jnp.dot(weights, keys, preferred_element_type=F32)

        def weigh_prefix(i, carried):
            return weigh(pl.ds(pl.multiple_of(i * KC, KC), KC), keys_at(i), carried)

        carried = (jnp.zeros((QT, 128), F32), jnp.zeros((QT, 2 * HD), F32))
        carried = lax.fori_loop(0, prefix // KC, weigh_prefix, carried, unroll=2)
        for i in range(2 * p + 2):
            carried = weigh(pl.ds(prefix + i * 256, 256), fresh[k, i].reshape(256, 2 * HD), carried)
        total, summed = carried
        mixed = (summed / jnp.sum(total, axis=1, keepdims=True)).astype(BF).reshape(2, 2, 64, 128)
        for z in (0, 1):
            for i in (0, 1):
                att[2 * k + i, (2 * p + z) * 64 : (2 * p + z + 1) * 64] = mixed[z, i]

    steps = weight_steps(planes)
    for n, (k, p) in enumerate(((0, 0), (1, 0), (0, 1), (1, 1))):
        attend(k, p)
        if n == 0:
            o_ring.near()
        if n == 2:
            o_ring.far()
        for step in steps[n]:
            step()
    own_wo.wait()

    one = RowScatter(links, part1, rc1, q1, xh1, xf1, True)

    def out_columns(n, carry):
        at = pl.ds(pl.multiple_of(n * 512, 512), 512)
        term = None
        for k in (0, 2):
            heads = jnp.concatenate([att[k], att[k + 1]], axis=1)
            product = jnp.dot(heads, wo_all[pl.ds(k, 2), :, at].reshape(256, 512), preferred_element_type=F32)
            term = product if term is None else term + product
        part1[:, :, at] = term.astype(BF).reshape(8, 32, 512)
        return carry

    lax.fori_loop(0, width // 512, out_columns, 0)
    one.cores()
    one.first()
    one.second()
    residual[...] = one.total() + hid[...].astype(F32)
    n2[...] = root_norm(residual[...], gain_two[...])
    ag2.start()
    own_rows = local.copy(n2, rows.at[0, x * 2 + c])
    for step in steps[4]:
        step()
    ag2.second()
    ag2.near(0)
    ag2.near(1)
    ag2.far(0)
    ag2.far(1)
    ag2.ready(0)
    own_rows.wait()
    for step in steps[5]:
        step()
    for copy in own_planes:
        copy.wait()

    twos = [RowScatter(links, part2.at[i], rc2.at[i], q2.at[i], xh2.at[i], xf2.at[i]) for i in (0, 1)]

    def feed(row):
        def units(h, carry):
            tokens = rows[row].reshape(256, width)
            some = pl.ds(h * 8, 8)
            gated = transposed_product(tokens, wall[0, some].reshape(256, width))
            raised = transposed_product(tokens, wall[1, some].reshape(256, width))
            act[h] = (gated / (1.0 + jnp.exp(-gated)) * raised).astype(BF)
            return carry

        lax.fori_loop(0, 2, units, 0)

        def columns(n, carry):
            at = pl.ds(pl.multiple_of(n * 512, 512), 512)
            activated = jnp.concatenate([act[0], act[1]], axis=1)
            term = jnp.dot(activated, wall[2, :, :, at].reshape(512, 512), preferred_element_type=F32)
            part2[row, :, :, at] = term.astype(BF).reshape(8, 32, 512)
            return carry

        lax.fori_loop(0, width // 512, columns, 0)

    feed(0)
    twos[0].cores()
    ag2.ready(1)
    feed(1)
    twos[1].cores()
    twos[1].first()
    twos[0].first()
    twos[1].second()
    twos[0].second()
    zsend[...] = twos[1].total().astype(BF)
    last = links.send(zsend, zrecv, ag2.zm)
    value = residual[...] + twos[0].total()
    links.recv(last, zrecv)
    out[...] = (value + zrecv[...].astype(F32)).astype(BF)
    for handle, region in kv_h:
        links.recv(handle, region)
    own_kv.wait()
    links.drain()


def weight_steps(planes):
    gate, up, down = planes

    def near(plane):
        return [lambda: plane.y_near(3), lambda: plane.y_near(1)]

    def last(plane):
        return [plane.y_near_far] + [lambda dz=dz: plane.y_far(dz) for dz in (0, 3, 1, 2)]

    return [
        [gate.z_near],
        [up.z_near],
        [down.z_near] + near(gate),
        [],
        [gate.z_far] + near(up) + [up.z_far] + near(down) + [down.z_far],
        last(gate) + last(up) + last(down),
    ]


def vmem(count):
    return [pl.BlockSpec(memory_space=pltpu.VMEM)] * count


def on_device(
    hidden_in, attention_gain, query_weight, keyval_weight, out_weight, feedforward_gain,
    gate_weight, up_weight, down_weight, prefix_pool, page_table, prefix_length,
):
    width = hidden_in.shape[2]
    tokens = 1024
    length = prefix_length[0]
    slots = prefix_pool.shape[1] * PAGE
    pool = prefix_pool[0].transpose(2, 0, 1, 3).reshape(KVH, slots, 2 * HD)

    logical = jnp.sum(
        jnp.where(
            page_table[0][None, :] == jnp.arange(256, dtype=jnp.int32)[:, None],
            jnp.arange(256, dtype=jnp.int32)[None, :],
            0,
        ),
        axis=1,
    )
    slot = logical[:, None] * PAGE + jnp.arange(PAGE, dtype=jnp.int32)[None, :]
    bias = jnp.where(slot < length, 0.0, MASKED).astype(F32)
    bias = bias.reshape(4, 8, slots).transpose(1, 0, 2).reshape(1, 32 * slots)

    index = jnp.arange(256, dtype=jnp.int32)
    column = (lax.axis_index("dev") // 2) % 4
    positions = (length + index // 64 * 256 + column * 64 + index % 64).astype(F32)
    half = HD // 2
    frequency = ROPE_BASE ** (-jnp.arange(half, dtype=F32) / half)
    angles = positions[:, None] * frequency[None, :]
    cosine, sine = jnp.cos(angles), jnp.sin(angles)
    cosine = jnp.concatenate([cosine] * 4, axis=1)
    sine = jnp.concatenate([-sine, sine, -sine, sine], axis=1)

    buffers = [
        ((8, 32, width), BF),
        ((2, slots, 2 * HD), BF),
        ((2, 8, 4, slots, 2 * HD), BF),
        ((4, 2, 32, width), BF),
        ((8, 32, width), BF),
        ((4, 128, width), BF),
        ((3, 16, 32, width), BF),
        ((256, width), BF),
        ((2, 4, 2, 64, 2 * HD), BF),
        ((2, 4, 4, 64, 2 * HD), BF),
        ((QT, 32 * slots + tokens), F32),
        ((4, 256, 2 * HD), BF),
        ((8, 32, width), BF),
        ((4, 32, width), BF),
        ((3, 32, width), BF),
        ((2, 16, width), BF),
        ((2, 32, width), BF),
        ((32, width), F32),
        ((32, width), BF),
        ((2, 8, 32, width), BF),
        ((2, 256, 256), BF),
        ((2, 8, 32, width), BF),
        ((2, 4, 32, width), BF),
        ((2, 3, 32, width), BF),
        ((2, 2, 16, width), BF),
        ((2, 2, 32, width), BF),
        ((32, width), BF),
        ((32, width), BF),
    ]
    hidden_out, kv_out = pl.pallas_call(
        layer_kernel,
        out_shape=[jax.ShapeDtypeStruct((32, width), BF), jax.ShapeDtypeStruct((8, 32, 2 * HD), BF)],
        in_specs=vmem(13),
        out_specs=vmem(2),
        scratch_shapes=[pltpu.VMEM(*b) for b in buffers] + [
            pltpu.SemaphoreType.DMA((COPIES,)),
            pltpu.SemaphoreType.DMA((COPIES,)),
            pltpu.SemaphoreType.DMA((16,)),
        ],
        compiler_params=pltpu.CompilerParams(collective_id=0, has_side_effects=True, vmem_limit_bytes=60 << 20),
        name="layer",
    )(
        hidden_in[0], pool, query_weight.reshape(2, 32, width), keyval_weight, out_weight,
        gate_weight, up_weight, down_weight,
        attention_gain.reshape(1, width), feedforward_gain.reshape(1, width), cosine, sine, bias,
    )
    return hidden_out[None], kv_out.transpose(1, 0, 2)[None]


COPIES = 230


def solution(mesh):
    placed = (
        P("req", "dev", None),
        P(),
        P("dev", None),
        P("dev", None),
        P("dev", None),
        P(),
        P(("req", "dev"), None),
        P(("req", "dev"), None),
        P(("req", "dev"), None),
        P("req", "dev", None, None, None),
        P("req", None),
        P("req"),
    )
    return jax.shard_map(
        on_device,
        mesh=mesh,
        in_specs=placed,
        out_specs=(P("req", "dev", None), P("req", "dev", None, None)),
        check_vma=False,
    )
```

```python
import jax
import jax.numpy as jnp
from jax import lax
from jax.experimental import pallas as pl
from jax.experimental.pallas import tpu as pltpu
from jax.sharding import PartitionSpec as P

MESH = pl.DeviceIdType.MESH
HQ = 32
KVH = 8
HD = 64
PAGE = 16
ROPE_BASE = 10000000.0
EPS = 1e-05
ATTENTION_SCALE = 0.015625
MASKED = -1e30
BF = jnp.bfloat16
F32 = jnp.float32
QT = 256
KC = 1024


def root_norm(activations, norm_gain):
    widened = activations.astype(F32)
    inverse_rms = lax.rsqrt(jnp.mean(widened * widened, axis=-1, keepdims=True) + EPS)
    return (widened * inverse_rms * norm_gain).astype(BF)


def transposed_product(left, right):
    return lax.dot_general(left, right, (((1,), (1,)), ((), ())), preferred_element_type=F32)


def dev_of(zh, x, c):
    return (zh * 4 + x) * 2 + c


def place():
    d = lax.axis_index("dev")
    return d // 8, (d // 2) % 4, d % 2


class Links:
    def __init__(self, send_sems, recv_sems):
        self.send_sems, self.recv_sems = send_sems, recv_sems
        self.copies = []

    def make(self, i, src, dst, to):
        return pltpu.make_async_remote_copy(
            src_ref=src,
            dst_ref=dst,
            send_sem=self.send_sems.at[i],
            recv_sem=self.recv_sems.at[i],
            device_id=to,
            device_id_type=MESH,
        )

    def send(self, src, dst, to):
        i = len(self.copies)
        copy = self.make(i, src, dst, to)
        copy.start()
        self.copies.append(copy)
        return i, to

    def recv(self, handle, region):
        i, to = handle
        self.make(i, region, region, to).wait_recv()

    def drain(self):
        for copy in self.copies:
            copy.wait_send()


class Locals:
    def __init__(self, sems):
        self.sems, self.copies = sems, []

    def copy(self, src, dst):
        copy = pltpu.make_async_copy(src, dst, self.sems.at[len(self.copies)])
        copy.start()
        self.copies.append(copy)
        return copy


def greet(partners):
    barrier = pltpu.get_barrier_semaphore()
    for partner in partners:
        pl.semaphore_signal(barrier, inc=1, device_id=partner, device_id_type=MESH)
    pl.semaphore_wait(barrier, len(partners))


def halves(ref, i):
    rows = ref.shape[1] // 2
    return [ref.at[i, pl.ds(0, rows)], ref.at[i, pl.ds(rows, rows)]]


class Ring:
    def __init__(self, links, i, tos, blk, half, own=None, mate=None, there=None):
        self.l, self.i, self.tos, self.blk, self.half = links, i, tos, blk, half
        self.own = blk(i) if own is None else own
        self.mate, self.there = mate, there
        self.waits = []

    def core(self, j, src=None):
        if self.mate is not None:
            here = self.blk(j)
            self.waits.append((self.l.send(here if src is None else src, here, self.mate), self.there(j)))

    def start(self, core=True):
        mine = self.blk(self.i)
        self.h = [self.l.send(self.own, mine, to) for to in self.tos]
        if core:
            self.core(self.i, self.own)

    def near(self):
        self.f = []
        for s, off in ((0, 3), (1, 1)):
            j = (self.i + off) % 4
            self.l.recv(self.h[s], self.blk(j))
            piece = self.half(j, s)
            self.f.append(self.l.send(piece, piece, self.tos[s]))
            self.core(j)

    def far(self):
        j = (self.i + 2) % 4
        for s in (0, 1):
            self.l.recv(self.f[s], self.half(j, s))
        self.core(j)

    def ready(self):
        for handle, region in self.waits:
            self.l.recv(handle, region)


class PlaneGather:
    def __init__(self, links, out, x_first):
        self.l, self.out, self.x_first = links, out, x_first
        zh, x, c = place()
        r = lax.axis_index("req")
        self.x, self.y, self.rows = x, r % 4, pl.ds(0 if x_first else 16, 16)
        xs = [{"dev": dev_of(zh, (x + s) % 4, c)} for s in (1, 3)]
        ys = [{"req": r // 4 * 4 + (self.y + s) % 4} for s in (1, 3)]
        self.one, self.two = (xs, ys) if x_first else (ys, xs)
        self.h2, self.f2 = {}, {}

    def id(self, a, b):
        dx, dy = (a, b) if self.x_first else (b, a)
        return (self.x + dx) % 4 * 4 + (self.y + dy) % 4

    def blk(self, a, b):
        return self.out.at[:, self.id(a, b), self.rows]

    def half(self, a, b, s):
        wide = self.out.shape[3] // 2
        return self.out.at[:, self.id(a, b), self.rows, pl.ds(s * wide, wide)]

    def both(self, ref, tos):
        return [self.l.send(ref, ref, to) for to in tos]

    def start_one(self):
        self.h1 = self.both(self.blk(0, 0), self.one)

    def start_two(self):
        self.h2[0] = self.both(self.blk(0, 0), self.two)

    def near_one(self):
        self.f1 = []
        for s, a in ((0, 3), (1, 1)):
            self.l.recv(self.h1[s], self.blk(a, 0))
            piece = self.half(a, 0, s)
            self.f1.append(self.l.send(piece, piece, self.one[s]))

    def spread(self):
        for a in (3, 1):
            self.h2[a] = self.both(self.blk(a, 0), self.two)

    def far_one(self):
        self.g2 = []
        for s in (0, 1):
            piece = self.half(2, 0, s)
            self.l.recv(self.f1[s], piece)
            self.g2.append(self.both(piece, self.two))

    def near_two(self, a):
        self.f2[a] = []
        for s, b in ((0, 3), (1, 1)):
            self.l.recv(self.h2[a][s], self.blk(a, b))
            piece = self.half(a, b, s)
            self.f2[a].append(self.l.send(piece, piece, self.two[s]))

    def near_two_far(self):
        self.f2[2] = []
        for s, b in ((0, 3), (1, 1)):
            piece = self.half(2, b, s)
            self.l.recv(self.g2[s][s], piece)
            self.f2[2].append(self.l.send(piece, piece, self.two[s]))
        for s, b in ((0, 3), (1, 1)):
            self.l.recv(self.g2[1 - s][s], self.half(2, b, 1 - s))

    def far_two(self):
        for a in (0, 3, 1, 2):
            for s in (0, 1):
                self.l.recv(self.f2[a][s], self.half(a, 2, s))


class RowScatter:
    def __init__(self, links, part, rc, q, xh, xf, along_z=False):
        self.l = links
        self.part, self.rc, self.q, self.xh, self.xf = part, rc, q, xh, xf
        zh, x, c = place()
        self.x, self.c = zh if along_z else x, c
        if along_z:
            self.xs = [{"dev": dev_of((zh + s) % 4, x, c)} for s in (1, 3)]
        else:
            self.xs = [{"dev": dev_of(zh, (x + s) % 4, c)} for s in (1, 3)]
        self.mate = {"dev": dev_of(zh, x, 1 - c)}
        self.dx = (2, 1, 3, 0)

    def block(self, k, other=False):
        return ((self.x + self.dx[k]) % 4) * 2 + (1 - self.c if other else self.c)

    def cores(self):
        self.ch = [self.l.send(self.part.at[self.block(k, True)], self.rc.at[k], self.mate) for k in range(4)]

    def pair_sum(self, k):
        self.l.recv(self.ch[k], self.rc.at[k])
        return self.part[self.block(k)].astype(F32) + self.rc[k].astype(F32)

    def first(self):
        self.q[0] = self.pair_sum(0).astype(BF)
        pieces = halves(self.q, 0)
        self.x1 = [self.l.send(pieces[s], self.xh.at[s], self.xs[s]) for s in (0, 1)]

    def second(self):
        self.x2 = []
        for s in (0, 1):
            value = self.pair_sum(1 + s)
            self.l.recv(self.x1[s], self.xh.at[s])
            arrived = self.xh[s].astype(F32)
            top = value[:16] + arrived if s == 0 else value[:16]
            low = value[16:] + arrived if s == 1 else value[16:]
            self.q[1 + s, pl.ds(0, 16)] = top.astype(BF)
            self.q[1 + s, pl.ds(16, 16)] = low.astype(BF)
            self.x2.append(self.l.send(self.q.at[1 + s], self.xf.at[s], self.xs[s]))

    def total(self):
        value = self.pair_sum(3)
        for s in (0, 1):
            self.l.recv(self.x2[s], self.xf.at[s])
            value = value + self.xf[s].astype(F32)
        return value


def z_neighbours():
    zh, x, c = place()
    r = lax.axis_index("req")
    z = zh * 2 + r // 4
    tos = []
    for step in (1, 7):
        other = (z + step) % 8
        tos.append({"req": other % 2 * 4 + r % 4, "dev": dev_of(other // 2, x, c)})
    return tos


class ColumnGather:
    def __init__(self, links, out):
        self.l, self.out = links, out
        self.tos = z_neighbours()
        zh, x, c = place()
        self.mate = {"dev": dev_of(zh, x, 1 - c)}
        self.h, self.waits = {}, {}

    def piece(self, k, p):
        return self.out.at[k % 8, 0, pl.ds(16 * p, 16)]

    def core(self, k):
        self.waits[k % 8] = self.l.send(self.out.at[k % 8, 0], self.out.at[k % 8, 1], self.mate)

    def pass_on(self, s, k, p):
        sign = -1 if s == 0 else 1
        self.h[s, k + 1, p] = self.l.send(self.piece(sign * k, p), self.piece(sign * (k + 1), p), self.tos[s])

    def start(self):
        for p in (0, 1):
            for s in (0, 1):
                self.pass_on(s, 0, p if s == 0 else 1 - p)
        self.core(0)

    def hop(self, k):
        for p in (0, 1):
            for s in (0, 1):
                q = p if s == 0 else 1 - p
                self.l.recv(self.h[s, k, q], self.piece(-k if s == 0 else k, q))
                if k < 3 or q == s:
                    self.pass_on(s, k, q)
        self.core(k)
        self.core(-k)

    def last(self):
        for s in (0, 1):
            self.l.recv(self.h[s, 4, s], self.piece(4, s))
        self.core(4)

    def ready(self, ks):
        for k in ks:
            self.l.recv(self.waits[k % 8], self.out.at[k % 8, 1])


class ColumnScatter:
    def __init__(self, links, part, rc, q, arrived):
        self.l, self.part, self.rc, self.q, self.arrived = links, part, rc, q, arrived
        self.tos = z_neighbours()
        zh, x, c = place()
        self.mate = {"dev": dev_of(zh, x, 1 - c)}
        self.ch, self.h = {}, {}

    def cores(self, ks):
        for k in ks:
            self.ch[k] = self.l.send(self.part.at[k, 1], self.rc.at[k], self.mate)

    def arrive(self, ks):
        for k in ks:
            self.l.recv(self.ch[k], self.rc.at[k])

    def own(self, k, p):
        at = pl.ds(16 * p, 16)
        return self.part[k % 8, 0, at].astype(F32) + self.rc[k % 8, at].astype(F32)

    def hop(self, k):
        for p in (0, 1):
            for s in (0, 1):
                q = p if s == 0 else 1 - p
                if k == 4 and q != s:
                    continue
                value = self.own(k if s == 0 else -k, q)
                if (s, k + 1, q) in self.h:
                    slot = self.arrived.at[s, k + 1 - 2, q]
                    self.l.recv(self.h[s, k + 1, q], slot)
                    value = value + slot[...].astype(F32)
                self.q[s, k - 1, q] = value.astype(BF)
                self.h[s, k, q] = self.l.send(self.q.at[s, k - 1, q], self.arrived.at[s, (k - 2) % 4, q], self.tos[s])

    def total(self, p):
        value = self.own(0, p)
        for s in (0, 1):
            slot = self.arrived.at[s, 3, p]
            self.l.recv(self.h[s, 1, p], slot)
            value = value + slot[...].astype(F32)
        return value


def layer_kernel(
    hid, pool, wq, wkv, wo, gate, up, down, gain_one, gain_two, cosine, sine, bias,
    out, kv_out,
    hid_col, relay, kv_all, wq_all, wkv_all, wo_all, wall, nrm, q_all, fresh, s_ref, att,
    part1, rc1, q1, xh1, xf1, residual, rows, act, part2, rc2, q2, arrived2,
    send_sems, recv_sems, local_sems,
):
    zh, x, c = place()
    r = lax.axis_index("req")
    width = hid.shape[1]
    links, local = Links(send_sems, recv_sems), Locals(local_sems)
    zs = [{"dev": dev_of((zh + s) % 4, x, c)} for s in (1, 3)]
    xs = [{"dev": dev_of(zh, (x + s) % 4, c)} for s in (1, 3)]
    mate = {"dev": dev_of(zh, x, 1 - c)}
    y = r % 4
    ys = [{"req": r // 4 * 4 + (y + s) % 4} for s in (1, 3)]
    a_plane, b_plane = PlaneGather(links, wall, True), PlaneGather(links, wall, False)
    ag2 = ColumnGather(links, rows)
    column = {(dz, dc): {"dev": dev_of((zh + dz) % 4, x, (c + dc) % 2)} for dz in range(4) for dc in range(2)}
    del column[0, 0]

    hidden = Ring(
        links, zh, zs, lambda j: hid_col.at[j * 2 + c], lambda j, s: hid_col.at[j * 2 + c, pl.ds(16 * s, 16)],
        hid, mate, lambda j: hid_col.at[j * 2 + 1 - c],
    )
    wide = width // 4

    def quarter(k):
        return pl.ds(pl.multiple_of(k * wide, wide), wide)

    q_ring = Ring(
        links, x, xs, lambda j: wq_all.at[j, :, :, quarter(y)], lambda j, s: wq_all.at[j, s, :, quarter(y)],
        wq.at[:, :, quarter(y)],
    )
    kv_ring = Ring(
        links, x, xs, lambda j: wkv_all.at[j * 2 + c, :, quarter(y)],
        lambda j, s: wkv_all.at[j * 2 + c, pl.ds(16 * s, 16), quarter(y)], wkv.at[:, quarter(y)],
    )
    y_rings = {}
    for dx in (1, 2, 3):
        j = (x + dx) % 4
        y_rings[dx] = [
            Ring(
                links, y, ys, lambda k, j=j: wkv_all.at[j * 2 + c, :, quarter(k)],
                lambda k, s, j=j: wkv_all.at[j * 2 + c, pl.ds(16 * s, 16), quarter(k)],
            ),
            Ring(
                links, y, ys, lambda k, j=j: wq_all.at[j, :, :, quarter(k)],
                lambda k, s, j=j: wq_all.at[j, s, :, quarter(k)],
            ),
        ]
    pages = Ring(
        links, x, xs, lambda j: kv_all.at[:, j * 2 + c], lambda j, s: kv_all.at[s, j * 2 + c],
        None, mate, lambda j: kv_all.at[:, j * 2 + 1 - c],
    )
    o_ring = Ring(
        links, x, xs, lambda j: wo_all.at[j, pl.ds(64, 64)], lambda j, s: wo_all.at[j, pl.ds(64 + 32 * s, 32)], wo,
    )
    new = Ring(
        links, x, xs, lambda j: fresh.at[c, :, j], lambda j, s: fresh.at[c, pl.ds(2 * s, 2), j],
        None, mate, lambda j: fresh.at[1 - c, :, j],
    )
    greet(list(column.values()) + xs + ag2.tos + ys)

    mine = x * 2 + c
    near_pages, relayed = [], []
    for s, dz in ((0, 1), (1, 3)):
        near_pages.append(links.send(pool.at[pl.ds(2 * ((zh + dz) % 4), 2)], kv_all.at[:, mine, zh], zs[s]))
        relayed.append(links.send(pool.at[2 * ((zh + 2) % 4) + s], relay.at[s], zs[s]))
    kv_ring.start()
    q_ring.start()
    hidden.start()
    w_core = [(links.send(wkv, wkv_all.at[mine], mate), wkv_all.at[x * 2 + 1 - c])]
    own_planes = [local.copy(own, wall.at[a, x * 4 + y]) for a, own in enumerate((gate, up, down))]
    own_pages = local.copy(pool.at[pl.ds(2 * zh, 2)], kv_all.at[:, mine, zh])
    early = [
        local.copy(hid, hid_col.at[zh * 2 + c]),
        local.copy(wkv, wkv_all.at[mine]),
        local.copy(wq, wq_all.at[x]),
    ]
    own_wo = local.copy(wo, wo_all.at[x, pl.ds(64, 64)])
    kv_ring.near()
    q_ring.near()
    for dx in (1, 3):
        for ring in y_rings[dx]:
            ring.start()
    for copy in own_planes:
        copy.wait()
    a_plane.start_one()
    kv_ring.far()
    q_ring.far()
    for ring in y_rings[2]:
        ring.start()
    b_plane.start_one()
    a_plane.start_two()
    far_pages = []
    for s, dz in ((0, 3), (1, 1)):
        links.recv(relayed[s], relay.at[s])
        far_pages.append(links.send(relay.at[s], kv_all.at[s, mine, (zh + dz) % 4], zs[s]))
    for dx in (1, 3):
        for ring in y_rings[dx]:
            ring.near()
    a_plane.near_one()
    for s, dz in ((0, 3), (1, 1)):
        links.recv(near_pages[s], kv_all.at[:, mine, (zh + dz) % 4])
    own_pages.wait()
    for s in (0, 1):
        links.recv(far_pages[s], kv_all.at[s, mine, (zh + 2) % 4])
    pages.start()
    for ring in y_rings[2]:
        ring.near()
    hidden.near()
    for k in range(4):
        wo_all[k, pl.ds(0, 64)] = jnp.zeros((64, width), BF)
    for copy in early:
        copy.wait()
    for dx in (1, 3, 2):
        for ring in y_rings[dx]:
            ring.far()
        block = (x + dx) % 4 * 2
        w_core.append((links.send(wkv_all.at[block + c], wkv_all.at[block + c], mate), wkv_all.at[block + 1 - c]))
    a_plane.spread()
    hidden.far()
    pages.near()
    hidden.ready()
    for handle, region in w_core:
        links.recv(handle, region)

    def norm(i, carry):
        nrm[pl.ds(pl.multiple_of(i * 32, 32), 32), :] = root_norm(hid_col[i], gain_one[...])
        return carry

    lax.fori_loop(0, 8, norm, 0)
    lane = lax.broadcasted_iota(jnp.int32, (256, 2 * HD), 1)
    first_half = lane % HD < HD // 2

    def rotate(pairs):
        swapped = jnp.where(first_half, pltpu.roll(pairs, 96, 1), pltpu.roll(pairs, 32, 1))
        return pairs * cosine[...] + swapped * sine[...]

    keyvals = transposed_product(nrm[...], wkv_all[...].reshape(256, width)).astype(BF)
    for k in (0, 1):
        pairs = keyvals[:, k * 128 : (k + 1) * 128].astype(F32)
        fresh[k, :, x] = jnp.where(lane < HD, rotate(pairs), pairs).astype(BF).reshape(4, 64, 128)
    new.start(False)
    kv_h = []
    for (dz, dc), to in column.items():
        src = fresh.at[c, (zh + dz) % 4, x, pl.ds(32 * ((c + dc) % 2), 32)]
        kv_h.append((links.send(src, kv_out.at[2 * zh + c], to), kv_out.at[2 * ((zh + 4 - dz) % 4) + (c + dc) % 2]))
    own_kv = local.copy(fresh.at[c, zh, x, pl.ds(32 * c, 32)], kv_out.at[2 * zh + c])
    queries = transposed_product(nrm[...], wq_all[...].reshape(256, width))
    for k in (0, 1):
        turned = rotate(queries[:, k * 128 : (k + 1) * 128]) * ATTENTION_SCALE
        for i in (0, 1):
            head = turned if i == 0 else pltpu.roll(turned, 64, 1)
            q_all[k, :, i] = jnp.where(lane < HD, head, 0.0).astype(BF).reshape(4, 64, 128)
    new.near()
    o_ring.start()
    pages.far()
    new.far()
    a_plane.far_one()
    b_plane.near_one()
    new.ready()
    pages.ready()

    prefix = 4096
    per_block = KC // 512

    def lanes_max(running, scores):
        for k in range(scores.shape[1] // 128):
            running = jnp.maximum(running, scores[:, k * 128 : (k + 1) * 128])
        return running

    def attend(k, p):
        q = q_all[k, 2 * p : 2 * p + 2].reshape(QT, 2 * HD)

        def keys_at(i):
            return kv_all[k, pl.ds(i * per_block, per_block)].reshape(KC, 2 * HD)

        def score_prefix(i, running):
            at = pl.ds(pl.multiple_of(i * KC, KC), KC)
            scores = transposed_product(q, keys_at(i)) + bias[:, at]
            s_ref[:, at] = scores
            return lanes_max(running, scores)

        running = lax.fori_loop(0, prefix // KC, score_prefix, jnp.full((QT, 128), MASKED, F32), unroll=2)
        row = lax.broadcasted_iota(jnp.int32, (QT, 256), 0)
        token = (2 * p + row // 128) * 256 + x * 64 + row % 64
        col = lax.broadcasted_iota(jnp.int32, (QT, 256), 1)
        for i in range(2 * p + 2):
            scores = transposed_product(q, fresh[k, i].reshape(256, 2 * HD))
            scores = jnp.where(col + i * 256 <= token, scores, MASKED)
            s_ref[:, prefix + i * 256 : prefix + (i + 1) * 256] = scores
            running = lanes_max(running, scores)
        top = jnp.broadcast_to(jnp.max(running, axis=1, keepdims=True), (QT, 128))

        def weigh(at, keys, carried):
            total, summed = carried
            scores = s_ref[:, at]
            pieces = []
            for n in range(scores.shape[1] // 128):
                weights = jnp.exp(scores[:, n * 128 : (n + 1) * 128] - top)
                total = total + weights
                pieces.append(weights.astype(BF))
            weights = jnp.concatenate(pieces, axis=1)
            return total, summed + jnp.dot(weights, keys, preferred_element_type=F32)

        def weigh_prefix(i, carried):
            return weigh(pl.ds(pl.multiple_of(i * KC, KC), KC), keys_at(i), carried)

        carried = (jnp.zeros((QT, 128), F32), jnp.zeros((QT, 2 * HD), F32))
        carried = lax.fori_loop(0, prefix // KC, weigh_prefix, carried, unroll=2)
        for i in range(2 * p + 2):
            carried = weigh(pl.ds(prefix + i * 256, 256), fresh[k, i].reshape(256, 2 * HD), carried)
        total, summed = carried
        mixed = (summed / jnp.sum(total, axis=1, keepdims=True)).astype(BF).reshape(2, 2, 64, 128)
        for z in (0, 1):
            for i in (0, 1):
                att[2 * k + i, (2 * p + z) * 64 : (2 * p + z + 1) * 64] = mixed[z, i]

    attend(0, 0)
    o_ring.near()
    b_plane.start_two()
    b_plane.spread()
    a_plane.near_two(0)
    attend(1, 0)
    b_plane.far_one()
    a_plane.near_two(3)
    attend(0, 1)
    o_ring.far()
    a_plane.near_two(1)
    attend(1, 1)
    own_wo.wait()

    one = RowScatter(links, part1, rc1, q1, xh1, xf1, True)

    def out_columns(n, carry):
        at = pl.ds(pl.multiple_of(n * 512, 512), 512)
        term = None
        for k in (0, 2):
            heads = jnp.concatenate([att[k], att[k + 1]], axis=1)
            product = jnp.dot(heads, wo_all[pl.ds(k, 2), :, at].reshape(256, 512), preferred_element_type=F32)
            term = product if term is None else term + product
        part1[:, :, at] = term.astype(BF).reshape(8, 32, 512)
        return carry

    lax.fori_loop(0, width // 512, out_columns, 0)
    one.cores()
    one.first()
    one.second()
    residual[...] = one.total() + hid[...].astype(F32)
    rows[0, 0] = root_norm(residual[...], gain_two[...])
    ag2.start()
    a_plane.near_two_far()
    b_plane.near_two(0)
    ag2.hop(1)
    ag2.hop(2)
    ag2.hop(3)
    b_plane.near_two(3)
    b_plane.near_two(1)
    b_plane.near_two_far()
    a_plane.far_two()
    ag2.ready((0, 1, 7, 2))
    b_plane.far_two()

    two = ColumnScatter(links, part2, rc2, q2, arrived2)

    def feed(ks):
        tokens = jnp.concatenate([rows[k].reshape(64, width) for k in ks], axis=0)
        nrm[...] = tokens

        def units(h, carry):
            some = pl.ds(h * 8, 8)
            gated = transposed_product(nrm[...], wall[0, some].reshape(256, width))
            raised = transposed_product(nrm[...], wall[1, some].reshape(256, width))
            act[h] = (gated / (1.0 + jnp.exp(-gated)) * raised).astype(BF)
            return carry

        lax.fori_loop(0, 2, units, 0)

        def columns(n, carry):
            at = pl.ds(pl.multiple_of(n * 512, 512), 512)
            activated = jnp.concatenate([act[0], act[1]], axis=1)
            term = jnp.dot(activated, wall[2, :, :, at].reshape(512, 512), preferred_element_type=F32)
            term = term.astype(BF).reshape(4, 2, 32, 512)
            for i, k in enumerate(ks):
                part2[k, :, :, at] = term[i]
            return carry

        lax.fori_loop(0, width // 512, columns, 0)

    feed((7, 0, 1, 2))
    two.cores((7, 0, 1, 2))
    ag2.last()
    ag2.ready((3, 5, 6, 4))
    feed((3, 4, 5, 6))
    two.cores((4, 3, 5, 6))
    two.arrive((7, 0, 1, 2, 4, 3, 5, 6))
    for k in (4, 3, 2, 1):
        two.hop(k)
    for p in (0, 1):
        at = pl.ds(16 * p, 16)
        out[at, :] = (residual[at, :] + two.total(p)).astype(BF)
    for handle, region in kv_h:
        links.recv(handle, region)
    own_kv.wait()
    links.drain()


def vmem(count):
    return [pl.BlockSpec(memory_space=pltpu.VMEM)] * count


def on_device(
    hidden_in, attention_gain, query_weight, keyval_weight, out_weight, feedforward_gain,
    gate_weight, up_weight, down_weight, prefix_pool, page_table, prefix_length,
):
    width = hidden_in.shape[2]
    tokens = 1024
    length = prefix_length[0]
    slots = prefix_pool.shape[1] * PAGE
    pool = prefix_pool[0].transpose(2, 0, 1, 3).reshape(KVH, slots, 2 * HD)

    logical = jnp.sum(
        jnp.where(
            page_table[0][None, :] == jnp.arange(256, dtype=jnp.int32)[:, None],
            jnp.arange(256, dtype=jnp.int32)[None, :],
            0,
        ),
        axis=1,
    )
    slot = logical[:, None] * PAGE + jnp.arange(PAGE, dtype=jnp.int32)[None, :]
    bias = jnp.where(slot < length, 0.0, MASKED).astype(F32)
    bias = bias.reshape(4, 8, slots).transpose(1, 0, 2).reshape(1, 32 * slots)

    index = jnp.arange(256, dtype=jnp.int32)
    column = (lax.axis_index("dev") // 2) % 4
    positions = (length + index // 64 * 256 + column * 64 + index % 64).astype(F32)
    half = HD // 2
    frequency = ROPE_BASE ** (-jnp.arange(half, dtype=F32) / half)
    angles = positions[:, None] * frequency[None, :]
    cosine, sine = jnp.cos(angles), jnp.sin(angles)
    cosine = jnp.concatenate([cosine] * 4, axis=1)
    sine = jnp.concatenate([-sine, sine, -sine, sine], axis=1)

    buffers = [
        ((8, 32, width), BF),
        ((2, slots, 2 * HD), BF),
        ((2, 8, 4, slots, 2 * HD), BF),
        ((4, 2, 32, width), BF),
        ((8, 32, width), BF),
        ((4, 128, width), BF),
        ((3, 16, 32, width), BF),
        ((256, width), BF),
        ((2, 4, 2, 64, 2 * HD), BF),
        ((2, 4, 4, 64, 2 * HD), BF),
        ((QT, 32 * slots + tokens), F32),
        ((4, 256, 2 * HD), BF),
        ((8, 32, width), BF),
        ((4, 32, width), BF),
        ((3, 32, width), BF),
        ((2, 16, width), BF),
        ((2, 32, width), BF),
        ((32, width), F32),
        ((8, 2, 32, width), BF),
        ((2, 256, 256), BF),
        ((8, 2, 32, width), BF),
        ((8, 32, width), BF),
        ((2, 4, 2, 16, width), BF),
        ((2, 4, 2, 16, width), BF),
    ]
    hidden_out, kv_out = pl.pallas_call(
        layer_kernel,
        out_shape=[jax.ShapeDtypeStruct((32, width), BF), jax.ShapeDtypeStruct((8, 32, 2 * HD), BF)],
        in_specs=vmem(13),
        out_specs=vmem(2),
        scratch_shapes=[pltpu.VMEM(*b) for b in buffers] + [
            pltpu.SemaphoreType.DMA((COPIES,)),
            pltpu.SemaphoreType.DMA((COPIES,)),
            pltpu.SemaphoreType.DMA((16,)),
        ],
        compiler_params=pltpu.CompilerParams(collective_id=0, has_side_effects=True, vmem_limit_bytes=60 << 20),
        name="layer",
    )(
        hidden_in[0], pool, query_weight.reshape(2, 32, width), keyval_weight, out_weight,
        gate_weight, up_weight, down_weight,
        attention_gain.reshape(1, width), feedforward_gain.reshape(1, width), cosine, sine, bias,
    )
    return hidden_out[None], kv_out.transpose(1, 0, 2)[None]


COPIES = 230


def solution(mesh):
    placed = (
        P("req", "dev", None),
        P(),
        P("dev", None),
        P("dev", None),
        P("dev", None),
        P(),
        P(("req", "dev"), None),
        P(("req", "dev"), None),
        P(("req", "dev"), None),
        P("req", "dev", None, None, None),
        P("req", None),
        P("req"),
    )
    return jax.shard_map(
        on_device,
        mesh=mesh,
        in_specs=placed,
        out_specs=(P("req", "dev", None), P("req", "dev", None, None)),
        check_vma=False,
    )
```

```python
import jax
import jax.numpy as jnp
from jax import lax
from jax.experimental import pallas as pl
from jax.experimental.pallas import tpu as pltpu
from jax.sharding import PartitionSpec as P

MESH = pl.DeviceIdType.MESH
HQ = 32
KVH = 8
HD = 64
PAGE = 16
ROPE_BASE = 10000000.0
EPS = 1e-05
ATTENTION_SCALE = 0.015625
MASKED = -1e30
BF = jnp.bfloat16
F32 = jnp.float32
QT = 256
KC = 1024


def root_norm(activations, norm_gain):
    widened = activations.astype(F32)
    inverse_rms = lax.rsqrt(jnp.mean(widened * widened, axis=-1, keepdims=True) + EPS)
    return (widened * inverse_rms * norm_gain).astype(BF)


def transposed_product(left, right):
    return lax.dot_general(left, right, (((1,), (1,)), ((), ())), preferred_element_type=F32)


def dev_of(zh, x, c):
    return (zh * 4 + x) * 2 + c


def place():
    d = lax.axis_index("dev")
    return d // 8, (d // 2) % 4, d % 2


class Links:
    def __init__(self, send_sems, recv_sems):
        self.send_sems, self.recv_sems = send_sems, recv_sems
        self.copies = []

    def make(self, i, src, dst, to):
        return pltpu.make_async_remote_copy(
            src_ref=src,
            dst_ref=dst,
            send_sem=self.send_sems.at[i],
            recv_sem=self.recv_sems.at[i],
            device_id=to,
            device_id_type=MESH,
        )

    def send(self, src, dst, to):
        i = len(self.copies)
        copy = self.make(i, src, dst, to)
        copy.start()
        self.copies.append(copy)
        return i, to

    def recv(self, handle, region):
        i, to = handle
        self.make(i, region, region, to).wait_recv()

    def drain(self):
        for copy in self.copies:
            copy.wait_send()


class Locals:
    def __init__(self, sems):
        self.sems, self.copies = sems, []

    def copy(self, src, dst):
        copy = pltpu.make_async_copy(src, dst, self.sems.at[len(self.copies)])
        copy.start()
        self.copies.append(copy)
        return copy


def greet(partners):
    barrier = pltpu.get_barrier_semaphore()
    for partner in partners:
        pl.semaphore_signal(barrier, inc=1, device_id=partner, device_id_type=MESH)
    pl.semaphore_wait(barrier, len(partners))


def halves(ref, i):
    rows = ref.shape[1] // 2
    return [ref.at[i, pl.ds(0, rows)], ref.at[i, pl.ds(rows, rows)]]


class Ring:
    def __init__(self, links, i, tos, blk, half, own=None, mate=None, there=None):
        self.l, self.i, self.tos, self.blk, self.half = links, i, tos, blk, half
        self.own = blk(i) if own is None else own
        self.mate, self.there = mate, there
        self.waits = []

    def core(self, j, src=None):
        if self.mate is not None:
            here = self.blk(j)
            self.waits.append((self.l.send(here if src is None else src, here, self.mate), self.there(j)))

    def start(self, core=True):
        mine = self.blk(self.i)
        self.h = [self.l.send(self.own, mine, to) for to in self.tos]
        if core:
            self.core(self.i, self.own)

    def near(self):
        self.f = []
        for s, off in ((0, 3), (1, 1)):
            j = (self.i + off) % 4
            self.l.recv(self.h[s], self.blk(j))
            piece = self.half(j, s)
            self.f.append(self.l.send(piece, piece, self.tos[s]))
            self.core(j)

    def far(self):
        j = (self.i + 2) % 4
        for s in (0, 1):
            self.l.recv(self.f[s], self.half(j, s))
        self.core(j)

    def ready(self):
        for handle, region in self.waits:
            self.l.recv(handle, region)


class PlaneGather:
    def __init__(self, links, out, x_first):
        self.l, self.out, self.x_first = links, out, x_first
        zh, x, c = place()
        r = lax.axis_index("req")
        self.x, self.y, self.rows = x, r % 4, pl.ds(0 if x_first else 16, 16)
        xs = [{"dev": dev_of(zh, (x + s) % 4, c)} for s in (1, 3)]
        ys = [{"req": r // 4 * 4 + (self.y + s) % 4} for s in (1, 3)]
        self.one, self.two = (xs, ys) if x_first else (ys, xs)
        self.h2, self.f2 = {}, {}

    def id(self, a, b):
        dx, dy = (a, b) if self.x_first else (b, a)
        return (self.x + dx) % 4 * 4 + (self.y + dy) % 4

    def blk(self, a, b):
        return self.out.at[:, self.id(a, b), self.rows]

    def half(self, a, b, s):
        wide = self.out.shape[3] // 2
        return self.out.at[:, self.id(a, b), self.rows, pl.ds(s * wide, wide)]

    def both(self, ref, tos):
        return [self.l.send(ref, ref, to) for to in tos]

    def start_one(self):
        self.h1 = self.both(self.blk(0, 0), self.one)

    def start_two(self):
        self.h2[0] = self.both(self.blk(0, 0), self.two)

    def near_one(self):
        self.f1 = []
        for s, a in ((0, 3), (1, 1)):
            self.l.recv(self.h1[s], self.blk(a, 0))
            piece = self.half(a, 0, s)
            self.f1.append(self.l.send(piece, piece, self.one[s]))

    def spread(self):
        for a in (3, 1):
            self.h2[a] = self.both(self.blk(a, 0), self.two)

    def far_one(self):
        self.g2 = []
        for s in (0, 1):
            piece = self.half(2, 0, s)
            self.l.recv(self.f1[s], piece)
            self.g2.append(self.both(piece, self.two))

    def near_two(self, a):
        self.f2[a] = []
        for s, b in ((0, 3), (1, 1)):
            self.l.recv(self.h2[a][s], self.blk(a, b))
            piece = self.half(a, b, s)
            self.f2[a].append(self.l.send(piece, piece, self.two[s]))

    def near_two_far(self):
        self.f2[2] = []
        for s, b in ((0, 3), (1, 1)):
            piece = self.half(2, b, s)
            self.l.recv(self.g2[s][s], piece)
            self.f2[2].append(self.l.send(piece, piece, self.two[s]))
        for s, b in ((0, 3), (1, 1)):
            self.l.recv(self.g2[1 - s][s], self.half(2, b, 1 - s))

    def far_two(self):
        for a in (0, 3, 1, 2):
            for s in (0, 1):
                self.l.recv(self.f2[a][s], self.half(a, 2, s))


class RowScatter:
    def __init__(self, links, part, rc, q, xh, xf, along_z=False):
        self.l = links
        self.part, self.rc, self.q, self.xh, self.xf = part, rc, q, xh, xf
        zh, x, c = place()
        self.x, self.c = zh if along_z else x, c
        if along_z:
            self.xs = [{"dev": dev_of((zh + s) % 4, x, c)} for s in (1, 3)]
        else:
            self.xs = [{"dev": dev_of(zh, (x + s) % 4, c)} for s in (1, 3)]
        self.mate = {"dev": dev_of(zh, x, 1 - c)}
        self.dx = (2, 1, 3, 0)
        self.ch, self.x1, self.x2 = {}, [], []

    def block(self, k, other=False):
        return ((self.x + self.dx[k]) % 4) * 2 + (1 - self.c if other else self.c)

    def cores(self, ks):
        for k in ks:
            self.ch[k] = self.l.send(self.part.at[self.block(k, True)], self.rc.at[k], self.mate)

    def arrive(self, k):
        self.l.recv(self.ch[k], self.rc.at[k])

    def own(self, k, at):
        return self.part[self.block(k), at].astype(F32) + self.rc[k, at].astype(F32)

    def first(self):
        self.arrive(0)
        for s in (0, 1):
            at = pl.ds(16 * s, 16)
            self.q[0, at] = self.own(0, at).astype(BF)
            self.x1.append(self.l.send(self.q.at[0, at], self.xh.at[s], self.xs[s]))

    def push(self, s, q, more=None):
        at = pl.ds(16 * q, 16)
        value = self.own(1 + s, at)
        if more is not None:
            value = value + more
        self.q[1 + s, at] = value.astype(BF)
        self.x2.append((self.l.send(self.q.at[1 + s, at], self.xf.at[s, at], self.xs[s]), self.xf.at[s, at]))

    def second(self):
        for s in (0, 1):
            self.arrive(1 + s)
            self.push(s, 1 - s)
        for s in (0, 1):
            self.l.recv(self.x1[s], self.xh.at[s])
            self.push(s, s, self.xh[s].astype(F32))

    def total(self):
        self.arrive(3)
        value = self.own(3, pl.ds(0, 32))
        for handle, region in self.x2:
            self.l.recv(handle, region)
        return value + self.xf[0].astype(F32) + self.xf[1].astype(F32)


def z_neighbours():
    zh, x, c = place()
    r = lax.axis_index("req")
    z = zh * 2 + r // 4
    tos = []
    for step in (1, 7):
        other = (z + step) % 8
        tos.append({"req": other % 2 * 4 + r % 4, "dev": dev_of(other // 2, x, c)})
    return tos


class ColumnGather:
    def __init__(self, links, out):
        self.l, self.out = links, out
        self.tos = z_neighbours()
        zh, x, c = place()
        self.mate = {"dev": dev_of(zh, x, 1 - c)}
        self.h, self.waits = {}, {}

    def piece(self, k, p):
        return self.out.at[k % 8, 0, pl.ds(16 * p, 16)]

    def core(self, k):
        self.waits[k % 8] = self.l.send(self.out.at[k % 8, 0], self.out.at[k % 8, 1], self.mate)

    def pass_on(self, s, k, p):
        sign = -1 if s == 0 else 1
        self.h[s, k + 1, p] = self.l.send(self.piece(sign * k, p), self.piece(sign * (k + 1), p), self.tos[s])

    def start(self):
        for p in (0, 1):
            for s in (0, 1):
                self.pass_on(s, 0, p if s == 0 else 1 - p)
        self.core(0)

    def hop(self, k):
        for p in (0, 1):
            for s in (0, 1):
                q = p if s == 0 else 1 - p
                self.l.recv(self.h[s, k, q], self.piece(-k if s == 0 else k, q))
                if k < 3 or q == s:
                    self.pass_on(s, k, q)
        self.core(k)
        self.core(-k)

    def last(self):
        for s in (0, 1):
            self.l.recv(self.h[s, 4, s], self.piece(4, s))
        self.core(4)

    def ready(self, ks):
        for k in ks:
            self.l.recv(self.waits[k % 8], self.out.at[k % 8, 1])


class ColumnScatter:
    def __init__(self, links, part, rc, q, arrived):
        self.l, self.part, self.rc, self.q, self.arrived = links, part, rc, q, arrived
        self.tos = z_neighbours()
        zh, x, c = place()
        self.mate = {"dev": dev_of(zh, x, 1 - c)}
        self.ch, self.h = {}, {}

    def cores(self, ks):
        for k in ks:
            self.ch[k] = self.l.send(self.part.at[k, 1], self.rc.at[k], self.mate)

    def arrive(self, ks):
        for k in ks:
            self.l.recv(self.ch[k], self.rc.at[k])

    def own(self, k, p):
        at = pl.ds(16 * p, 16)
        return self.part[k % 8, 0, at].astype(F32) + self.rc[k % 8, at].astype(F32)

    def hop(self, k):
        for p in (0, 1):
            for s in (0, 1):
                q = 1 - s if p == 0 else s
                if k == 4 and q != s:
                    continue
                value = self.own(k if s == 0 else -k, q)
                if (s, k + 1, q) in self.h:
                    slot = self.arrived.at[s, k + 1 - 2, q]
                    self.l.recv(self.h[s, k + 1, q], slot)
                    value = value + slot[...].astype(F32)
                self.q[s, k - 1, q] = value.astype(BF)
                self.h[s, k, q] = self.l.send(self.q.at[s, k - 1, q], self.arrived.at[s, (k - 2) % 4, q], self.tos[s])

    def total(self, p):
        value = self.own(0, p)
        for s in (0, 1):
            slot = self.arrived.at[s, 3, p]
            self.l.recv(self.h[s, 1, p], slot)
            value = value + slot[...].astype(F32)
        return value


def layer_kernel(
    hid, pool, wq, wkv, wo, gate, up, down, gain_one, gain_two, cosine, sine, bias,
    out, kv_out,
    hid_col, relay, kv_all, wq_all, wkv_all, wo_all, wall, nrm, q_all, fresh, s_ref, att,
    part1, rc1, q1, xh1, xf1, residual, rows, act, part2, rc2, q2, arrived2,
    send_sems, recv_sems, local_sems,
):
    zh, x, c = place()
    r = lax.axis_index("req")
    width = hid.shape[1]
    links, local = Links(send_sems, recv_sems), Locals(local_sems)
    zs = [{"dev": dev_of((zh + s) % 4, x, c)} for s in (1, 3)]
    xs = [{"dev": dev_of(zh, (x + s) % 4, c)} for s in (1, 3)]
    mate = {"dev": dev_of(zh, x, 1 - c)}
    y = r % 4
    ys = [{"req": r // 4 * 4 + (y + s) % 4} for s in (1, 3)]
    a_plane, b_plane = PlaneGather(links, wall, True), PlaneGather(links, wall, False)
    ag2 = ColumnGather(links, rows)
    column = {(dz, dc): {"dev": dev_of((zh + dz) % 4, x, (c + dc) % 2)} for dz in range(4) for dc in range(2)}
    del column[0, 0]

    hidden = Ring(
        links, zh, zs, lambda j: hid_col.at[j * 2 + c], lambda j, s: hid_col.at[j * 2 + c, pl.ds(16 * s, 16)],
        hid, mate, lambda j: hid_col.at[j * 2 + 1 - c],
    )
    wide = width // 4

    def quarter(k):
        return pl.ds(pl.multiple_of(k * wide, wide), wide)

    q_ring = Ring(
        links, x, xs, lambda j: wq_all.at[j, :, :, quarter(y)], lambda j, s: wq_all.at[j, s, :, quarter(y)],
        wq.at[:, :, quarter(y)],
    )
    kv_ring = Ring(
        links, x, xs, lambda j: wkv_all.at[j * 2 + c, :, quarter(y)],
        lambda j, s: wkv_all.at[j * 2 + c, pl.ds(16 * s, 16), quarter(y)], wkv.at[:, quarter(y)],
    )
    o_ring = Ring(
        links, x, xs, lambda j: wo_all.at[j, pl.ds(64, 64), quarter(y)],
        lambda j, s: wo_all.at[j, pl.ds(64 + 32 * s, 32), quarter(y)], wo.at[:, quarter(y)],
    )
    o_rings = {}
    for dx in (1, 2, 3):
        o_rings[dx] = Ring(
            links, y, ys, lambda k, j=(x + dx) % 4: wo_all.at[j, pl.ds(64, 64), quarter(k)],
            lambda k, s, j=(x + dx) % 4: wo_all.at[j, pl.ds(64 + 32 * s, 32), quarter(k)],
        )
    y_rings = {}
    for dx in (1, 2, 3):
        j = (x + dx) % 4
        y_rings[dx] = [
            Ring(
                links, y, ys, lambda k, j=j: wkv_all.at[j * 2 + c, :, quarter(k)],
                lambda k, s, j=j: wkv_all.at[j * 2 + c, pl.ds(16 * s, 16), quarter(k)],
            ),
            Ring(
                links, y, ys, lambda k, j=j: wq_all.at[j, :, :, quarter(k)],
                lambda k, s, j=j: wq_all.at[j, s, :, quarter(k)],
            ),
        ]
    pages = Ring(
        links, x, xs, lambda j: kv_all.at[:, j * 2 + c], lambda j, s: kv_all.at[s, j * 2 + c],
        None, mate, lambda j: kv_all.at[:, j * 2 + 1 - c],
    )
    new = Ring(
        links, x, xs, lambda j: fresh.at[c, :, j], lambda j, s: fresh.at[c, pl.ds(2 * s, 2), j],
        None, mate, lambda j: fresh.at[1 - c, :, j],
    )
    greet(list(column.values()) + xs + ag2.tos + ys)

    mine = x * 2 + c
    near_pages, relayed = [], []
    for s, dz in ((0, 1), (1, 3)):
        near_pages.append(links.send(pool.at[pl.ds(2 * ((zh + dz) % 4), 2)], kv_all.at[:, mine, zh], zs[s]))
        relayed.append(links.send(pool.at[2 * ((zh + 2) % 4) + s], relay.at[s], zs[s]))
    kv_ring.start()
    q_ring.start()
    hidden.start()
    o_ring.start()
    w_core = [(links.send(wkv, wkv_all.at[mine], mate), wkv_all.at[x * 2 + 1 - c])]
    own_planes = [local.copy(own, wall.at[a, x * 4 + y]) for a, own in enumerate((gate, up, down))]
    own_pages = local.copy(pool.at[pl.ds(2 * zh, 2)], kv_all.at[:, mine, zh])
    early = [
        local.copy(hid, hid_col.at[zh * 2 + c]),
        local.copy(wkv, wkv_all.at[mine]),
        local.copy(wq, wq_all.at[x]),
    ]
    own_wo = local.copy(wo, wo_all.at[x, pl.ds(64, 64)])
    kv_ring.near()
    q_ring.near()
    for dx in (1, 3):
        for ring in y_rings[dx]:
            ring.start()
    o_ring.near()
    for copy in own_planes:
        copy.wait()
    a_plane.start_one()
    kv_ring.far()
    q_ring.far()
    for ring in y_rings[2]:
        ring.start()
    far_pages = []
    for s, dz in ((0, 3), (1, 1)):
        links.recv(relayed[s], relay.at[s])
        far_pages.append(links.send(relay.at[s], kv_all.at[s, mine, (zh + dz) % 4], zs[s]))
    for dx in (1, 3, 2):
        for ring in y_rings[dx]:
            ring.near()
    o_ring.far()
    for dx in (1, 3, 2):
        o_rings[dx].start()
    b_plane.start_one()
    a_plane.start_two()
    for s, dz in ((0, 3), (1, 1)):
        links.recv(near_pages[s], kv_all.at[:, mine, (zh + dz) % 4])
    own_pages.wait()
    for s in (0, 1):
        links.recv(far_pages[s], kv_all.at[s, mine, (zh + 2) % 4])
    pages.start()
    hidden.near()
    a_plane.near_one()
    for k in range(4):
        wo_all[k, pl.ds(0, 64)] = jnp.zeros((64, width), BF)
    for copy in early:
        copy.wait()
    for dx in (1, 3, 2):
        for ring in y_rings[dx]:
            ring.far()
        block = (x + dx) % 4 * 2
        w_core.append((links.send(wkv_all.at[block + c], wkv_all.at[block + c], mate), wkv_all.at[block + 1 - c]))
    for dx in (1, 3, 2):
        o_rings[dx].near()
    hidden.far()
    pages.near()
    b_plane.near_one()
    a_plane.spread()
    hidden.ready()
    for handle, region in w_core:
        links.recv(handle, region)

    def norm(i, carry):
        nrm[pl.ds(pl.multiple_of(i * 32, 32), 32), :] = root_norm(hid_col[i], gain_one[...])
        return carry

    lax.fori_loop(0, 8, norm, 0, unroll=2)
    lane = lax.broadcasted_iota(jnp.int32, (256, 2 * HD), 1)
    first_half = lane % HD < HD // 2

    def rotate(pairs):
        swapped = jnp.where(first_half, pltpu.roll(pairs, 96, 1), pltpu.roll(pairs, 32, 1))
        return pairs * cosine[...] + swapped * sine[...]

    keyvals = transposed_product(nrm[...], wkv_all[...].reshape(256, width)).astype(BF)
    for k in (0, 1):
        pairs = keyvals[:, k * 128 : (k + 1) * 128].astype(F32)
        fresh[k, :, x] = jnp.where(lane < HD, rotate(pairs), pairs).astype(BF).reshape(4, 64, 128)
    new.start(False)
    kv_h = []
    for (dz, dc), to in column.items():
        src = fresh.at[c, (zh + dz) % 4, x, pl.ds(32 * ((c + dc) % 2), 32)]
        kv_h.append((links.send(src, kv_out.at[2 * zh + c], to), kv_out.at[2 * ((zh + 4 - dz) % 4) + (c + dc) % 2]))
    own_kv = local.copy(fresh.at[c, zh, x, pl.ds(32 * c, 32)], kv_out.at[2 * zh + c])
    queries = transposed_product(nrm[...], wq_all[...].reshape(256, width))
    for k in (0, 1):
        turned = rotate(queries[:, k * 128 : (k + 1) * 128]) * ATTENTION_SCALE
        for i in (0, 1):
            head = turned if i == 0 else pltpu.roll(turned, 64, 1)
            q_all[k, :, i] = jnp.where(lane < HD, head, 0.0).astype(BF).reshape(4, 64, 128)
    pages.far()
    pages.ready()

    prefix = 4096
    per_block = KC // 512

    def lanes_max(running, scores):
        for k in range(scores.shape[1] // 128):
            running = jnp.maximum(running, scores[:, k * 128 : (k + 1) * 128])
        return running

    def keys_at(k, i):
        return kv_all[k, pl.ds(i * per_block, per_block)].reshape(KC, 2 * HD)

    def queries_of(k, p):
        return q_all[k, pl.ds(2 * p, 2)].reshape(QT, 2 * HD)

    def score(k, p):
        q = queries_of(k, p)

        def score_prefix(i, running):
            at = pl.ds(pl.multiple_of(i * KC, KC), KC)
            scores = transposed_product(q, keys_at(k, i)) + bias[:, at]
            s_ref[k, :, at] = scores
            return lanes_max(running, scores)

        return lax.fori_loop(0, prefix // KC, score_prefix, jnp.full((QT, 128), MASKED, F32), unroll=True)

    def attend(k, p, running):
        q = queries_of(k, p)
        row = lax.broadcasted_iota(jnp.int32, (QT, KC), 0)
        token = (2 * p + row // 128) * 256 + x * 64 + row % 64
        col = lax.broadcasted_iota(jnp.int32, (QT, KC), 1)
        added = fresh[k].reshape(KC, 2 * HD)
        scores = jnp.where(col <= token, transposed_product(q, added), MASKED)
        s_ref[k, :, pl.ds(prefix, KC)] = scores
        running = lanes_max(running, scores)
        top = jnp.broadcast_to(jnp.max(running, axis=1, keepdims=True), (QT, 128))

        def weigh(at, keys, carried):
            total, summed = carried
            scores = s_ref[k, :, at]
            pieces = []
            for n in range(scores.shape[1] // 128):
                weights = jnp.exp(scores[:, n * 128 : (n + 1) * 128] - top)
                total = total + weights
                pieces.append(weights.astype(BF))
            weights = jnp.concatenate(pieces, axis=1)
            return total, summed + jnp.dot(weights, keys, preferred_element_type=F32)

        def weigh_prefix(i, carried):
            return weigh(pl.ds(pl.multiple_of(i * KC, KC), KC), keys_at(k, i), carried)

        carried = (jnp.zeros((QT, 128), F32), jnp.zeros((QT, 2 * HD), F32))
        carried = lax.fori_loop(0, prefix // KC, weigh_prefix, carried, unroll=True)
        total, summed = weigh(pl.ds(prefix, KC), added, carried)
        mixed = (summed / jnp.sum(total, axis=1, keepdims=True)).astype(BF).reshape(2, 2, 64, 128)
        for z in (0, 1):
            for i in (0, 1):
                att[2 * k + i, pl.ds(pl.multiple_of((2 * p + z) * 64, 64), 64)] = mixed[z, i]

    one = RowScatter(links, part1, rc1, q1, xh1, xf1, True)

    def out_project(p):
        tokens = pl.ds(pl.multiple_of(p * 128, 128), 128)

        def columns(n, carry):
            at = pl.ds(pl.multiple_of(n * 512, 512), 512)
            term = None
            for k in (0, 2):
                heads = jnp.concatenate([att[k, tokens], att[k + 1, tokens]], axis=1)
                product = jnp.dot(heads, wo_all[pl.ds(k, 2), :, at].reshape(256, 512), preferred_element_type=F32)
                term = product if term is None else term + product
            part1[pl.ds(4 * p, 4), :, at] = term.astype(BF).reshape(4, 32, 512)
            return carry

        lax.fori_loop(0, width // 512, columns, 0, unroll=True)

    far_pair, own_pair = 1 - zh // 2, zh // 2
    running = [score(0, far_pair)]
    new.near()
    running.append(score(1, far_pair))
    new.far()
    a_plane.far_one()
    b_plane.start_two()
    b_plane.spread()
    new.ready()
    attend(0, far_pair, running[0])
    for dx in (1, 3, 2):
        o_rings[dx].far()
    own_wo.wait()
    a_plane.near_two(0)
    attend(1, far_pair, running[1])
    out_project(far_pair)
    one.cores((0,))
    a_plane.near_two(3)
    attend(0, own_pair, score(0, own_pair))
    one.first()
    b_plane.far_one()
    a_plane.near_two(1)
    b_plane.near_two(0)
    attend(1, own_pair, score(1, own_pair))
    out_project(own_pair)
    one.cores((1, 2, 3))
    one.second()
    residual[...] = one.total() + hid[...].astype(F32)
    rows[0, 0] = root_norm(residual[...], gain_two[...])
    ag2.start()
    b_plane.near_two(3)
    b_plane.near_two(1)
    a_plane.near_two_far()
    ag2.hop(1)
    b_plane.near_two_far()
    ag2.hop(2)
    ag2.hop(3)
    a_plane.far_two()
    b_plane.far_two()
    ag2.ready((0, 1, 7, 2))

    two = ColumnScatter(links, part2, rc2, q2, arrived2)

    def feed(ks):
        tokens = jnp.concatenate([rows[k].reshape(64, width) for k in ks], axis=0)
        nrm[...] = tokens

        def units(h, carry):
            some = pl.ds(h * 8, 8)
            gated = transposed_product(nrm[...], wall[0, some].reshape(256, width))
            raised = transposed_product(nrm[...], wall[1, some].reshape(256, width))
            act[h] = (gated / (1.0 + jnp.exp(-gated)) * raised).astype(BF)
            return carry

        lax.fori_loop(0, 2, units, 0, unroll=True)

        def columns(n, carry):
            at = pl.ds(pl.multiple_of(n * 512, 512), 512)
            activated = jnp.concatenate([act[0], act[1]], axis=1)
            term = jnp.dot(activated, wall[2, :, :, at].reshape(512, 512), preferred_element_type=F32)
            term = term.astype(BF).reshape(4, 2, 32, 512)
            for i, k in enumerate(ks):
                part2[k, :, :, at] = term[i]
            return carry

        lax.fori_loop(0, width // 512, columns, 0, unroll=True)

    feed((7, 0, 1, 2))
    two.cores((7, 0, 1, 2))
    ag2.last()
    ag2.ready((3, 5, 6, 4))
    feed((3, 4, 5, 6))
    two.cores((4, 3, 5, 6))
    two.arrive((7, 0, 1, 2, 4, 3, 5, 6))
    for k in (4, 3, 2, 1):
        two.hop(k)
    for p in (0, 1):
        at = pl.ds(16 * p, 16)
        out[at, :] = (residual[at, :] + two.total(p)).astype(BF)
    for handle, region in kv_h:
        links.recv(handle, region)
    own_kv.wait()
    links.drain()


def vmem(count):
    return [pl.BlockSpec(memory_space=pltpu.VMEM)] * count


def on_device(
    hidden_in, attention_gain, query_weight, keyval_weight, out_weight, feedforward_gain,
    gate_weight, up_weight, down_weight, prefix_pool, page_table, prefix_length,
):
    width = hidden_in.shape[2]
    tokens = 1024
    length = prefix_length[0]
    slots = prefix_pool.shape[1] * PAGE
    pool = prefix_pool[0].transpose(2, 0, 1, 3).reshape(KVH, slots, 2 * HD)

    logical = jnp.sum(
        jnp.where(
            page_table[0][None, :] == jnp.arange(256, dtype=jnp.int32)[:, None],
            jnp.arange(256, dtype=jnp.int32)[None, :],
            0,
        ),
        axis=1,
    )
    slot = logical[:, None] * PAGE + jnp.arange(PAGE, dtype=jnp.int32)[None, :]
    bias = jnp.where(slot < length, 0.0, MASKED).astype(F32)
    bias = bias.reshape(4, 8, slots).transpose(1, 0, 2).reshape(1, 32 * slots)

    index = jnp.arange(256, dtype=jnp.int32)
    column = (lax.axis_index("dev") // 2) % 4
    positions = (length + index // 64 * 256 + column * 64 + index % 64).astype(F32)
    half = HD // 2
    frequency = ROPE_BASE ** (-jnp.arange(half, dtype=F32) / half)
    angles = positions[:, None] * frequency[None, :]
    cosine, sine = jnp.cos(angles), jnp.sin(angles)
    cosine = jnp.concatenate([cosine] * 4, axis=1)
    sine = jnp.concatenate([-sine, sine, -sine, sine], axis=1)

    buffers = [
        ((8, 32, width), BF),
        ((2, slots, 2 * HD), BF),
        ((2, 8, 4, slots, 2 * HD), BF),
        ((4, 2, 32, width), BF),
        ((8, 32, width), BF),
        ((4, 128, width), BF),
        ((3, 16, 32, width), BF),
        ((256, width), BF),
        ((2, 4, 2, 64, 2 * HD), BF),
        ((2, 4, 4, 64, 2 * HD), BF),
        ((2, QT, 32 * slots + tokens), F32),
        ((4, 256, 2 * HD), BF),
        ((8, 32, width), BF),
        ((4, 32, width), BF),
        ((3, 32, width), BF),
        ((2, 16, width), BF),
        ((2, 32, width), BF),
        ((32, width), F32),
        ((8, 2, 32, width), BF),
        ((2, 256, 256), BF),
        ((8, 2, 32, width), BF),
        ((8, 32, width), BF),
        ((2, 4, 2, 16, width), BF),
        ((2, 4, 2, 16, width), BF),
    ]
    hidden_out, kv_out = pl.pallas_call(
        layer_kernel,
        out_shape=[jax.ShapeDtypeStruct((32, width), BF), jax.ShapeDtypeStruct((8, 32, 2 * HD), BF)],
        in_specs=vmem(13),
        out_specs=vmem(2),
        scratch_shapes=[pltpu.VMEM(*b) for b in buffers] + [
            pltpu.SemaphoreType.DMA((COPIES,)),
            pltpu.SemaphoreType.DMA((COPIES,)),
            pltpu.SemaphoreType.DMA((16,)),
        ],
        compiler_params=pltpu.CompilerParams(collective_id=0, has_side_effects=True, vmem_limit_bytes=60 << 20),
        name="layer",
    )(
        hidden_in[0], pool, query_weight.reshape(2, 32, width), keyval_weight, out_weight,
        gate_weight, up_weight, down_weight,
        attention_gain.reshape(1, width), feedforward_gain.reshape(1, width), cosine, sine, bias,
    )
    return hidden_out[None], kv_out.transpose(1, 0, 2)[None]


COPIES = 230


def solution(mesh):
    placed = (
        P("req", "dev", None),
        P(),
        P("dev", None),
        P("dev", None),
        P("dev", None),
        P(),
        P(("req", "dev"), None),
        P(("req", "dev"), None),
        P(("req", "dev"), None),
        P("req", "dev", None, None, None),
        P("req", None),
        P("req"),
    )
    return jax.shard_map(
        on_device,
        mesh=mesh,
        in_specs=placed,
        out_specs=(P("req", "dev", None), P("req", "dev", None, None)),
        check_vma=False,
    )
```

```python
import jax
import jax.numpy as jnp
from jax import lax
from jax.experimental import pallas as pl
from jax.experimental.pallas import tpu as pltpu
from jax.sharding import PartitionSpec as P

MESH = pl.DeviceIdType.MESH
HQ = 32
KVH = 8
HD = 64
PAGE = 16
ROPE_BASE = 10000000.0
EPS = 1e-05
ATTENTION_SCALE = 0.015625
MASKED = -1e30
BF = jnp.bfloat16
F32 = jnp.float32
QT = 256
KC = 1024


def root_norm(activations, norm_gain):
    widened = activations.astype(F32)
    inverse_rms = lax.rsqrt(jnp.mean(widened * widened, axis=-1, keepdims=True) + EPS)
    return (widened * inverse_rms * norm_gain).astype(BF)


def transposed_product(left, right):
    return lax.dot_general(left, right, (((1,), (1,)), ((), ())), preferred_element_type=F32)


def dev_of(zh, x, c):
    return (zh * 4 + x) * 2 + c


def place():
    d = lax.axis_index("dev")
    return d // 8, (d // 2) % 4, d % 2


class Links:
    def __init__(self, send_sems, recv_sems):
        self.send_sems, self.recv_sems = send_sems, recv_sems
        self.copies = []

    def make(self, i, src, dst, to):
        return pltpu.make_async_remote_copy(
            src_ref=src,
            dst_ref=dst,
            send_sem=self.send_sems.at[i],
            recv_sem=self.recv_sems.at[i],
            device_id=to,
            device_id_type=MESH,
        )

    def send(self, src, dst, to):
        i = len(self.copies)
        copy = self.make(i, src, dst, to)
        copy.start()
        self.copies.append(copy)
        return i, to

    def recv(self, handle, region):
        i, to = handle
        self.make(i, region, region, to).wait_recv()

    def drain(self):
        for copy in self.copies:
            copy.wait_send()


class Locals:
    def __init__(self, sems):
        self.sems, self.copies = sems, []

    def copy(self, src, dst):
        copy = pltpu.make_async_copy(src, dst, self.sems.at[len(self.copies)])
        copy.start()
        self.copies.append(copy)
        return copy


def greet(partners):
    barrier = pltpu.get_barrier_semaphore()
    for partner in partners:
        pl.semaphore_signal(barrier, inc=1, device_id=partner, device_id_type=MESH)
    pl.semaphore_wait(barrier, len(partners))


def halves(ref, i):
    rows = ref.shape[1] // 2
    return [ref.at[i, pl.ds(0, rows)], ref.at[i, pl.ds(rows, rows)]]


class Ring:
    def __init__(self, links, i, tos, blk, half, own=None, mate=None, there=None):
        self.l, self.i, self.tos, self.blk, self.half = links, i, tos, blk, half
        self.own = blk(i) if own is None else own
        self.mate, self.there = mate, there
        self.waits = []

    def core(self, j, src=None):
        if self.mate is not None:
            here = self.blk(j)
            self.waits.append((self.l.send(here if src is None else src, here, self.mate), self.there(j)))

    def start(self, core=True):
        mine = self.blk(self.i)
        self.h = [self.l.send(self.own, mine, to) for to in self.tos]
        if core:
            self.core(self.i, self.own)

    def near(self):
        self.f = []
        for s, off in ((0, 3), (1, 1)):
            j = (self.i + off) % 4
            self.l.recv(self.h[s], self.blk(j))
            piece = self.half(j, s)
            self.f.append(self.l.send(piece, piece, self.tos[s]))
            self.core(j)

    def far(self):
        j = (self.i + 2) % 4
        for s in (0, 1):
            self.l.recv(self.f[s], self.half(j, s))
        self.core(j)

    def ready(self):
        for handle, region in self.waits:
            self.l.recv(handle, region)


class PlaneGather:
    def __init__(self, links, out, x_first):
        self.l, self.out, self.x_first = links, out, x_first
        zh, x, c = place()
        r = lax.axis_index("req")
        self.x, self.y, self.rows = x, r % 4, pl.ds(0 if x_first else 16, 16)
        xs = [{"dev": dev_of(zh, (x + s) % 4, c)} for s in (1, 3)]
        ys = [{"req": r // 4 * 4 + (self.y + s) % 4} for s in (1, 3)]
        self.one, self.two = (xs, ys) if x_first else (ys, xs)
        self.h2, self.f2 = {}, {}

    def id(self, a, b):
        dx, dy = (a, b) if self.x_first else (b, a)
        return (self.x + dx) % 4 * 4 + (self.y + dy) % 4

    def blk(self, a, b):
        return self.out.at[:, self.id(a, b), self.rows]

    def half(self, a, b, s):
        wide = self.out.shape[3] // 2
        return self.out.at[:, self.id(a, b), self.rows, pl.ds(s * wide, wide)]

    def both(self, ref, tos):
        return [self.l.send(ref, ref, to) for to in tos]

    def start_one(self):
        self.h1 = self.both(self.blk(0, 0), self.one)

    def start_two(self):
        self.h2[0] = self.both(self.blk(0, 0), self.two)

    def near_one(self):
        self.f1 = []
        for s, a in ((0, 3), (1, 1)):
            self.l.recv(self.h1[s], self.blk(a, 0))
            piece = self.half(a, 0, s)
            self.f1.append(self.l.send(piece, piece, self.one[s]))

    def spread(self):
        for a in (3, 1):
            self.h2[a] = self.both(self.blk(a, 0), self.two)

    def far_one(self):
        self.g2 = []
        for s in (0, 1):
            piece = self.half(2, 0, s)
            self.l.recv(self.f1[s], piece)
            self.g2.append(self.both(piece, self.two))

    def near_two(self, a):
        self.f2[a] = []
        for s, b in ((0, 3), (1, 1)):
            self.l.recv(self.h2[a][s], self.blk(a, b))
            piece = self.half(a, b, s)
            self.f2[a].append(self.l.send(piece, piece, self.two[s]))

    def near_two_far(self):
        self.f2[2] = []
        for s, b in ((0, 3), (1, 1)):
            piece = self.half(2, b, s)
            self.l.recv(self.g2[s][s], piece)
            self.f2[2].append(self.l.send(piece, piece, self.two[s]))
        for s, b in ((0, 3), (1, 1)):
            self.l.recv(self.g2[1 - s][s], self.half(2, b, 1 - s))

    def far_two(self):
        for a in (0, 3, 1, 2):
            for s in (0, 1):
                self.l.recv(self.f2[a][s], self.half(a, 2, s))


class RowScatter:
    def __init__(self, links, part, rc, q, xh, xf, along_z=False):
        self.l = links
        self.part, self.rc, self.q, self.xh, self.xf = part, rc, q, xh, xf
        zh, x, c = place()
        self.x, self.c = zh if along_z else x, c
        if along_z:
            self.xs = [{"dev": dev_of((zh + s) % 4, x, c)} for s in (1, 3)]
        else:
            self.xs = [{"dev": dev_of(zh, (x + s) % 4, c)} for s in (1, 3)]
        self.mate = {"dev": dev_of(zh, x, 1 - c)}
        self.dx = (2, 1, 3, 0)
        self.ch, self.x1, self.x2 = {}, [], []

    def block(self, k, other=False):
        return ((self.x + self.dx[k]) % 4) * 2 + (1 - self.c if other else self.c)

    def cores(self, ks):
        for k in ks:
            self.ch[k] = self.l.send(self.part.at[self.block(k, True)], self.rc.at[k], self.mate)

    def arrive(self, k):
        self.l.recv(self.ch[k], self.rc.at[k])

    def own(self, k, at):
        return self.part[self.block(k), at].astype(F32) + self.rc[k, at].astype(F32)

    def first(self):
        self.arrive(0)
        for s in (0, 1):
            at = pl.ds(16 * s, 16)
            self.q[0, at] = self.own(0, at).astype(BF)
            self.x1.append(self.l.send(self.q.at[0, at], self.xh.at[s], self.xs[s]))

    def push(self, s, q, more=None):
        at = pl.ds(16 * q, 16)
        value = self.own(1 + s, at)
        if more is not None:
            value = value + more
        self.q[1 + s, at] = value.astype(BF)
        self.x2.append((self.l.send(self.q.at[1 + s, at], self.xf.at[s, at], self.xs[s]), self.xf.at[s, at]))

    def second(self):
        for s in (0, 1):
            self.arrive(1 + s)
            self.push(s, 1 - s)
        for s in (0, 1):
            self.l.recv(self.x1[s], self.xh.at[s])
            self.push(s, s, self.xh[s].astype(F32))

    def total(self):
        self.arrive(3)
        value = self.own(3, pl.ds(0, 32))
        for handle, region in self.x2:
            self.l.recv(handle, region)
        return value + self.xf[0].astype(F32) + self.xf[1].astype(F32)


def z_neighbours():
    zh, x, c = place()
    r = lax.axis_index("req")
    z = zh * 2 + r // 4
    tos = []
    for step in (1, 7):
        other = (z + step) % 8
        tos.append({"req": other % 2 * 4 + r % 4, "dev": dev_of(other // 2, x, c)})
    return tos


class ColumnGather:
    def __init__(self, links, out):
        self.l, self.out = links, out
        self.tos = z_neighbours()
        zh, x, c = place()
        self.mate = {"dev": dev_of(zh, x, 1 - c)}
        self.h, self.waits = {}, {}

    def piece(self, k, p):
        return self.out.at[k % 8, 0, pl.ds(16 * p, 16)]

    def core(self, k):
        self.waits[k % 8] = self.l.send(self.out.at[k % 8, 0], self.out.at[k % 8, 1], self.mate)

    def pass_on(self, s, k, p):
        sign = -1 if s == 0 else 1
        self.h[s, k + 1, p] = self.l.send(self.piece(sign * k, p), self.piece(sign * (k + 1), p), self.tos[s])

    def start(self):
        for p in (0, 1):
            for s in (0, 1):
                self.pass_on(s, 0, p if s == 0 else 1 - p)
        self.core(0)

    def hop(self, k):
        for p in (0, 1):
            for s in (0, 1):
                q = p if s == 0 else 1 - p
                self.l.recv(self.h[s, k, q], self.piece(-k if s == 0 else k, q))
                if k < 3 or q == s:
                    self.pass_on(s, k, q)
        self.core(k)
        self.core(-k)

    def last(self):
        for s in (0, 1):
            self.l.recv(self.h[s, 4, s], self.piece(4, s))
        self.core(4)

    def ready(self, ks):
        for k in ks:
            self.l.recv(self.waits[k % 8], self.out.at[k % 8, 1])


class ColumnScatter:
    def __init__(self, links, part, rc, q, arrived):
        self.l, self.part, self.rc, self.q, self.arrived = links, part, rc, q, arrived
        self.tos = z_neighbours()
        zh, x, c = place()
        self.mate = {"dev": dev_of(zh, x, 1 - c)}
        self.ch, self.h = {}, {}

    def cores(self, ks):
        for k in ks:
            self.ch[k] = self.l.send(self.part.at[k, 1], self.rc.at[k], self.mate)

    def arrive(self, ks):
        for k in ks:
            self.l.recv(self.ch[k], self.rc.at[k])

    def own(self, k, p):
        at = pl.ds(16 * p, 16)
        return self.part[k % 8, 0, at].astype(F32) + self.rc[k % 8, at].astype(F32)

    def hop(self, k):
        for p in (0, 1):
            for s in (0, 1):
                q = 1 - s if p == 0 else s
                if k == 4 and q != s:
                    continue
                value = self.own(k if s == 0 else -k, q)
                if (s, k + 1, q) in self.h:
                    slot = self.arrived.at[s, k + 1 - 2, q]
                    self.l.recv(self.h[s, k + 1, q], slot)
                    value = value + slot[...].astype(F32)
                self.q[s, k - 1, q] = value.astype(BF)
                self.h[s, k, q] = self.l.send(self.q.at[s, k - 1, q], self.arrived.at[s, (k - 2) % 4, q], self.tos[s])

    def total(self, p):
        value = self.own(0, p)
        for s in (0, 1):
            slot = self.arrived.at[s, 3, p]
            self.l.recv(self.h[s, 1, p], slot)
            value = value + slot[...].astype(F32)
        return value


def layer_kernel(
    hid, pool, wq, wkv, wo, gate, up, down, gain_one, gain_two, cosine, sine, bias,
    out, kv_out,
    hid_col, relay, kv_all, wq_all, wkv_all, wo_all, wall, nrm, q_all, fresh, s_ref, att,
    part1, rc1, q1, xh1, xf1, residual, rows, act, part2, rc2, q2, arrived2, kv_got,
    send_sems, recv_sems, local_sems,
):
    zh, x, c = place()
    r = lax.axis_index("req")
    width = hid.shape[1]
    links, local = Links(send_sems, recv_sems), Locals(local_sems)
    zs = [{"dev": dev_of((zh + s) % 4, x, c)} for s in (1, 3)]
    xs = [{"dev": dev_of(zh, (x + s) % 4, c)} for s in (1, 3)]
    mate = {"dev": dev_of(zh, x, 1 - c)}
    y = r % 4
    ys = [{"req": r // 4 * 4 + (y + s) % 4} for s in (1, 3)]
    a_plane, b_plane = PlaneGather(links, wall, True), PlaneGather(links, wall, False)
    ag2 = ColumnGather(links, rows)
    column = {(dz, dc): {"dev": dev_of((zh + dz) % 4, x, (c + dc) % 2)} for dz in range(4) for dc in range(2)}
    del column[0, 0]

    hidden = Ring(
        links, zh, zs, lambda j: hid_col.at[j * 2 + c], lambda j, s: hid_col.at[j * 2 + c, pl.ds(16 * s, 16)],
        hid, mate, lambda j: hid_col.at[j * 2 + 1 - c],
    )
    wide = width // 4

    def quarter(k):
        return pl.ds(pl.multiple_of(k * wide, wide), wide)

    q_ring = Ring(
        links, x, xs, lambda j: wq_all.at[j, :, :, quarter(y)], lambda j, s: wq_all.at[j, s, :, quarter(y)],
        wq.at[:, :, quarter(y)],
    )
    kv_ring = Ring(
        links, x, xs, lambda j: wkv_all.at[j * 2 + c, :, quarter(y)],
        lambda j, s: wkv_all.at[j * 2 + c, pl.ds(16 * s, 16), quarter(y)], wkv.at[:, quarter(y)],
    )
    o_ring = Ring(
        links, x, xs, lambda j: wo_all.at[j, pl.ds(64, 64), quarter(y)],
        lambda j, s: wo_all.at[j, pl.ds(64 + 32 * s, 32), quarter(y)], wo.at[:, quarter(y)],
    )
    o_rings = {}
    for dx in (1, 2, 3):
        o_rings[dx] = Ring(
            links, y, ys, lambda k, j=(x + dx) % 4: wo_all.at[j, pl.ds(64, 64), quarter(k)],
            lambda k, s, j=(x + dx) % 4: wo_all.at[j, pl.ds(64 + 32 * s, 32), quarter(k)],
        )
    y_rings = {}
    for dx in (1, 2, 3):
        j = (x + dx) % 4
        y_rings[dx] = [
            Ring(
                links, y, ys, lambda k, j=j: wkv_all.at[j * 2 + c, :, quarter(k)],
                lambda k, s, j=j: wkv_all.at[j * 2 + c, pl.ds(16 * s, 16), quarter(k)],
            ),
            Ring(
                links, y, ys, lambda k, j=j: wq_all.at[j, :, :, quarter(k)],
                lambda k, s, j=j: wq_all.at[j, s, :, quarter(k)],
            ),
        ]
    pages = Ring(
        links, x, xs, lambda j: kv_all.at[:, j * 2 + c], lambda j, s: kv_all.at[s, j * 2 + c],
        None, mate, lambda j: kv_all.at[:, j * 2 + 1 - c],
    )
    new = Ring(
        links, x, xs, lambda j: fresh.at[c, :, j], lambda j, s: fresh.at[c, pl.ds(2 * s, 2), j],
        None, mate, lambda j: fresh.at[1 - c, :, j],
    )
    greet(list(column.values()) + xs + ag2.tos + ys)

    mine = x * 2 + c
    near_pages, relayed, far_pages = [], [], []
    for s in (0, 1):
        relayed.append(links.send(pool.at[2 * ((zh + 2) % 4) + s], relay.at[s], zs[s]))
    for s, dz in ((0, 1), (1, 3)):
        near_pages.append(links.send(pool.at[pl.ds(2 * ((zh + dz) % 4), 2)], kv_all.at[:, mine, zh], zs[s]))
    kv_ring.start()
    q_ring.start()
    o_ring.start()
    w_core = [(links.send(wkv, wkv_all.at[mine], mate), wkv_all.at[x * 2 + 1 - c])]
    own_planes = [local.copy(own, wall.at[a, x * 4 + y]) for a, own in enumerate((gate, up, down))]
    own_pages = local.copy(pool.at[pl.ds(2 * zh, 2)], kv_all.at[:, mine, zh])
    early = [
        local.copy(hid, hid_col.at[zh * 2 + c]),
        local.copy(wkv, wkv_all.at[mine]),
        local.copy(wq, wq_all.at[x]),
    ]
    own_wo = local.copy(wo, wo_all.at[x, pl.ds(64, 64)])
    kv_ring.near()
    for s, dz in ((0, 3), (1, 1)):
        links.recv(relayed[s], relay.at[s])
        far_pages.append(links.send(relay.at[s], kv_all.at[s, mine, (zh + dz) % 4], zs[s]))
    hidden.start()
    q_ring.near()
    for dx in (1, 3):
        for ring in y_rings[dx]:
            ring.start()
    o_ring.near()
    for copy in own_planes:
        copy.wait()
    a_plane.start_one()
    kv_ring.far()
    q_ring.far()
    for ring in y_rings[2]:
        ring.start()
    for s, dz in ((0, 3), (1, 1)):
        links.recv(near_pages[s], kv_all.at[:, mine, (zh + dz) % 4])
    own_pages.wait()
    for s in (0, 1):
        links.recv(far_pages[s], kv_all.at[s, mine, (zh + 2) % 4])
    pages.start()
    for dx in (1, 3, 2):
        for ring in y_rings[dx]:
            ring.near()
    o_ring.far()
    for dx in (1, 3, 2):
        o_rings[dx].start()
    b_plane.start_one()
    a_plane.start_two()
    a_plane.near_one()
    for k in range(4):
        wo_all[k, pl.ds(0, 64)] = jnp.zeros((64, width), BF)
    for copy in early:
        copy.wait()
    hidden.near()
    pages.near()
    for dx in (1, 3, 2):
        for ring in y_rings[dx]:
            ring.far()
        block = (x + dx) % 4 * 2
        w_core.append((links.send(wkv_all.at[block + c], wkv_all.at[block + c], mate), wkv_all.at[block + 1 - c]))
    hidden.far()
    hidden.ready()
    for handle, region in w_core:
        links.recv(handle, region)

    def norm(i, carry):
        nrm[pl.ds(pl.multiple_of(i * 32, 32), 32), :] = root_norm(hid_col[i], gain_one[...])
        return carry

    lax.fori_loop(0, 8, norm, 0, unroll=2)
    lane = lax.broadcasted_iota(jnp.int32, (256, 2 * HD), 1)
    first_half = lane % HD < HD // 2

    def rotate(pairs):
        swapped = jnp.where(first_half, pltpu.roll(pairs, 96, 1), pltpu.roll(pairs, 32, 1))
        return pairs * cosine[...] + swapped * sine[...]

    keyvals = transposed_product(nrm[...], wkv_all[...].reshape(256, width)).astype(BF)
    for k in (0, 1):
        pairs = keyvals[:, k * 128 : (k + 1) * 128].astype(F32)
        fresh[k, :, x] = jnp.where(lane < HD, rotate(pairs), pairs).astype(BF).reshape(4, 64, 128)
    new.start(False)
    kv_h = []
    for (dz, dc), to in column.items():
        src = fresh.at[c, (zh + dz) % 4, x, pl.ds(32 * ((c + dc) % 2), 32)]
        kv_h.append((links.send(src, kv_got.at[2 * zh + c], to), kv_got.at[2 * ((zh + 4 - dz) % 4) + (c + dc) % 2]))
    own_kv = local.copy(fresh.at[c, zh, x, pl.ds(32 * c, 32)], kv_got.at[2 * zh + c])
    queries = transposed_product(nrm[...], wq_all[...].reshape(256, width))
    for k in (0, 1):
        turned = rotate(queries[:, k * 128 : (k + 1) * 128]) * ATTENTION_SCALE
        for i in (0, 1):
            head = turned if i == 0 else pltpu.roll(turned, 64, 1)
            q_all[k, :, i] = jnp.where(lane < HD, head, 0.0).astype(BF).reshape(4, 64, 128)
    pages.far()
    for dx in (1, 3, 2):
        o_rings[dx].near()
    a_plane.spread()
    pages.ready()

    prefix = 4096
    per_block = KC // 512

    def lanes_max(running, scores):
        for k in range(scores.shape[1] // 128):
            running = jnp.maximum(running, scores[:, k * 128 : (k + 1) * 128])
        return running

    def keys_at(k, i):
        return kv_all[k, pl.ds(i * per_block, per_block)].reshape(KC, 2 * HD)

    def queries_of(k, p):
        return q_all[k, pl.ds(2 * p, 2)].reshape(QT, 2 * HD)

    def score(k, p):
        q = queries_of(k, p)

        def score_prefix(i, running):
            at = pl.ds(pl.multiple_of(i * KC, KC), KC)
            scores = transposed_product(q, keys_at(k, i)) + bias[:, at]
            s_ref[k, :, at] = scores
            return lanes_max(running, scores)

        return lax.fori_loop(0, prefix // KC, score_prefix, jnp.full((QT, 128), MASKED, F32), unroll=True)

    def attend(k, p, running):
        q = queries_of(k, p)
        row = lax.broadcasted_iota(jnp.int32, (QT, KC), 0)
        token = (2 * p + row // 128) * 256 + x * 64 + row % 64
        col = lax.broadcasted_iota(jnp.int32, (QT, KC), 1)
        added = fresh[k].reshape(KC, 2 * HD)
        scores = jnp.where(col <= token, transposed_product(q, added), MASKED)
        s_ref[k, :, pl.ds(prefix, KC)] = scores
        running = lanes_max(running, scores)
        top = jnp.broadcast_to(jnp.max(running, axis=1, keepdims=True), (QT, 128))

        def weigh(at, keys, carried):
            total, summed = carried
            scores = s_ref[k, :, at]
            pieces = []
            for n in range(scores.shape[1] // 128):
                weights = jnp.exp(scores[:, n * 128 : (n + 1) * 128] - top)
                total = total + weights
                pieces.append(weights.astype(BF))
            weights = jnp.concatenate(pieces, axis=1)
            return total, summed + jnp.dot(weights, keys, preferred_element_type=F32)

        def weigh_prefix(i, carried):
            return weigh(pl.ds(pl.multiple_of(i * KC, KC), KC), keys_at(k, i), carried)

        carried = (jnp.zeros((QT, 128), F32), jnp.zeros((QT, 2 * HD), F32))
        carried = lax.fori_loop(0, prefix // KC, weigh_prefix, carried, unroll=True)
        total, summed = weigh(pl.ds(prefix, KC), added, carried)
        mixed = (summed / jnp.sum(total, axis=1, keepdims=True)).astype(BF).reshape(2, 2, 64, 128)
        for z in (0, 1):
            for i in (0, 1):
                att[2 * k + i, pl.ds(pl.multiple_of((2 * p + z) * 64, 64), 64)] = mixed[z, i]

    one = RowScatter(links, part1, rc1, q1, xh1, xf1, True)

    def out_project(p):
        tokens = pl.ds(pl.multiple_of(p * 128, 128), 128)

        def columns(n, carry):
            at = pl.ds(pl.multiple_of(n * 512, 512), 512)
            term = None
            for k in (0, 2):
                heads = jnp.concatenate([att[k, tokens], att[k + 1, tokens]], axis=1)
                product = jnp.dot(heads, wo_all[pl.ds(k, 2), :, at].reshape(256, 512), preferred_element_type=F32)
                term = product if term is None else term + product
            part1[pl.ds(4 * p, 4), :, at] = term.astype(BF).reshape(4, 32, 512)
            return carry

        lax.fori_loop(0, width // 512, columns, 0, unroll=True)

    far_pair, own_pair = 1 - zh // 2, zh // 2
    new.near()
    running = [score(0, far_pair)]
    new.far()
    b_plane.near_one()
    running.append(score(1, far_pair))
    a_plane.far_one()
    b_plane.start_two()
    b_plane.spread()
    new.ready()
    attend(0, far_pair, running[0])
    for dx in (1, 3, 2):
        o_rings[dx].far()
    own_wo.wait()
    a_plane.near_two(0)
    attend(1, far_pair, running[1])
    out_project(far_pair)
    one.cores((0,))
    a_plane.near_two(3)
    attend(0, own_pair, score(0, own_pair))
    one.first()
    a_plane.near_two(1)
    b_plane.near_two(0)
    attend(1, own_pair, score(1, own_pair))
    out_project(own_pair)
    one.cores((1, 2, 3))
    one.second()
    b_plane.far_one()
    residual[...] = one.total() + hid[...].astype(F32)
    rows[0, 0] = root_norm(residual[...], gain_two[...])
    ag2.start()
    b_plane.near_two(3)
    b_plane.near_two(1)
    a_plane.near_two_far()
    ag2.hop(1)
    b_plane.near_two_far()
    ag2.hop(2)
    ag2.hop(3)
    a_plane.far_two()
    b_plane.far_two()
    ag2.ready((0, 1, 7, 2))

    two = ColumnScatter(links, part2, rc2, q2, arrived2)

    def feed(ks):
        tokens = jnp.concatenate([rows[k].reshape(64, width) for k in ks], axis=0)
        nrm[...] = tokens

        def units(h, carry):
            some = pl.ds(h * 8, 8)
            gated = transposed_product(nrm[...], wall[0, some].reshape(256, width))
            raised = transposed_product(nrm[...], wall[1, some].reshape(256, width))
            act[h] = (gated / (1.0 + jnp.exp(-gated)) * raised).astype(BF)
            return carry

        lax.fori_loop(0, 2, units, 0, unroll=True)

        def columns(n, carry):
            at = pl.ds(pl.multiple_of(n * 512, 512), 512)
            activated = jnp.concatenate([act[0], act[1]], axis=1)
            term = jnp.dot(activated, wall[2, :, :, at].reshape(512, 512), preferred_element_type=F32)
            term = term.astype(BF).reshape(4, 2, 32, 512)
            for i, k in enumerate(ks):
                part2[k, :, :, at] = term[i]
            return carry

        lax.fori_loop(0, width // 512, columns, 0, unroll=True)

    feed((7, 0, 1, 2))
    two.cores((7, 0, 1, 2))
    ag2.last()
    ag2.ready((3, 5, 6, 4))
    feed((3, 4, 5, 6))
    two.cores((4, 3, 5, 6))
    for k, blocks in ((4, (4,)), (3, (3, 5)), (2, (2, 6)), (1, (1, 7))):
        two.arrive(blocks)
        two.hop(k)
    for handle, region in kv_h:
        links.recv(handle, region)
    own_kv.wait()
    kv_out[...] = jnp.swapaxes(kv_got[...].astype(F32), 0, 1).astype(BF)
    two.arrive((0,))
    for p in (0, 1):
        at = pl.ds(16 * p, 16)
        out[at, :] = (residual[at, :] + two.total(p)).astype(BF)
    links.drain()


def vmem(count):
    return [pl.BlockSpec(memory_space=pltpu.VMEM)] * count


def on_device(
    hidden_in, attention_gain, query_weight, keyval_weight, out_weight, feedforward_gain,
    gate_weight, up_weight, down_weight, prefix_pool, page_table, prefix_length,
):
    width = hidden_in.shape[2]
    tokens = 1024
    length = prefix_length[0]
    slots = prefix_pool.shape[1] * PAGE
    pool = prefix_pool[0].transpose(2, 0, 1, 3).reshape(KVH, slots, 2 * HD)

    logical = jnp.sum(
        jnp.where(
            page_table[0][None, :] == jnp.arange(256, dtype=jnp.int32)[:, None],
            jnp.arange(256, dtype=jnp.int32)[None, :],
            0,
        ),
        axis=1,
    )
    slot = logical[:, None] * PAGE + jnp.arange(PAGE, dtype=jnp.int32)[None, :]
    bias = jnp.where(slot < length, 0.0, MASKED).astype(F32)
    bias = bias.reshape(4, 8, slots).transpose(1, 0, 2).reshape(1, 32 * slots)

    index = jnp.arange(256, dtype=jnp.int32)
    column = (lax.axis_index("dev") // 2) % 4
    positions = (length + index // 64 * 256 + column * 64 + index % 64).astype(F32)
    half = HD // 2
    frequency = ROPE_BASE ** (-jnp.arange(half, dtype=F32) / half)
    angles = positions[:, None] * frequency[None, :]
    cosine, sine = jnp.cos(angles), jnp.sin(angles)
    cosine = jnp.concatenate([cosine] * 4, axis=1)
    sine = jnp.concatenate([-sine, sine, -sine, sine], axis=1)

    buffers = [
        ((8, 32, width), BF),
        ((2, slots, 2 * HD), BF),
        ((2, 8, 4, slots, 2 * HD), BF),
        ((4, 2, 32, width), BF),
        ((8, 32, width), BF),
        ((4, 128, width), BF),
        ((3, 16, 32, width), BF),
        ((256, width), BF),
        ((2, 4, 2, 64, 2 * HD), BF),
        ((2, 4, 4, 64, 2 * HD), BF),
        ((2, QT, 32 * slots + tokens), F32),
        ((4, 256, 2 * HD), BF),
        ((8, 32, width), BF),
        ((4, 32, width), BF),
        ((3, 32, width), BF),
        ((2, 16, width), BF),
        ((2, 32, width), BF),
        ((32, width), F32),
        ((8, 2, 32, width), BF),
        ((2, 256, 256), BF),
        ((8, 2, 32, width), BF),
        ((8, 32, width), BF),
        ((2, 4, 2, 16, width), BF),
        ((2, 4, 2, 16, width), BF),
        ((KVH, 32, 2 * HD), BF),
    ]
    hidden_out, kv_out = pl.pallas_call(
        layer_kernel,
        out_shape=[jax.ShapeDtypeStruct((32, width), BF), jax.ShapeDtypeStruct((32, 8, 2 * HD), BF)],
        in_specs=vmem(13),
        out_specs=vmem(2),
        scratch_shapes=[pltpu.VMEM(*b) for b in buffers] + [
            pltpu.SemaphoreType.DMA((COPIES,)),
            pltpu.SemaphoreType.DMA((COPIES,)),
            pltpu.SemaphoreType.DMA((16,)),
        ],
        compiler_params=pltpu.CompilerParams(collective_id=0, has_side_effects=True, vmem_limit_bytes=60 << 20),
        name="layer",
    )(
        hidden_in[0], pool, query_weight.reshape(2, 32, width), keyval_weight, out_weight,
        gate_weight, up_weight, down_weight,
        attention_gain.reshape(1, width), feedforward_gain.reshape(1, width), cosine, sine, bias,
    )
    return hidden_out[None], kv_out[None]


COPIES = 230


def solution(mesh):
    placed = (
        P("req", "dev", None),
        P(),
        P("dev", None),
        P("dev", None),
        P("dev", None),
        P(),
        P(("req", "dev"), None),
        P(("req", "dev"), None),
        P(("req", "dev"), None),
        P("req", "dev", None, None, None),
        P("req", None),
        P("req"),
    )
    return jax.shard_map(
        on_device,
        mesh=mesh,
        in_specs=placed,
        out_specs=(P("req", "dev", None), P("req", "dev", None, None)),
        check_vma=False,
    )
```

```python
import jax
import jax.numpy as jnp
from jax import lax
from jax.experimental import pallas as pl
from jax.experimental.pallas import tpu as pltpu
from jax.sharding import PartitionSpec as P

MESH = pl.DeviceIdType.MESH
HQ = 32
KVH = 8
HD = 64
PAGE = 16
ROPE_BASE = 10000000.0
EPS = 1e-05
ATTENTION_SCALE = 0.015625
MASKED = -1e30
BF = jnp.bfloat16
F32 = jnp.float32
QT = 256
KC = 1024


def root_norm(activations, norm_gain):
    widened = activations.astype(F32)
    inverse_rms = lax.rsqrt(jnp.mean(widened * widened, axis=-1, keepdims=True) + EPS)
    return (widened * inverse_rms * norm_gain).astype(BF)


def transposed_product(left, right):
    return lax.dot_general(left, right, (((1,), (1,)), ((), ())), preferred_element_type=F32)


def dev_of(zh, x, c):
    return (zh * 4 + x) * 2 + c


def place():
    d = lax.axis_index("dev")
    return d // 8, (d // 2) % 4, d % 2


class Links:
    def __init__(self, send_sems, recv_sems):
        self.send_sems, self.recv_sems = send_sems, recv_sems
        self.copies = []

    def make(self, i, src, dst, to):
        return pltpu.make_async_remote_copy(
            src_ref=src,
            dst_ref=dst,
            send_sem=self.send_sems.at[i],
            recv_sem=self.recv_sems.at[i],
            device_id=to,
            device_id_type=MESH,
        )

    def send(self, src, dst, to):
        i = len(self.copies)
        copy = self.make(i, src, dst, to)
        copy.start()
        self.copies.append(copy)
        return i, to

    def recv(self, handle, region):
        i, to = handle
        self.make(i, region, region, to).wait_recv()

    def drain(self):
        for copy in self.copies:
            copy.wait_send()


class Locals:
    def __init__(self, sems):
        self.sems, self.copies = sems, []

    def copy(self, src, dst):
        copy = pltpu.make_async_copy(src, dst, self.sems.at[len(self.copies)])
        copy.start()
        self.copies.append(copy)
        return copy


def greet(partners):
    barrier = pltpu.get_barrier_semaphore()
    for partner in partners:
        pl.semaphore_signal(barrier, inc=1, device_id=partner, device_id_type=MESH)
    pl.semaphore_wait(barrier, len(partners))


def halves(ref, i):
    rows = ref.shape[1] // 2
    return [ref.at[i, pl.ds(0, rows)], ref.at[i, pl.ds(rows, rows)]]


class Ring:
    def __init__(self, links, i, tos, blk, half, own=None, mate=None, there=None):
        self.l, self.i, self.tos, self.blk, self.half = links, i, tos, blk, half
        self.own = blk(i) if own is None else own
        self.mate, self.there = mate, there
        self.waits = []

    def core(self, j, src=None):
        if self.mate is not None:
            here = self.blk(j)
            self.waits.append((self.l.send(here if src is None else src, here, self.mate), self.there(j)))

    def start(self, core=True):
        mine = self.blk(self.i)
        self.h = [self.l.send(self.own, mine, to) for to in self.tos]
        if core:
            self.core(self.i, self.own)

    def near(self):
        self.f = []
        for s, off in ((0, 3), (1, 1)):
            j = (self.i + off) % 4
            self.l.recv(self.h[s], self.blk(j))
            piece = self.half(j, s)
            self.f.append(self.l.send(piece, piece, self.tos[s]))
            self.core(j)

    def far(self):
        j = (self.i + 2) % 4
        for s in (0, 1):
            self.l.recv(self.f[s], self.half(j, s))
        self.core(j)

    def ready(self):
        for handle, region in self.waits:
            self.l.recv(handle, region)


class PlaneGather:
    def __init__(self, links, out, x_first):
        self.l, self.out, self.x_first = links, out, x_first
        zh, x, c = place()
        r = lax.axis_index("req")
        self.x, self.y, self.rows = x, r % 4, pl.ds(0 if x_first else 16, 16)
        xs = [{"dev": dev_of(zh, (x + s) % 4, c)} for s in (1, 3)]
        ys = [{"req": r // 4 * 4 + (self.y + s) % 4} for s in (1, 3)]
        self.one, self.two = (xs, ys) if x_first else (ys, xs)
        self.h2, self.f2 = {}, {}

    def id(self, a, b):
        dx, dy = (a, b) if self.x_first else (b, a)
        return (self.x + dx) % 4 * 4 + (self.y + dy) % 4

    def blk(self, a, b):
        return self.out.at[:, self.id(a, b), self.rows]

    def half(self, a, b, s):
        wide = self.out.shape[3] // 2
        return self.out.at[:, self.id(a, b), self.rows, pl.ds(s * wide, wide)]

    def both(self, ref, tos):
        return [self.l.send(ref, ref, to) for to in tos]

    def start_one(self):
        self.h1 = self.both(self.blk(0, 0), self.one)

    def start_two(self):
        self.h2[0] = self.both(self.blk(0, 0), self.two)

    def near_one(self):
        self.f1 = []
        for s, a in ((0, 3), (1, 1)):
            self.l.recv(self.h1[s], self.blk(a, 0))
            piece = self.half(a, 0, s)
            self.f1.append(self.l.send(piece, piece, self.one[s]))

    def spread(self):
        for a in (3, 1):
            self.h2[a] = self.both(self.blk(a, 0), self.two)

    def far_one(self):
        self.g2 = []
        for s in (0, 1):
            piece = self.half(2, 0, s)
            self.l.recv(self.f1[s], piece)
            self.g2.append(self.both(piece, self.two))

    def near_two(self, a):
        self.f2[a] = []
        for s, b in ((0, 3), (1, 1)):
            self.l.recv(self.h2[a][s], self.blk(a, b))
            piece = self.half(a, b, s)
            self.f2[a].append(self.l.send(piece, piece, self.two[s]))

    def near_two_far(self):
        self.f2[2] = []
        for s, b in ((0, 3), (1, 1)):
            piece = self.half(2, b, s)
            self.l.recv(self.g2[s][s], piece)
            self.f2[2].append(self.l.send(piece, piece, self.two[s]))
        for s, b in ((0, 3), (1, 1)):
            self.l.recv(self.g2[1 - s][s], self.half(2, b, 1 - s))

    def far_two(self):
        for a in (0, 3, 1, 2):
            for s in (0, 1):
                self.l.recv(self.f2[a][s], self.half(a, 2, s))


class RowScatter:
    def __init__(self, links, part, rc, q, xh, xf, along_z=False):
        self.l = links
        self.part, self.rc, self.q, self.xh, self.xf = part, rc, q, xh, xf
        zh, x, c = place()
        self.x, self.c = zh if along_z else x, c
        if along_z:
            self.xs = [{"dev": dev_of((zh + s) % 4, x, c)} for s in (1, 3)]
        else:
            self.xs = [{"dev": dev_of(zh, (x + s) % 4, c)} for s in (1, 3)]
        self.mate = {"dev": dev_of(zh, x, 1 - c)}
        self.dx = (2, 1, 3, 0)
        self.ch, self.x1, self.x2 = {}, [], []

    def block(self, k, other=False):
        return ((self.x + self.dx[k]) % 4) * 2 + (1 - self.c if other else self.c)

    def cores(self, ks):
        for k in ks:
            self.ch[k] = self.l.send(self.part.at[self.block(k, True)], self.rc.at[k], self.mate)

    def arrive(self, k):
        self.l.recv(self.ch[k], self.rc.at[k])

    def own(self, k, at):
        return self.part[self.block(k), at].astype(F32) + self.rc[k, at].astype(F32)

    def first(self):
        self.arrive(0)
        for s in (0, 1):
            at = pl.ds(16 * s, 16)
            self.q[0, at] = self.own(0, at).astype(BF)
            self.x1.append(self.l.send(self.q.at[0, at], self.xh.at[s], self.xs[s]))

    def push(self, s, q, more=None):
        at = pl.ds(16 * q, 16)
        value = self.own(1 + s, at)
        if more is not None:
            value = value + more
        self.q[1 + s, at] = value.astype(BF)
        self.x2.append((self.l.send(self.q.at[1 + s, at], self.xf.at[s, at], self.xs[s]), self.xf.at[s, at]))

    def second(self):
        for s in (0, 1):
            self.arrive(1 + s)
            self.push(s, 1 - s)
        for s in (0, 1):
            self.l.recv(self.x1[s], self.xh.at[s])
            self.push(s, s, self.xh[s].astype(F32))

    def total(self):
        self.arrive(3)
        value = self.own(3, pl.ds(0, 32))
        for handle, region in self.x2:
            self.l.recv(handle, region)
        return value + self.xf[0].astype(F32) + self.xf[1].astype(F32)


def z_neighbours():
    zh, x, c = place()
    r = lax.axis_index("req")
    z = zh * 2 + r // 4
    tos = []
    for step in (1, 7):
        other = (z + step) % 8
        tos.append({"req": other % 2 * 4 + r % 4, "dev": dev_of(other // 2, x, c)})
    return tos


class ColumnGather:
    def __init__(self, links, out):
        self.l, self.out = links, out
        self.tos = z_neighbours()
        zh, x, c = place()
        self.mate = {"dev": dev_of(zh, x, 1 - c)}
        self.h, self.waits = {}, {}

    def piece(self, k, p):
        return self.out.at[k % 8, 0, pl.ds(16 * p, 16)]

    def core(self, k):
        self.waits[k % 8] = self.l.send(self.out.at[k % 8, 0], self.out.at[k % 8, 1], self.mate)

    def pass_on(self, s, k, p):
        sign = -1 if s == 0 else 1
        self.h[s, k + 1, p] = self.l.send(self.piece(sign * k, p), self.piece(sign * (k + 1), p), self.tos[s])

    def start(self):
        for p in (0, 1):
            for s in (0, 1):
                self.pass_on(s, 0, p if s == 0 else 1 - p)
        self.core(0)

    def hop(self, k):
        for p in (0, 1):
            for s in (0, 1):
                q = p if s == 0 else 1 - p
                self.l.recv(self.h[s, k, q], self.piece(-k if s == 0 else k, q))
                if k < 3 or q == s:
                    self.pass_on(s, k, q)
        self.core(k)
        self.core(-k)

    def last(self):
        for s in (0, 1):
            self.l.recv(self.h[s, 4, s], self.piece(4, s))
        self.core(4)

    def ready(self, ks):
        for k in ks:
            self.l.recv(self.waits[k % 8], self.out.at[k % 8, 1])


class ColumnScatter:
    def __init__(self, links, part, rc, q, arrived):
        self.l, self.part, self.rc, self.q, self.arrived = links, part, rc, q, arrived
        self.tos = z_neighbours()
        zh, x, c = place()
        self.mate = {"dev": dev_of(zh, x, 1 - c)}
        self.ch, self.h = {}, {}

    def cores(self, ks):
        for k in ks:
            self.ch[k] = self.l.send(self.part.at[k, 1], self.rc.at[k], self.mate)

    def arrive(self, ks):
        for k in ks:
            self.l.recv(self.ch[k], self.rc.at[k])

    def own(self, k, p):
        at = pl.ds(16 * p, 16)
        return self.part[k % 8, 0, at].astype(F32) + self.rc[k % 8, at].astype(F32)

    def hop(self, k):
        for p in (0, 1):
            for s in (0, 1):
                q = 1 - s if p == 0 else s
                if k == 4 and q != s:
                    continue
                value = self.own(k if s == 0 else -k, q)
                if (s, k + 1, q) in self.h:
                    slot = self.arrived.at[s, k + 1 - 2, q]
                    self.l.recv(self.h[s, k + 1, q], slot)
                    value = value + slot[...].astype(F32)
                self.q[s, k - 1, q] = value.astype(BF)
                self.h[s, k, q] = self.l.send(self.q.at[s, k - 1, q], self.arrived.at[s, (k - 2) % 4, q], self.tos[s])

    def total(self, p):
        value = self.own(0, p)
        for s in (0, 1):
            slot = self.arrived.at[s, 3, p]
            self.l.recv(self.h[s, 1, p], slot)
            value = value + slot[...].astype(F32)
        return value


def layer_kernel(
    hid, pool, wq, wkv, wo, gate, up, down, gain_one, gain_two, cosine, sine, bias,
    out, kv_out,
    hid_col, relay, kv_all, wq_all, wkv_all, wo_all, wall, nrm, q_all, fresh, s_ref, att,
    part1, rc1, q1, xh1, xf1, residual, rows, act, part2, rc2, q2, arrived2, kv_got, kv_relay,
    send_sems, recv_sems, local_sems,
):
    zh, x, c = place()
    r = lax.axis_index("req")
    width = hid.shape[1]
    links, local = Links(send_sems, recv_sems), Locals(local_sems)
    zs = [{"dev": dev_of((zh + s) % 4, x, c)} for s in (1, 3)]
    xs = [{"dev": dev_of(zh, (x + s) % 4, c)} for s in (1, 3)]
    mate = {"dev": dev_of(zh, x, 1 - c)}
    y = r % 4
    ys = [{"req": r // 4 * 4 + (y + s) % 4} for s in (1, 3)]
    a_plane, b_plane = PlaneGather(links, wall, True), PlaneGather(links, wall, False)
    ag2 = ColumnGather(links, rows)
    column = {(dz, dc): {"dev": dev_of((zh + dz) % 4, x, (c + dc) % 2)} for dz in range(4) for dc in range(2)}
    del column[0, 0]

    hidden = Ring(
        links, zh, zs, lambda j: hid_col.at[j * 2 + c], lambda j, s: hid_col.at[j * 2 + c, pl.ds(16 * s, 16)],
        hid, mate, lambda j: hid_col.at[j * 2 + 1 - c],
    )
    wide = width // 4

    def quarter(k):
        return pl.ds(pl.multiple_of(k * wide, wide), wide)

    q_ring = Ring(
        links, x, xs, lambda j: wq_all.at[j, :, :, quarter(y)], lambda j, s: wq_all.at[j, s, :, quarter(y)],
        wq.at[:, :, quarter(y)],
    )
    kv_ring = Ring(
        links, x, xs, lambda j: wkv_all.at[j * 2 + c, :, quarter(y)],
        lambda j, s: wkv_all.at[j * 2 + c, pl.ds(16 * s, 16), quarter(y)], wkv.at[:, quarter(y)],
    )
    o_ring = Ring(
        links, x, xs, lambda j: wo_all.at[j, pl.ds(64, 64), quarter(y)],
        lambda j, s: wo_all.at[j, pl.ds(64 + 32 * s, 32), quarter(y)], wo.at[:, quarter(y)],
    )
    o_rings = {}
    for dx in (1, 2, 3):
        o_rings[dx] = Ring(
            links, y, ys, lambda k, j=(x + dx) % 4: wo_all.at[j, pl.ds(64, 64), quarter(k)],
            lambda k, s, j=(x + dx) % 4: wo_all.at[j, pl.ds(64 + 32 * s, 32), quarter(k)],
        )
    y_rings = {}
    for dx in (1, 2, 3):
        j = (x + dx) % 4
        y_rings[dx] = [
            Ring(
                links, y, ys, lambda k, j=j: wkv_all.at[j * 2 + c, :, quarter(k)],
                lambda k, s, j=j: wkv_all.at[j * 2 + c, pl.ds(16 * s, 16), quarter(k)],
            ),
            Ring(
                links, y, ys, lambda k, j=j: wq_all.at[j, :, :, quarter(k)],
                lambda k, s, j=j: wq_all.at[j, s, :, quarter(k)],
            ),
        ]
    pages = Ring(
        links, x, xs, lambda j: kv_all.at[:, j * 2 + c], lambda j, s: kv_all.at[s, j * 2 + c],
        None, mate, lambda j: kv_all.at[:, j * 2 + 1 - c],
    )
    new = Ring(
        links, x, xs, lambda j: fresh.at[c, :, j], lambda j, s: fresh.at[c, pl.ds(2 * s, 2), j],
        None, mate, lambda j: fresh.at[1 - c, :, j],
    )
    greet([to for (dz, dc), to in column.items() if dz != 2] + xs + ag2.tos + ys)

    mine = x * 2 + c
    near_pages, relayed, far_pages = [], [], []
    for s in (0, 1):
        relayed.append(links.send(pool.at[2 * ((zh + 2) % 4) + s], relay.at[s], zs[s]))
    for s, dz in ((0, 1), (1, 3)):
        near_pages.append(links.send(pool.at[pl.ds(2 * ((zh + dz) % 4), 2)], kv_all.at[:, mine, zh], zs[s]))
    kv_ring.start()
    q_ring.start()
    o_ring.start()
    w_core = [(links.send(wkv, wkv_all.at[mine], mate), wkv_all.at[x * 2 + 1 - c])]
    own_planes = [local.copy(own, wall.at[a, x * 4 + y]) for a, own in enumerate((gate, up, down))]
    own_pages = local.copy(pool.at[pl.ds(2 * zh, 2)], kv_all.at[:, mine, zh])
    early = [
        local.copy(hid, hid_col.at[zh * 2 + c]),
        local.copy(wkv, wkv_all.at[mine]),
        local.copy(wq, wq_all.at[x]),
    ]
    own_wo = local.copy(wo, wo_all.at[x, pl.ds(64, 64)])
    kv_ring.near()
    for s, dz in ((0, 3), (1, 1)):
        links.recv(relayed[s], relay.at[s])
        far_pages.append(links.send(relay.at[s], kv_all.at[s, mine, (zh + dz) % 4], zs[s]))
    hidden.start()
    q_ring.near()
    for dx in (1, 3):
        for ring in y_rings[dx]:
            ring.start()
    o_ring.near()
    for copy in own_planes:
        copy.wait()
    a_plane.start_one()
    kv_ring.far()
    q_ring.far()
    for ring in y_rings[2]:
        ring.start()
    for s, dz in ((0, 3), (1, 1)):
        links.recv(near_pages[s], kv_all.at[:, mine, (zh + dz) % 4])
    own_pages.wait()
    for s in (0, 1):
        links.recv(far_pages[s], kv_all.at[s, mine, (zh + 2) % 4])
    pages.start()
    for dx in (1, 3, 2):
        for ring in y_rings[dx]:
            ring.near()
    o_ring.far()
    for dx in (1, 3, 2):
        o_rings[dx].start()
    b_plane.start_one()
    a_plane.start_two()
    a_plane.near_one()
    for k in range(4):
        wo_all[k, pl.ds(0, 64)] = jnp.zeros((64, width), BF)
    for copy in early:
        copy.wait()
    hidden.near()

    def norm(dz):
        for core in (0, 1):
            block = (zh + dz) % 4 * 2 + core
            nrm[pl.ds(pl.multiple_of(block * 32, 32), 32), :] = root_norm(hid_col[block], gain_one[...])

    for n, dz in enumerate((0, 3, 1)):
        links.recv(*hidden.waits[n])
        norm(dz)
    pages.near()
    for dx in (1, 3, 2):
        for ring in y_rings[dx]:
            ring.far()
        block = (x + dx) % 4 * 2
        w_core.append((links.send(wkv_all.at[block + c], wkv_all.at[block + c], mate), wkv_all.at[block + 1 - c]))
    hidden.far()
    links.recv(*hidden.waits[3])
    for handle, region in w_core:
        links.recv(handle, region)

    norm(2)
    lane = lax.broadcasted_iota(jnp.int32, (256, 2 * HD), 1)
    first_half = lane % HD < HD // 2

    def rotate(pairs):
        swapped = jnp.where(first_half, pltpu.roll(pairs, 96, 1), pltpu.roll(pairs, 32, 1))
        return pairs * cosine[...] + swapped * sine[...]

    keyvals = transposed_product(nrm[...], wkv_all[...].reshape(256, width)).astype(BF)
    for k in (0, 1):
        pairs = keyvals[:, k * 128 : (k + 1) * 128].astype(F32)
        fresh[k, :, x] = jnp.where(lane < HD, rotate(pairs), pairs).astype(BF).reshape(4, 64, 128)
    new.start(False)
    kv_h, kv_far = [], []
    for (dz, dc), to in column.items():
        src = fresh.at[c, (zh + dz) % 4, x, pl.ds(32 * ((c + dc) % 2), 32)]
        if dz == 2:
            kv_far.append(links.send(src, kv_relay.at[dc], column[1, 0]))
        else:
            region = kv_got.at[2 * ((zh + 4 - dz) % 4) + (c + dc) % 2]
            kv_h.append((links.send(src, kv_got.at[2 * zh + c], to), region))
    own_kv = local.copy(fresh.at[c, zh, x, pl.ds(32 * c, 32)], kv_got.at[2 * zh + c])
    queries = transposed_product(nrm[...], wq_all[...].reshape(256, width))
    for k in (0, 1):
        turned = rotate(queries[:, k * 128 : (k + 1) * 128]) * ATTENTION_SCALE
        for i in (0, 1):
            head = turned if i == 0 else pltpu.roll(turned, 64, 1)
            q_all[k, :, i] = jnp.where(lane < HD, head, 0.0).astype(BF).reshape(4, 64, 128)
    pages.far()
    for dx in (1, 3, 2):
        o_rings[dx].near()
    a_plane.spread()
    pages.ready()

    prefix = 4096
    per_block = KC // 512

    def lanes_max(running, scores):
        for k in range(scores.shape[1] // 128):
            running = jnp.maximum(running, scores[:, k * 128 : (k + 1) * 128])
        return running

    def keys_at(k, i):
        return kv_all[k, pl.ds(i * per_block, per_block)].reshape(KC, 2 * HD)

    def queries_of(k, p):
        return q_all[k, pl.ds(2 * p, 2)].reshape(QT, 2 * HD)

    def score(k, p):
        q = queries_of(k, p)

        def score_prefix(i, running):
            at = pl.ds(pl.multiple_of(i * KC, KC), KC)
            scores = transposed_product(q, keys_at(k, i)) + bias[:, at]
            s_ref[k, :, at] = scores
            return lanes_max(running, scores)

        return lax.fori_loop(0, prefix // KC, score_prefix, jnp.full((QT, 128), MASKED, F32), unroll=True)

    def attend(k, p, running):
        q = queries_of(k, p)
        row = lax.broadcasted_iota(jnp.int32, (QT, KC), 0)
        token = (2 * p + row // 128) * 256 + x * 64 + row % 64
        col = lax.broadcasted_iota(jnp.int32, (QT, KC), 1)
        added = fresh[k].reshape(KC, 2 * HD)
        scores = jnp.where(col <= token, transposed_product(q, added), MASKED)
        s_ref[k, :, pl.ds(prefix, KC)] = scores
        running = lanes_max(running, scores)
        top = jnp.broadcast_to(jnp.max(running, axis=1, keepdims=True), (QT, 128))

        def weigh(at, keys, carried):
            total, summed = carried
            scores = s_ref[k, :, at]
            pieces = []
            for n in range(scores.shape[1] // 128):
                weights = jnp.exp(scores[:, n * 128 : (n + 1) * 128] - top)
                total = total + weights
                pieces.append(weights.astype(BF))
            weights = jnp.concatenate(pieces, axis=1)
            return total, summed + jnp.dot(weights, keys, preferred_element_type=F32)

        def weigh_prefix(i, carried):
            return weigh(pl.ds(pl.multiple_of(i * KC, KC), KC), keys_at(k, i), carried)

        carried = (jnp.zeros((QT, 128), F32), jnp.zeros((QT, 2 * HD), F32))
        carried = lax.fori_loop(0, prefix // KC, weigh_prefix, carried, unroll=True)
        total, summed = weigh(pl.ds(prefix, KC), added, carried)
        mixed = (summed / jnp.sum(total, axis=1, keepdims=True)).astype(BF).reshape(2, 2, 64, 128)
        for z in (0, 1):
            for i in (0, 1):
                att[2 * k + i, pl.ds(pl.multiple_of((2 * p + z) * 64, 64), 64)] = mixed[z, i]

    one = RowScatter(links, part1, rc1, q1, xh1, xf1, True)

    def out_project(p):
        tokens = pl.ds(pl.multiple_of(p * 128, 128), 128)

        def columns(n, carry):
            at = pl.ds(pl.multiple_of(n * 512, 512), 512)
            term = None
            for k in (0, 2):
                heads = jnp.concatenate([att[k, tokens], att[k + 1, tokens]], axis=1)
                product = jnp.dot(heads, wo_all[pl.ds(k, 2), :, at].reshape(256, 512), preferred_element_type=F32)
                term = product if term is None else term + product
            part1[pl.ds(4 * p, 4), :, at] = term.astype(BF).reshape(4, 32, 512)
            return carry

        lax.fori_loop(0, width // 512, columns, 0, unroll=True)

    far_pair, own_pair = 1 - zh // 2, zh // 2
    new.near()
    running = [score(0, far_pair)]
    b_plane.near_one()
    running.append(score(1, far_pair))
    new.far()
    for dc in (0, 1):
        links.recv(kv_far[dc], kv_relay.at[dc])
        onward = links.send(kv_relay.at[dc], kv_got.at[2 * ((zh + 3) % 4) + c], column[1, dc])
        kv_h.append((onward, kv_got.at[2 * ((zh + 2) % 4) + (c + dc) % 2]))
    a_plane.far_one()
    b_plane.start_two()
    b_plane.spread()
    new.ready()
    attend(0, far_pair, running[0])
    for dx in (1, 3, 2):
        o_rings[dx].far()
    own_wo.wait()
    a_plane.near_two(0)
    attend(1, far_pair, running[1])
    out_project(far_pair)
    one.cores((0,))
    a_plane.near_two(3)
    attend(0, own_pair, score(0, own_pair))
    one.first()
    a_plane.near_two(1)
    b_plane.near_two(0)
    attend(1, own_pair, score(1, own_pair))
    out_project(own_pair)
    one.cores((1, 2, 3))
    one.second()
    b_plane.far_one()
    residual[...] = one.total() + hid[...].astype(F32)
    rows[0, 0] = root_norm(residual[...], gain_two[...])
    ag2.start()
    b_plane.near_two(3)
    b_plane.near_two(1)
    a_plane.near_two_far()
    ag2.hop(1)
    b_plane.near_two_far()
    ag2.hop(2)
    ag2.hop(3)
    a_plane.far_two()
    b_plane.far_two()
    ag2.ready((0, 1, 7, 2))

    two = ColumnScatter(links, part2, rc2, q2, arrived2)

    def feed(ks):
        tokens = jnp.concatenate([rows[k].reshape(64, width) for k in ks], axis=0)
        nrm[...] = tokens

        def units(h, carry):
            some = pl.ds(h * 8, 8)
            gated = transposed_product(nrm[...], wall[0, some].reshape(256, width))
            raised = transposed_product(nrm[...], wall[1, some].reshape(256, width))
            act[h] = (gated / (1.0 + jnp.exp(-gated)) * raised).astype(BF)
            return carry

        lax.fori_loop(0, 2, units, 0, unroll=True)

        def columns(n, carry):
            at = pl.ds(pl.multiple_of(n * 512, 512), 512)
            activated = jnp.concatenate([act[0], act[1]], axis=1)
            term = jnp.dot(activated, wall[2, :, :, at].reshape(512, 512), preferred_element_type=F32)
            term = term.astype(BF).reshape(4, 2, 32, 512)
            for i, k in enumerate(ks):
                part2[k, :, :, at] = term[i]
            return carry

        lax.fori_loop(0, width // 512, columns, 0, unroll=True)

    feed((7, 0, 1, 2))
    two.cores((7, 0, 1, 2))
    ag2.last()
    ag2.ready((3, 5, 6, 4))
    feed((3, 4, 5, 6))
    two.cores((4, 3, 5, 6))
    for k, blocks in ((4, (4,)), (3, (3, 5)), (2, (2, 6)), (1, (1, 7))):
        two.arrive(blocks)
        two.hop(k)
    for handle, region in kv_h:
        links.recv(handle, region)
    own_kv.wait()
    kv_out[...] = jnp.swapaxes(kv_got[...].astype(F32), 0, 1).astype(BF)
    two.arrive((0,))
    for p in (0, 1):
        at = pl.ds(16 * p, 16)
        out[at, :] = (residual[at, :] + two.total(p)).astype(BF)
    links.drain()


def vmem(count):
    return [pl.BlockSpec(memory_space=pltpu.VMEM)] * count


def on_device(
    hidden_in, attention_gain, query_weight, keyval_weight, out_weight, feedforward_gain,
    gate_weight, up_weight, down_weight, prefix_pool, page_table, prefix_length,
):
    width = hidden_in.shape[2]
    tokens = 1024
    length = prefix_length[0]
    slots = prefix_pool.shape[1] * PAGE
    pool = prefix_pool[0].transpose(2, 0, 1, 3).reshape(KVH, slots, 2 * HD)

    logical = jnp.sum(
        jnp.where(
            page_table[0][None, :] == jnp.arange(256, dtype=jnp.int32)[:, None],
            jnp.arange(256, dtype=jnp.int32)[None, :],
            0,
        ),
        axis=1,
    )
    slot = logical[:, None] * PAGE + jnp.arange(PAGE, dtype=jnp.int32)[None, :]
    bias = jnp.where(slot < length, 0.0, MASKED).astype(F32)
    bias = bias.reshape(4, 8, slots).transpose(1, 0, 2).reshape(1, 32 * slots)

    index = jnp.arange(256, dtype=jnp.int32)
    column = (lax.axis_index("dev") // 2) % 4
    positions = (length + index // 64 * 256 + column * 64 + index % 64).astype(F32)
    half = HD // 2
    frequency = ROPE_BASE ** (-jnp.arange(half, dtype=F32) / half)
    angles = positions[:, None] * frequency[None, :]
    cosine, sine = jnp.cos(angles), jnp.sin(angles)
    cosine = jnp.concatenate([cosine] * 4, axis=1)
    sine = jnp.concatenate([-sine, sine, -sine, sine], axis=1)

    buffers = [
        ((8, 32, width), BF),
        ((2, slots, 2 * HD), BF),
        ((2, 8, 4, slots, 2 * HD), BF),
        ((4, 2, 32, width), BF),
        ((8, 32, width), BF),
        ((4, 128, width), BF),
        ((3, 16, 32, width), BF),
        ((256, width), BF),
        ((2, 4, 2, 64, 2 * HD), BF),
        ((2, 4, 4, 64, 2 * HD), BF),
        ((2, QT, 32 * slots + tokens), F32),
        ((4, 256, 2 * HD), BF),
        ((8, 32, width), BF),
        ((4, 32, width), BF),
        ((3, 32, width), BF),
        ((2, 16, width), BF),
        ((2, 32, width), BF),
        ((32, width), F32),
        ((8, 2, 32, width), BF),
        ((2, 256, 256), BF),
        ((8, 2, 32, width), BF),
        ((8, 32, width), BF),
        ((2, 4, 2, 16, width), BF),
        ((2, 4, 2, 16, width), BF),
        ((KVH, 32, 2 * HD), BF),
        ((2, 32, 2 * HD), BF),
    ]
    hidden_out, kv_out = pl.pallas_call(
        layer_kernel,
        out_shape=[jax.ShapeDtypeStruct((32, width), BF), jax.ShapeDtypeStruct((32, 8, 2 * HD), BF)],
        in_specs=vmem(13),
        out_specs=vmem(2),
        scratch_shapes=[pltpu.VMEM(*b) for b in buffers] + [
            pltpu.SemaphoreType.DMA((COPIES,)),
            pltpu.SemaphoreType.DMA((COPIES,)),
            pltpu.SemaphoreType.DMA((16,)),
        ],
        compiler_params=pltpu.CompilerParams(collective_id=0, has_side_effects=True, vmem_limit_bytes=60 << 20),
        name="layer",
    )(
        hidden_in[0], pool, query_weight.reshape(2, 32, width), keyval_weight, out_weight,
        gate_weight, up_weight, down_weight,
        attention_gain.reshape(1, width), feedforward_gain.reshape(1, width), cosine, sine, bias,
    )
    return hidden_out[None], kv_out[None]


COPIES = 230


def solution(mesh):
    placed = (
        P("req", "dev", None),
        P(),
        P("dev", None),
        P("dev", None),
        P("dev", None),
        P(),
        P(("req", "dev"), None),
        P(("req", "dev"), None),
        P(("req", "dev"), None),
        P("req", "dev", None, None, None),
        P("req", None),
        P("req"),
    )
    return jax.shard_map(
        on_device,
        mesh=mesh,
        in_specs=placed,
        out_specs=(P("req", "dev", None), P("req", "dev", None, None)),
        check_vma=False,
    )
```
